32 devices in a mesh: fsdp: 2 (over x), ctx: 4 (over z), tp: 4 (over y, core).
Axes of the slice: x: 2, y: 2, z: 4, core: 2. Of those that a mesh axis runs over, the one named last changes fastest.
Arguments:
- inputs: bfloat16 [2, 1024, 1024], P('fsdp', 'ctx'), may hold values from -6 to 6
- upstream: bfloat16 [2, 1024, 1024], P('fsdp', 'ctx'), may hold values from -6 to 6
- teacher: bfloat16 [2, 1024, 1024], P('fsdp', 'ctx'), may hold values from -8 to 8
- valid: int32 [2, 1024], P('fsdp', 'ctx'), may hold values from 0 to 1, as said below
- segment: int32 [2, 1024], P('fsdp', 'ctx'), may hold values from 0 to 7, never falling along the last dimension, each value on 1 to 512 neighbouring positions
- gain_one: float32 [1024], replicated, may hold values from 0.25 to 1.75
- query_weight: bfloat16 [1024, 1024], P('fsdp', 'tp'), may hold values from -0.1875 to 0.1875
- key_weight: bfloat16 [1024, 1024], P('fsdp', 'tp'), may hold values from -0.1875 to 0.1875
- value_weight: bfloat16 [1024, 1024], P('fsdp', 'tp'), may hold values from -0.1875 to 0.1875
- out_weight: bfloat16 [1024, 1024], P('tp', 'fsdp'), may hold values from -0.75 to 0.75
- gain_two: float32 [1024], replicated, may hold values from 0.25 to 1.75
- gate_weight: bfloat16 [1024, 2816], P('fsdp', 'tp'), may hold values from -0.1875 to 0.1875
- up_weight: bfloat16 [1024, 2816], P('fsdp', 'tp'), may hold values from -0.1875 to 0.1875
- down_weight: bfloat16 [2816, 1024], P('tp', 'fsdp'), may hold values from -0.21875 to 0.21875
Outputs:
- output: bfloat16 [2, 1024, 1024], P('fsdp', 'ctx')
- loss: float32 [2], replicated
- grad_inputs: float32 [2, 1024, 1024], P('fsdp', 'ctx')
- grad_gain_one: float32 [1024], P('fsdp')
- grad_query: float32 [1024, 1024], P('fsdp', 'tp')
- grad_key: float32 [1024, 1024], P('fsdp', 'tp')
- grad_value: float32 [1024, 1024], P('fsdp', 'tp')
- grad_out: float32 [1024, 1024], P('tp', 'fsdp')
- grad_gain_two: float32 [1024], P('fsdp')
- grad_gate: float32 [1024, 2816], P('fsdp', 'tp')
- grad_up: float32 [1024, 2816], P('fsdp', 'tp')
- grad_down: float32 [2816, 1024], P('tp', 'fsdp')
The draws below stay inside these ranges and needn't reach their ends.
Inputs may be any that keep to these rules, and one draw needn't show every extreme that they name: `segment`: segment numbers never fall along a sequence; each document has 1 to 512 positions and one has exactly 512. The first token of every sequence is valid.
All inputs are finite; a program needn't handle non-finite values.
Results may differ from the reference program's by a relative error of at most 0.018.
Values may be sent and summed in bfloat16 or wider, within the bound.
A program may use at most 128 MiB of HBM per device.

```python
import math
import jax
import jax.numpy as jnp
import numpy as np
from jax import lax

D = 1024
HEADS = 16
HEAD_DIM = 64
FF = 2816
SEQS = 2
LEN = 1024


def draw_teacher(key, part):
    values_out = jax.random.normal(key, (SEQS, LEN, D), dtype=jnp.float32)
    return jnp.clip(values_out, -8.0, 8.0).astype(jnp.bfloat16)


def draw_valid(key, part):
    overall = SEQS * LEN
    places = jnp.arange(overall, dtype=jnp.int32).reshape(SEQS, LEN)
    ticket = jax.random.randint(key, (SEQS, LEN), 0, 4 * overall, dtype=jnp.int32)
    chosen = (ticket < overall + 2 * places).astype(jnp.int32)
    opening = jnp.arange(LEN, dtype=jnp.int32)[None, :] == 0
    return jnp.where(opening, 1, chosen).astype(jnp.int32)


def shard_levels(rng, shape, pieces, smallest, high):
    factor_of, own = 1.0, jax.random.fold_in(rng, 6)
    for dim, shards_of in pieces:
        draws = jnp.exp(jax.random.uniform(jax.random.fold_in(own, dim), (shards_of,), jnp.float32, smallest / len(pieces), high / len(pieces)))
        factor_of = factor_of * jnp.repeat(draws, shape[dim] // shards_of).reshape([-1 if axis == dim else 1 for axis in range(len(shape))])
    return factor_of


def profile(count, total, most, slope):
    weights = [(1 << 20) // math.isqrt(standing ** slope) + 1 for standing in range(2, count + 1)]
    surplus, holding = total - most - (count - 1), [1] * (count - 1)
    while surplus > 0:
        free = [i for i in range(count - 1) if holding[i] < most]
        mass, remaining = sum([weights[i] for i in free]), surplus
        for i in free:
            addition = min(most - holding[i], max(1, remaining * weights[i] // mass), surplus)
            holding[i] = holding[i] + addition
            surplus = surplus - addition
    return np.array([most] + holding)


def uneven_parts(stream_key, amount, total, bound, skew):
    if amount == 2:
        one = jax.random.randint(stream_key, (), max(1, total - bound), min(bound, total - 1) + 1)
        return jnp.stack([one, total - one])
    lengths = jnp.asarray(profile(amount, total, bound, skew), jnp.int32)
    twos = (amount - 1) // 2
    giver, sink = lengths[1:1 + 2 * twos:2], lengths[2:2 + 2 * twos:2]
    margin = jnp.minimum(giver - 1, bound - sink)
    moved = jax.random.randint(jax.random.fold_in(stream_key, 1), (twos,), 0, 1 << 20) % (margin + 1)
    lengths = lengths.at[1:1 + 2 * twos:2].set(giver - moved).at[2:2 + 2 * twos:2].set(sink + moved)
    return lengths[jax.random.permutation(jax.random.fold_in(stream_key, 2), amount)]


def bell_draw(rng, shape, scale, limit, shards=(), kind=jnp.bfloat16):
    loudness = shard_levels(rng, shape, shards, -0.22, 0.18) if shards else 1.0
    values = jax.random.normal(rng, shape, jnp.float32) * scale * loudness
    return jnp.minimum(jnp.maximum(values, -limit), limit).astype(kind)


def setup_inputs(seed: int = 0) -> dict:
    streams_of = jax.random.split(jax.random.key(seed), 15)
    inputs = bell_draw(streams_of[0], (SEQS, LEN, D), 1.0, 6.0, ((0, 2), (1, 4)))
    upstream = bell_draw(streams_of[1], (SEQS, LEN, D), 1.0, 6.0, ((0, 2), (1, 4)))
    teacher = draw_teacher(jax.random.fold_in(streams_of[14], 71), 0)
    valid = draw_valid(jax.random.fold_in(streams_of[14], 71), 0)
    segment = jax.vmap(lambda own: jnp.searchsorted(jnp.cumsum(uneven_parts(own, max(LEN // 128, 4), LEN, LEN // 2, 2)), jnp.arange(LEN), side="right"))(jax.random.split(streams_of[4], SEQS)).reshape((SEQS, LEN)).astype(jnp.int32)
    gain_one = jnp.clip(1.0 + 0.15 * jax.random.normal(streams_of[5], (D,), jnp.float32), 0.25, 1.75)
    query_weight = bell_draw(streams_of[6], (D, D), D ** -0.5, 0.1875, ((0, 2), (1, 4)))
    key_weight = bell_draw(streams_of[7], (D, D), D ** -0.5, 0.1875, ((0, 2), (1, 4)))
    value_weight = bell_draw(streams_of[8], (D, D), D ** -0.5, 0.1875, ((0, 2), (1, 4)))
    out_weight = bell_draw(streams_of[9], (D, D), (D // 16) ** -0.5, 0.75, ((0, 4), (1, 2)))
    gain_two = jnp.clip(1.0 + 0.15 * jax.random.normal(streams_of[10], (D,), jnp.float32), 0.25, 1.75)
    gate_weight = bell_draw(streams_of[11], (D, FF), D ** -0.5, 0.1875, ((0, 2), (1, 4)))
    up_weight = bell_draw(streams_of[12], (D, FF), D ** -0.5, 0.1875, ((0, 2), (1, 4)))
    down_weight = bell_draw(streams_of[13], (FF, D), (FF // 4) ** -0.5, 0.21875, ((0, 4), (1, 2)))
    return {"inputs": inputs, "upstream": upstream, "teacher": teacher, "valid": valid, "segment": segment, "gain_one": gain_one, "query_weight": query_weight, "key_weight": key_weight, "value_weight": value_weight, "out_weight": out_weight, "gain_two": gain_two, "gate_weight": gate_weight, "up_weight": up_weight, "down_weight": down_weight}


@jax.custom_vjp
def low(v):
    return lax.optimization_barrier(v.astype(jnp.bfloat16)).astype(jnp.float32)

@jax.custom_vjp
def low_back(v):
    return v

def low_keep(v):
    return (low(v), None)

def low_pass(kept, grad):
    return (grad,)

def back_keep(v):
    return (v, None)

def back_low(kept, grad):
    return (low(grad),)
low.defvjp(low_keep, low_pass)
low_back.defvjp(back_keep, back_low)

def matmul_high(left, right):
    return jnp.dot(left, right, precision=lax.Precision.HIGHEST, preferred_element_type=jnp.float32)

def rms_scale(values_in, scales_in):
    return values_in * lax.rsqrt(lax.optimization_barrier(jnp.mean(values_in * values_in, axis=-1, keepdims=True)) + 1e-05) * scales_in

def attend(bundle):
    queries, keys_in, values_in, seg_row = bundle
    scores = jnp.einsum('qhd,khd->hqk', queries, keys_in, precision=lax.Precision.HIGHEST) * HEAD_DIM ** (-0.5)
    scores = low_back(scores)
    places = jnp.arange(LEN)
    allowed = (places[None, :] <= places[:, None]) & (seg_row[None, :] == seg_row[:, None])
    scores = jnp.where(allowed[None], scores, -1e+30)
    attn_probs = jax.nn.softmax(scores, axis=-1)
    return jnp.einsum('hqk,khd->qhd', low(attn_probs), values_in, precision=lax.Precision.HIGHEST)

def layer(inputs, gain_one, query_weight, key_weight, value_weight, out_weight, gain_two, gate_weight, up_weight, down_weight, segment):
    flat_in = inputs.reshape(SEQS * LEN, D)
    normed_one = low(rms_scale(flat_in, gain_one))
    queries = low(low_back(matmul_high(normed_one, query_weight)))
    keys_all = low(low_back(matmul_high(normed_one, key_weight)))
    values_all = low(low_back(matmul_high(normed_one, value_weight)))
    shaped = (SEQS, LEN, HEADS, HEAD_DIM)
    mixed = lax.map(jax.checkpoint(attend), (queries.reshape(shaped), keys_all.reshape(shaped), values_all.reshape(shaped), segment))
    mixed = low(low_back(mixed.reshape(SEQS * LEN, D)))
    middle = flat_in + low_back(matmul_high(mixed, out_weight))
    normed_two = low(rms_scale(middle, gain_two))
    gate_act = low(low_back(matmul_high(normed_two, gate_weight)))
    up_act = low(low_back(matmul_high(normed_two, up_weight)))
    hidden = low(jax.nn.silu(gate_act) * up_act)
    result = middle + low_back(matmul_high(hidden, down_weight))
    return result.reshape(SEQS, LEN, D)

def reference(inputs, upstream, teacher, valid, segment, gain_one, query_weight, key_weight, value_weight, out_weight, gain_two, gate_weight, up_weight, down_weight):
    float_args = (inputs.astype(jnp.float32), gain_one.astype(jnp.float32), query_weight.astype(jnp.float32), key_weight.astype(jnp.float32), value_weight.astype(jnp.float32), out_weight.astype(jnp.float32), gain_two.astype(jnp.float32), gate_weight.astype(jnp.float32), up_weight.astype(jnp.float32), down_weight.astype(jnp.float32))

    def forward(*floats):
        return layer(*floats, segment)
    result, pullback = jax.vjp(forward, *float_args)
    weighting = valid.astype(jnp.float32)[..., None]
    differ = result - teacher.astype(jnp.float32)
    counted = jnp.sum(valid.astype(jnp.float32))
    loss_value = lax.optimization_barrier(jnp.sum(weighting * differ * differ, axis=(1, 2))) * SEQS / (counted * D)
    gradients = pullback(upstream.astype(jnp.float32) + weighting * differ)
    return (result.astype(jnp.bfloat16), loss_value, gradients[0], gradients[1], gradients[2], gradients[3], gradients[4], gradients[5], gradients[6], gradients[7], gradients[8], gradients[9])
```

```python
import functools
from types import SimpleNamespace

import jax
import jax.numpy as jnp
from jax import lax
from jax.experimental import pallas as pl
from jax.experimental.pallas import tpu as pltpu
from jax.sharding import PartitionSpec as P

HEAD_DIM = 64
EPS = 1e-05
MESH = pl.DeviceIdType.MESH
NCHK = 4
SKEW = 3
f32, bf16 = jnp.float32, jnp.bfloat16


class Plan:
    def __init__(self, fsdp, ctx, rows, width, head_cols, hidden, seq_len):
        self.F, self.C, self.R, self.D = fsdp, ctx, rows, width
        self.HC, self.FF = head_cols, hidden
        self.DF = width // fsdp
        self.W = -(-(seq_len // 2 - 1) // rows)
        self.N = 3 * hidden + 4 * head_cols
        self.CH = next(
            k for k in range(16, self.N + 1, 16) if self.N % k == 0 and k * self.DF >= 32768
        )
        self.NCH = self.N // self.CH
        self.base, self.total = SimpleNamespace(), 0
        peers = fsdp - 1
        for name, count in dict(
            xz=self.W, sg=self.W, xc=self.W, wd=10 * peers, wr=10 * peers,
            a=3 * NCHK, b=3 * NCHK, n2=NCHK, yb=1, dy=NCHK, dh=NCHK,
            lc=1, lr=ctx, ll=ctx, lx=peers, d1=self.W + 1, d2=self.W + 1, dz=self.W + 1,
            g1=1, g2=1, i1=1, i2=1, i3=1, gx=peers * (self.NCH + 1),
            zin=self.NCH + 1, zmid=self.NCH + 1, zout=self.NCH + 1,
        ).items():
            setattr(self.base, name, self.total)
            self.total += count


def contract(left, right, dims):
    return lax.dot_general(left, right, ((dims[:1], dims[1:]), ((), ())), preferred_element_type=f32)


def total_of(v):
    return jnp.sum(jnp.sum(v, axis=1, keepdims=True), axis=0, keepdims=True)


def scratch_of(p):
    R, D, HC, FF, DF, F, C, W = p.R, p.D, p.HC, p.FF, p.DF, p.F, p.C, p.W
    HF, Q, KR, H = R // 2, R // 4, (p.W + 1) * p.R, p.HC // HEAD_DIM
    NG = p.N + 16
    return dict(
        XB=((KR, D), bf16), SG=((W + 1, 1, R), jnp.int32), N1=((KR, D), bf16),
        WQKV=((D, 3 * HC), bf16), WO=((HC, D), bf16), WG=((D, FF), bf16),
        WU=((D, FF), bf16), WD=((FF, D), bf16),
        QB=((R, HC), bf16), KB=((KR, HC), bf16), VB=((KR, HC), bf16),
        PM=((H, R, KR), f32), S=((R, KR), f32), PB=((R, KR), bf16), DSB=((R, KR), bf16),
        BIAS=((R, KR), f32), O32=((R, HC), f32), DK32=((KR, HC), f32), DV32=((KR, HC), f32),
        OB=((R, HC), bf16), DOB=((R, HC), bf16), VC=((R, 128), f32),
        H=((HF, D), f32), DY=((HF, D), f32), DH=((HF, D), f32), P32=((HF, D), f32),
        UP=((HF, D), bf16), TE=((HF, D), bf16),
        N2=((R, D), bf16), DYB=((R, D), bf16), DHB=((R, D), bf16),
        GB=((R, FF), bf16), UB=((R, FF), bf16), AB=((R, FF), bf16),
        DGB=((R, FF), bf16), DUB=((R, FF), bf16), DA32=((R, FF), f32),
        DALL=((KR, 3 * HC), bf16),
        D1S=((W + 1, HF, D), bf16), D1R=((W + 1, HF, D), bf16), D1O=((W + 1, HF, D), f32),
        D2S=((W + 1, Q, D), bf16), D2R=((W + 1, Q, D), bf16), DZR=((W + 1, Q, D), bf16),
        DZS=((W + 1, Q, D), bf16),
        GT=((3, 8, D), f32), GR=((2, 8, D), f32),
        LT=((2, 8, 128), f32), LB=((C, 8, 128), f32), LX=((F, C, 8, 128), f32),
        XS=((F, NG, DF), bf16), XR=((F - 1, NG, DF), bf16), SI=((NG, DF), bf16),
        ZO=((NG, DF), bf16), ZI=((NG, DF), bf16),
        S1=((3, HF, D), bf16), R1=((3, HF, D), bf16), S2=((3, HF, D), bf16), R2=((3, HF, D), bf16),
    )


def layer_kernel(p, names, *refs):
    v = SimpleNamespace(**dict(zip(names, refs[18:], strict=False)))
    (
        v.x, v.upstream, v.teacher, v.valid, v.segment, v.gain_one, v.wq, v.wk, v.wv, v.wo,
        v.gain_two, v.wg, v.wu, v.wd, v.GRAD, v.GIB, v.YB, v.LOSS,
    ) = refs[:18]
    ss, rs, ls = refs[-3:]
    R, D, HC, FF, DF, F, C, W, N, CH, NCH = (
        p.R, p.D, p.HC, p.FF, p.DF, p.F, p.C, p.W, p.N, p.CH, p.NCH
    )
    HF, Q, KR, H = R // 2, R // 4, (W + 1) * R, HC // HEAD_DIM
    RC = HF // NCHK
    base = p.base
    fs, z, t = lax.axis_index("fsdp"), lax.axis_index("ctx"), lax.axis_index("tp")
    core, yy, par = lax.rem(t, 2), t // 2, lax.rem(z, 2)
    to_core, to_y = {"tp": t + 1 - 2 * core}, {"tp": lax.rem(t + 2, 4)}
    to_next, to_prev = {"ctx": lax.rem(z + 1, C)}, {"ctx": lax.rem(z + C - 1, C)}
    to_pair = {"ctx": z + 1 - 2 * par}
    has_next, has_prev = z < C - 1, z > 0
    half = C // 2
    left_side = z < half
    hop = jnp.where(left_side, z, C - 1 - z)
    step_in = jnp.where(left_side, 1, -1)
    to_inner = {"ctx": z + step_in}
    to_outer = {"ctx": lax.rem(z - step_in + C, C)}
    is_outer, is_mid = hop == 0, hop == half - 1

    def owner(d):
        return lax.rem(fs + d, F)

    def rcopy(src, dst, k, dev):
        return pltpu.make_async_remote_copy(
            src_ref=src, dst_ref=dst, send_sem=ss.at[k], recv_sem=rs.at[k],
            device_id=dev, device_id_type=MESH,
        )

    unsent = []

    def send(src, dst, k, dev, cond=None):
        if cond is None:
            rcopy(src, dst, k, dev).start()
        else:
            pl.when(cond)(lambda: rcopy(src, dst, k, dev).start())
        unsent.append((src, k, cond))

    def got(dst, k):
        rcopy(dst, dst, k, to_core).wait_recv()

    def hint(i, m):
        return pl.multiple_of(i, m)

    def rows(off, n, m=16):
        return pl.ds(hint(off, m), n)

    local = []

    def fetch(src, dst):
        cp = pltpu.make_async_copy(src, dst, ls.at[len(local)])
        cp.start()
        local.append(cp)
        return cp

    own_half = rows(core * HF, HF)
    x_copy = fetch(v.x, v.XB.at[pl.ds(0, R)])
    own_cols = pl.ds(hint(fs * DF, 128), DF)

    def by_row(dst, col0, cols):
        def region(who, off, n):
            return dst.at[rows(who * DF + off, n), pl.ds(col0, cols)]
        return region

    def by_col(dst):
        def region(who, off, n):
            return dst.at[rows(off, n), pl.ds(hint(who * DF, 128), DF)]
        return region

    weights = (
        (v.wq, by_row(v.WQKV, 0, HC), 1), (v.wk, by_row(v.WQKV, HC, HC), 1),
        (v.wv, by_row(v.WQKV, 2 * HC, HC), 1), (v.wo, by_col(v.WO), 1),
        (v.wg, by_row(v.WG, 0, FF), 2), (v.wu, by_row(v.WU, 0, FF), 2), (v.wd, by_col(v.WD), 2),
    )
    gathers = []
    count = 0
    for source, region, parts in weights:
        tall = source.shape[0]
        cut = tall // 2 // parts
        gathers.append((
            source, fetch(source, region(fs, 0, tall)),
            [(region, tall // 2, k * cut, cut, count + k) for k in range(parts)],
        ))
        count += parts
    wq, wk, wv, wo, wg, wu, wd = gathers
    te_copy = fetch(v.teacher.at[own_half], v.TE)
    up_copy = fetch(v.upstream.at[own_half], v.UP)

    barrier = pltpu.get_barrier_semaphore()

    def greet(dev):
        pl.semaphore_signal(barrier, inc=1, device_id=dev, device_id_type=MESH)

    greet(to_core)
    greet(to_y)
    for d in range(1, F):
        greet({"fsdp": owner(d)})
    pl.when(has_next)(lambda: greet(to_next))
    pl.when(has_prev)(lambda: greet(to_prev))
    pl.semaphore_wait(
        barrier, 2 + F - 1 + has_next.astype(jnp.int32) + has_prev.astype(jnp.int32)
    )

    def piece_index(kind, number, d):
        return kind + number * (F - 1) + d - 1

    for source, _, pieces in gathers:
        for region, tall, at, n, number in pieces:
            for d in range(1, F):
                off = par * tall + at
                send(
                    source.at[rows(off, n)], region(fs, off, n), piece_index(base.wd, number, d),
                    {"fsdp": owner(d)},
                )

    def relay(weight, which):
        region, tall, at, n, number = weight[2][which]
        for d in range(1, F):
            part = region(owner(F - d), par * tall + at, n)
            got(part, piece_index(base.wd, number, d))
            send(part, part, piece_index(base.wr, number, d), to_pair)

    def relayed(weight):
        weight[1].wait()
        for region, tall, at, n, number in weight[2]:
            for d in range(1, F):
                got(region(owner(F - d), (1 - par) * tall + at, n), piece_index(base.wr, number, d))

    def x_half(j, which):
        return v.XB.at[rows(j * R + which * HF, HF)]

    send(v.x.at[own_half], x_half(1, core), base.xz, to_next, has_next)
    v.SG[0] = v.segment[...]
    send(v.segment, v.SG.at[1], base.sg, to_next, has_next)
    for j in range(1, W + 1):
        @pl.when(z < j)
        def _(j=j):
            v.XB[pl.ds(j * R, R), :] = jnp.zeros((R, D), bf16)
            v.SG[j] = jnp.full((1, R), -1, jnp.int32)

    def x_pass(j):
        @pl.when(z >= j)
        def _():
            got(x_half(j, core), base.xz + j - 1)
            got(v.SG.at[j], base.sg + j - 1)
        send(x_half(j, core), x_half(j, core), base.xc + j - 1, to_core, z >= j)
        if j < W:
            both = (z >= j) & has_next
            send(x_half(j, core), x_half(j + 1, core), base.xz + j, to_next, both)
            send(v.SG.at[j], v.SG.at[j + 1], base.sg + j, to_next, both)

    def x_done(j):
        pl.when(z >= j)(lambda: got(x_half(j, 1 - core), base.xc + j - 1))

    def norm_rows(j):
        def body(i, _):
            at = rows(j * R + i * RC, RC)
            xs = v.XB[at, :].astype(f32)
            r = lax.rsqrt(jnp.mean(xs * xs, axis=-1, keepdims=True) + EPS)
            v.N1[at, :] = (xs * r * v.gain_one[...]).astype(bf16)
            return 0
        lax.fori_loop(0, R // RC, body, 0)

    x_copy.wait()
    norm_rows(0)
    relay(wq, 0)
    relay(wk, 0)
    x_pass(1)
    relay(wv, 0)

    eye = lax.broadcasted_iota(jnp.int32, (R, R), 0) == lax.broadcasted_iota(jnp.int32, (R, R), 1)

    def column(row):
        return jnp.sum(jnp.where(eye, row.astype(f32), 0.0), axis=1, keepdims=True)

    v.VC[...] = jnp.broadcast_to(column(v.valid[...]), (R, 128))
    x_done(1)
    norm_rows(1)
    for j in range(2, W + 1):
        x_pass(j)
        x_done(j)
        norm_rows(j)
    seg_col = column(v.SG[0])
    for j in range(W + 1):
        same = seg_col == v.SG[j].astype(f32)
        if j == 0:
            same = same & (
                lax.broadcasted_iota(jnp.int32, (R, R), 1) <= lax.broadcasted_iota(jnp.int32, (R, R), 0)
            )
        v.BIAS[:, pl.ds(j * R, R)] = jnp.where(same, 0.0, -1e30)
    relayed(wq)
    v.QB[...] = jnp.dot(
        v.N1[pl.ds(0, R), :], v.WQKV[:, pl.ds(0, HC)], preferred_element_type=f32
    ).astype(bf16)
    relayed(wk)
    relayed(wv)
    for dst, col in ((v.KB, HC), (v.VB, 2 * HC)):
        dst[...] = jnp.dot(
            v.N1[...], v.WQKV[:, pl.ds(col, HC)], preferred_element_type=f32
        ).astype(bf16)
    relay(wo, 0)

    AR = 64 if R % 64 == 0 else R // 4

    def of_head(ref, h):
        val = ref[...]
        lane = lax.broadcasted_iota(jnp.int32, val.shape, 1) // HEAD_DIM
        return jnp.where(lane == h, val, jnp.zeros_like(val))

    def head_forward(h):
        v.S[...] = contract(of_head(v.QB, h), v.KB[...], (1, 1))

        def soft(i, _):
            at = rows(i * AR, AR)
            s = v.S[at, :] * (HEAD_DIM**-0.5) + v.BIAS[at, :]
            e = jnp.exp(s - jnp.max(s, axis=-1, keepdims=True))
            prob = e / jnp.sum(e, axis=-1, keepdims=True)
            v.PM[h, at, :] = prob
            v.PB[at, :] = prob.astype(bf16)
            return 0

        lax.fori_loop(0, R // AR, soft, 0)
        mix = jnp.dot(v.PB[...], of_head(v.VB, h), preferred_element_type=f32)
        v.O32[...] = v.O32[...] + mix

    v.O32[...] = jnp.zeros((R, HC), f32)
    lax.fori_loop(0, H, lambda h, _: (head_forward(h), 0)[1], 0)
    v.OB[...] = v.O32[...].astype(bf16)
    relay(wg, 0)

    def chunk(i):
        return pl.ds(i * RC, RC)

    def sum_begin(a, product):
        s1, r1, s2, r2 = v.S1.at[a], v.R1.at[a], v.S2.at[a], v.R2.at[a]
        s1[...] = product((1 - core) * HF).astype(bf16)
        for i in range(NCHK):
            send(s1.at[chunk(i)], r1.at[chunk(i)], base.a + a * NCHK + i, to_core)
        v.P32[...] = product(core * HF)
        for i in range(NCHK):
            got(r1.at[chunk(i)], base.a + a * NCHK + i)
            s2[chunk(i), :] = (v.P32[chunk(i), :] + r1[chunk(i), :].astype(f32)).astype(bf16)
            send(s2.at[chunk(i)], r2.at[chunk(i)], base.b + a * NCHK + i, to_y)

    def sum_end(a, i):
        s2, r2 = v.S2.at[a], v.R2.at[a]
        got(r2.at[chunk(i)], base.b + a * NCHK + i)
        return s2[chunk(i), :].astype(f32) + r2[chunk(i), :].astype(f32)

    def my_rows(i):
        return rows(core * HF + i * RC, RC)

    def their_rows(i):
        return rows((1 - core) * HF + i * RC, RC)

    def share(ref, flow, i):
        send(ref.at[my_rows(i)], ref.at[my_rows(i)], flow + i, to_core)

    def shared(ref, flow):
        for i in range(NCHK):
            got(ref.at[their_rows(i)], flow + i)

    relayed(wo)
    sum_begin(
        0,
        lambda off: jnp.dot(v.OB[rows(off, HF), :], v.WO[...], preferred_element_type=f32),
    )
    relay(wg, 1)
    for i in range(NCHK):
        h_now = v.XB[my_rows(i), :].astype(f32) + sum_end(0, i)
        v.H[chunk(i), :] = h_now
        r = lax.rsqrt(jnp.mean(h_now * h_now, axis=-1, keepdims=True) + EPS)
        v.N2[my_rows(i), :] = (h_now * r * v.gain_two[...]).astype(bf16)
        share(v.N2, base.n2, i)
    relay(wu, 0)
    relay(wu, 1)
    shared(v.N2, base.n2)

    relayed(wg)
    v.GB[...] = jnp.dot(v.N2[...], v.WG[...], preferred_element_type=f32).astype(bf16)
    relay(wd, 0)
    relayed(wu)
    v.UB[...] = jnp.dot(v.N2[...], v.WU[...], preferred_element_type=f32).astype(bf16)

    def activate(i, _):
        at = rows(i * RC, RC)
        g, u = v.GB[at, :].astype(f32), v.UB[at, :].astype(f32)
        v.AB[at, :] = (g / (1.0 + jnp.exp(-g)) * u).astype(bf16)
        return 0

    lax.fori_loop(0, R // RC, activate, 0)
    relay(wd, 1)
    relayed(wd)
    sum_begin(
        1,
        lambda off: jnp.dot(v.AB[rows(off, HF), :], v.WD[...], preferred_element_type=f32),
    )
    te_copy.wait()
    up_copy.wait()
    squares, counted = jnp.zeros((1, 1), f32), jnp.zeros((1, 1), f32)
    for i in range(NCHK):
        y_now = v.H[chunk(i), :] + sum_end(1, i)
        v.YB[my_rows(i), :] = y_now.astype(bf16)
        weighting = v.VC[my_rows(i), pl.ds(0, 1)]
        differ = y_now - v.TE[chunk(i), :].astype(f32)
        squares = squares + total_of(weighting * differ * differ)
        counted = counted + total_of(weighting)
        dy = v.UP[chunk(i), :].astype(f32) + weighting * differ
        v.DY[chunk(i), :] = dy
        v.DYB[my_rows(i), :] = dy.astype(bf16)
        share(v.DYB, base.dy, i)
    tile_row = lax.broadcasted_iota(jnp.int32, (8, 128), 0)
    v.LT[0] = jnp.where(
        tile_row == 0, jnp.broadcast_to(squares, (8, 128)), jnp.broadcast_to(counted, (8, 128))
    )
    send(v.LT.at[0], v.LT.at[1], base.lc, to_core)
    y_half = v.YB.at[own_half]
    send(y_half, y_half, base.yb, to_core)
    shared(v.DYB, base.dy)

    def weight_grad(left, right, at, d, tokens=R, col=None, n=None):
        who = owner(d)
        lhs = left[...] if col is None else left[pl.ds(0, tokens), pl.ds(col, n)]
        n = lhs.shape[1]
        if d == 0:
            own_done[0] = at + n
        rhs = right[pl.ds(0, tokens), pl.ds(hint(who * DF, 128), DF)]
        v.XS[who, pl.ds(at, n), :] = contract(lhs, rhs, (0, 0)).astype(bf16)

    def grad_index(d, j):
        return base.gx + (d - 1) * (NCH + 1) + j

    def grad_send(d, at, j):
        rcopy(
            v.XS.at[owner(d), at], v.XR.at[d - 1, at], grad_index(d, j), {"fsdp": owner(d)}
        ).start()

    sent, own_done = [0], [0]

    def grads_ready(upto):
        first, last = sent[0], upto // CH
        sent[0] = last

        def body(j, _):
            for d in range(1, F):
                grad_send(d, rows(j * CH, CH), j)
            return 0

        if last > first:
            lax.fori_loop(first, last, body, 0)

    def inward(at, j):
        for d in range(1, F):
            got(v.XR.at[d - 1, at], grad_index(d, j))
        acc = v.XS[fs, at, :].astype(f32)
        for d in range(1, F):
            acc = acc + v.XR[d - 1, at, :].astype(f32)
        v.SI[at, :] = acc.astype(bf16)

        @pl.when(jnp.logical_not(is_outer))
        def _():
            got(v.ZO.at[at], base.zin + j)
            v.SI[at, :] = (acc + v.ZO[at, :].astype(f32)).astype(bf16)

        @pl.when(is_mid)
        def _():
            rcopy(v.SI.at[at], v.ZI.at[at], base.zmid + j, to_inner).start()

        @pl.when(jnp.logical_not(is_mid))
        def _():
            rcopy(v.SI.at[at], v.ZO.at[at], base.zin + j, to_inner).start()

    def outward(at, j):
        @pl.when(is_mid)
        def _():
            got(v.ZI.at[at], base.zmid + j)
            whole = v.SI[at, :].astype(f32) + v.ZI[at, :].astype(f32)
            v.GRAD[at, :] = whole.astype(bf16)

        @pl.when(jnp.logical_not(is_mid))
        def _():
            got(v.ZI.at[at], base.zout + j)
            v.GRAD[at, :] = v.ZI[at, :]

        @pl.when(jnp.logical_not(is_outer))
        def _():
            rcopy(v.GRAD.at[at], v.ZI.at[at], base.zout + j, to_outer).start()

    lag_in, lag_out = SKEW * hop, SKEW * (2 * half - 1 - hop)
    LAST = NCH + SKEW * (2 * half - 1)

    def pump(first, last):
        def body(i, _):
            ja, jb = i - lag_in, i - lag_out
            pl.when((ja >= 0) & (ja < NCH))(lambda: inward(rows(ja * CH, CH), ja))
            pl.when((jb >= 0) & (jb < NCH))(lambda: outward(rows(jb * CH, CH), jb))
            return 0

        if last > first:
            lax.fori_loop(first, last, body, 0)

    pumped = [0]

    def pump_to(last):
        ready = min(sent[0], own_done[0] // CH)
        last = min(last, ready if ready < NCH else LAST)
        if last > pumped[0]:
            pump(pumped[0], last)
            pumped[0] = last

    peers = range(1, F)
    for d in peers:
        weight_grad(v.AB, v.DYB, 0, d)
    grads_ready(FF)
    v.DA32[...] = contract(v.DYB[...], v.WD[...], (1, 1))

    def activate_back(i, _):
        at = rows(i * RC, RC)
        g, u, da = v.GB[at, :].astype(f32), v.UB[at, :].astype(f32), v.DA32[at, :]
        sig = 1.0 / (1.0 + jnp.exp(-g))
        v.DGB[at, :] = (da * u * (sig * (1.0 + g * (1.0 - sig)))).astype(bf16)
        v.DUB[at, :] = (da * (g * sig)).astype(bf16)
        return 0

    lax.fori_loop(0, R // RC, activate_back, 0)
    sum_begin(
        2,
        lambda off: contract(v.DGB[rows(off, HF), :], v.WG[...], (1, 1))
        + contract(v.DUB[rows(off, HF), :], v.WU[...], (1, 1)),
    )
    weight_grad(v.AB, v.DYB, 0, 0)
    for d in peers:
        weight_grad(v.DGB, v.N2, FF, d)
    grads_ready(2 * FF)
    pump_to(2)
    for i in range(NCHK):
        dn2 = sum_end(2, i)
        h_now = v.H[chunk(i), :]
        r = lax.rsqrt(jnp.mean(h_now * h_now, axis=-1, keepdims=True) + EPS)
        gd = v.gain_two[...] * dn2
        dh = v.DY[chunk(i), :] + r * gd - h_now * (
            r * r * r * jnp.mean(gd * h_now, axis=-1, keepdims=True)
        )
        v.DH[chunk(i), :] = dh
        v.DHB[my_rows(i), :] = dh.astype(bf16)
        share(v.DHB, base.dh, i)
        part = jnp.sum(dn2 * h_now * r, axis=0, keepdims=True)
        part = jnp.where(yy == i // (NCHK // 2), part, 0.0)
        if i == 0:
            v.GT[0] = jnp.zeros((8, D), f32)
        v.GT[0, pl.ds(0, 1), :] = v.GT[0, pl.ds(0, 1), :] + part
    for d in peers:
        weight_grad(v.DUB, v.N2, 2 * FF, d)
    grads_ready(3 * FF)
    weight_grad(v.DGB, v.N2, FF, 0)
    weight_grad(v.DUB, v.N2, 2 * FF, 0)
    shared(v.DHB, base.dh)
    v.DOB[...] = contract(v.DHB[...], v.WO[...], (1, 1)).astype(bf16)
    pump_to(6)
    for d in peers:
        weight_grad(v.OB, v.DHB, 3 * FF, d)
    grads_ready(3 * FF + HC)
    weight_grad(v.OB, v.DHB, 3 * FF, 0)
    pump_to(10)

    v.O32[...] = jnp.zeros((R, HC), f32)
    v.DK32[...] = jnp.zeros((KR, HC), f32)
    v.DV32[...] = jnp.zeros((KR, HC), f32)

    def head_backward(h):
        doh = of_head(v.DOB, h)
        v.S[...] = contract(doh, v.VB[...], (1, 1))

        def soft_back(i, _):
            at = rows(i * AR, AR)
            prob, dp = v.PM[h, at, :], v.S[at, :]
            ds = prob * (dp - jnp.sum(prob * dp, axis=-1, keepdims=True))
            v.PB[at, :] = prob.astype(bf16)
            v.DSB[at, :] = ds.astype(bf16)
            return 0

        lax.fori_loop(0, R // AR, soft_back, 0)
        v.DV32[...] = v.DV32[...] + contract(v.PB[...], doh, (0, 0))
        v.O32[...] = v.O32[...] + jnp.dot(
            v.DSB[...], of_head(v.KB, h), preferred_element_type=f32
        )
        v.DK32[...] = v.DK32[...] + contract(v.DSB[...], of_head(v.QB, h), (0, 0))

    lax.fori_loop(0, H, lambda h, _: (head_backward(h), 0)[1], 0)
    scale = HEAD_DIM**-0.5
    v.DALL[pl.ds(0, R), pl.ds(0, HC)] = (v.O32[...] * scale).astype(bf16)
    v.DALL[:, pl.ds(HC, HC)] = (v.DK32[...] * scale).astype(bf16)
    v.DALL[:, pl.ds(2 * HC, HC)] = v.DV32[...].astype(bf16)
    pump_to(16)

    def dn1_product(j, which):
        at = rows(j * R + which * HF, HF)
        c0 = 0 if j == 0 else HC
        return contract(
            v.DALL[at, pl.ds(c0, 3 * HC - c0)], v.WQKV[:, pl.ds(c0, 3 * HC - c0)], (1, 1)
        )

    for j in range(W, -1, -1):
        v.D1S[j] = dn1_product(j, 1 - core).astype(bf16)
        send(v.D1S.at[j], v.D1R.at[j], base.d1 + j, to_core)
        v.D1O[j] = dn1_product(j, core)
    for d in list(peers) + [0]:
        at = 3 * FF + HC
        weight_grad(v.DALL, v.N1, at, d, R, 0, HC)
        weight_grad(v.DALL, v.N1, at + HC, d, KR, HC, HC)
        weight_grad(v.DALL, v.N1, at + 2 * HC, d, KR, 2 * HC, HC)
        if d == F - 1:
            grads_ready(N)
    for j in range(W, -1, -1):
        got(v.D1R.at[j], base.d1 + j)
        there = rows((1 - yy) * Q, Q)
        v.D2S[j] = (v.D1O[j, there, :] + v.D1R[j, there, :].astype(f32)).astype(bf16)
        send(v.D2S.at[j], v.D2R.at[j], base.d2 + j, to_y)
    pump_to(20)
    here = rows(yy * Q, Q)
    for j in range(W, 0, -1):
        got(v.D2R.at[j], base.d2 + j)
        own = v.D1O[j, here, :] + v.D1R[j, here, :].astype(f32) + v.D2R[j].astype(f32)
        v.DZS[j] = own.astype(bf16)
        if j < W:
            @pl.when(has_next & (z >= j))
            def _(j=j, own=own):
                got(v.DZR.at[j + 1], base.dz + j + 1)
                v.DZS[j] = (own + v.DZR[j + 1].astype(f32)).astype(bf16)
        send(v.DZS.at[j], v.DZR.at[j], base.dz + j, to_prev, z >= j)
        pump_to(26 + 3 * (W - j))

    got(v.LT.at[1], base.lc)
    v.LB[z] = v.LT[0] + v.LT[1]
    for s in range(C - 1):
        left_tile, right_tile = z - s, z + s
        send(v.LB.at[jnp.maximum(left_tile, 0)], v.LB.at[jnp.maximum(left_tile, 0)],
             base.lr + s, to_next, has_next & (left_tile >= 0))
        send(v.LB.at[jnp.minimum(right_tile, C - 1)], v.LB.at[jnp.minimum(right_tile, C - 1)],
             base.ll + s, to_prev, has_prev & (right_tile <= C - 1))
        if s == 0:
            pump_to(30)
        pl.when(left_tile - 1 >= 0)(
            lambda i=left_tile - 1, s=s: got(v.LB.at[jnp.maximum(i, 0)], base.lr + s)
        )
        pl.when(right_tile + 1 <= C - 1)(
            lambda i=right_tile + 1, s=s: got(v.LB.at[jnp.minimum(i, C - 1)], base.ll + s)
        )
    v.LX[fs] = v.LB[...]
    for d in peers:
        send(v.LB, v.LX.at[fs], base.lx + d - 1, {"fsdp": owner(d)})

    pump_to(34)
    got(v.D2R.at[0], base.d2)
    v.P32[pl.ds(0, Q), :] = (
        v.D1O[0, here, :] + v.D1R[0, here, :].astype(f32) + v.D2R[0].astype(f32)
    )

    @pl.when(has_next)
    def _():
        got(v.DZR.at[1], base.dz + 1)
        v.P32[pl.ds(0, Q), :] = v.P32[pl.ds(0, Q), :] + v.DZR[1].astype(f32)

    quarter = rows(core * HF + yy * Q, Q)
    dn1 = v.P32[pl.ds(0, Q), :]
    x_now = v.XB[quarter, :].astype(f32)
    r = lax.rsqrt(jnp.mean(x_now * x_now, axis=-1, keepdims=True) + EPS)
    gd = v.gain_one[...] * dn1
    gi = v.DH[here, :] + r * gd - x_now * (
        r * r * r * jnp.mean(gd * x_now, axis=-1, keepdims=True)
    )
    v.GIB[quarter, :] = gi.astype(bf16)
    mine = v.GIB.at[quarter]
    send(mine, mine, base.i1, to_y)
    send(mine, mine, base.i2, to_core)
    v.GT[0, pl.ds(1, 1), :] = jnp.sum(dn1 * x_now * r, axis=0, keepdims=True)
    send(v.GT.at[0], v.GR.at[0], base.g1, to_core)
    pump_to(38)
    got(v.GR.at[0], base.g1)
    v.GT[1] = v.GT[0] + v.GR[0]
    send(v.GT.at[1], v.GR.at[1], base.g2, to_y)
    from_y = v.GIB.at[rows(core * HF + (1 - yy) * Q, Q)]
    got(from_y, base.i1)
    send(from_y, from_y, base.i3, to_core)
    pump_to(42)
    got(v.GR.at[1], base.g2)
    v.GT[2] = v.GT[1] + v.GR[1]
    for d in list(peers) + [0]:
        tile = v.GT[2, :, pl.ds(hint(owner(d) * DF, 128), DF)]
        v.XS[owner(d), pl.ds(N, 16), :] = jnp.concatenate([tile, jnp.zeros_like(tile)], 0).astype(bf16)
        if d:
            grad_send(d, pl.ds(N, 16), NCH)

    for d in peers:
        got(v.LX.at[owner(F - d)], base.lx + d - 1)
    sums = [sum(v.LX[s, c] for c in range(C)) for s in range(F)]
    counted = sum(s[1:2, :] for s in sums)
    for s in range(F):
        v.LOSS[pl.ds(s, 1), :] = sums[s][0:1, :] * F / (counted * D)

    pump_to(LAST - SKEW * (2 * half - 1))
    gain_rows = pl.ds(N, 16)
    inward(gain_rows, NCH)
    pump_to(LAST)
    outward(gain_rows, NCH)
    got(v.YB.at[rows((1 - core) * HF, HF)], base.yb)
    got(v.GIB.at[rows((1 - core) * HF + yy * Q, Q)], base.i2)
    got(v.GIB.at[rows((1 - core) * HF + (1 - yy) * Q, Q)], base.i3)

    def left(src, k):
        rcopy(src, src, k, to_core).wait_send()

    for src, k, cond in unsent:
        if cond is None:
            left(src, k)
        else:
            pl.when(cond)(functools.partial(left, src, k))

    def drain(at, j):
        for d in peers:
            left(v.XS.at[owner(d), at], grad_index(d, j))
        pl.when(is_mid)(lambda: left(v.SI.at[at], base.zmid + j))
        pl.when(jnp.logical_not(is_mid))(lambda: left(v.SI.at[at], base.zin + j))
        pl.when(jnp.logical_not(is_outer))(lambda: left(v.GRAD.at[at], base.zout + j))

    lax.fori_loop(0, NCH, lambda j, _: (drain(rows(j * CH, CH), j), 0)[1], 0)
    drain(gain_rows, NCH)


def finish_kernel(p, grad, gib, yb, loss, y_out, loss_out, gi_out, one, gq, gk, gv, go, two, gg, gu, gd):
    FF, HC, N = p.FF, p.HC, p.N
    y_out[0] = yb[...]
    gi_out[0] = gib[...].astype(f32)
    at = 3 * FF
    gd[...] = grad[pl.ds(0, FF), :].astype(f32)
    go[...] = grad[pl.ds(at, HC), :].astype(f32)
    for ref, first, n in (
        (gg, FF, FF), (gu, 2 * FF, FF), (gq, at + HC, HC), (gk, at + 2 * HC, HC), (gv, at + 3 * HC, HC),
    ):
        for c in range(0, n, 128):
            w = min(128, n - c)
            ref[:, pl.ds(c, w)] = grad[pl.ds(first + c, w), :].astype(f32).T
    gains = grad[pl.ds(N, 16), :].astype(f32)
    two[...] = gains[0:1, :]
    one[...] = gains[1:2, :]
    for s in range(p.F):
        loss_out[s] = jnp.max(loss[pl.ds(s, 1), :])


def shards(mesh_shape, seq_len, *args):
    (inputs, upstream, teacher, valid, segment, gain_one, wq, wk, wv, wo, gain_two, wg, wu, wd) = args
    _, rows_here, width = inputs.shape
    p = Plan(
        mesh_shape["fsdp"], mesh_shape["ctx"], rows_here, width, wq.shape[1], wg.shape[1], seq_len
    )
    R, D, DF, HC, FF, F = p.R, p.D, p.DF, p.HC, p.FF, p.F
    NG = p.N + 16
    scratch = scratch_of(p)
    vmem = pl.BlockSpec(memory_space=pltpu.VMEM)
    anywhere = pl.BlockSpec(memory_space=pl.ANY)
    in_specs = [anywhere] * 3 + [vmem] * 3 + [anywhere] * 4 + [vmem] + [anywhere] * 3
    sds = jax.ShapeDtypeStruct
    grad, gib, yb, loss = pl.pallas_call(
        functools.partial(layer_kernel, p, tuple(scratch)),
        out_shape=(
            sds((NG, DF), bf16), sds((R, D), bf16), sds((R, D), bf16), sds((max(F, 8), 128), f32),
        ),
        in_specs=in_specs,
        out_specs=(vmem,) * 4,
        scratch_shapes=[pltpu.VMEM(s, dt) for s, dt in scratch.values()]
        + [
            pltpu.SemaphoreType.DMA((p.total,)), pltpu.SemaphoreType.DMA((p.total,)),
            pltpu.SemaphoreType.DMA((10,)),
        ],
        compiler_params=pltpu.CompilerParams(
            collective_id=0, has_side_effects=True, vmem_limit_bytes=67043328
        ),
        name="layer",
    )(
        inputs.reshape(R, D), upstream.reshape(R, D), teacher.reshape(R, D), valid, segment,
        gain_one.reshape(1, D), wq, wk, wv, wo, gain_two.reshape(1, D), wg, wu, wd,
    )
    outs = pl.pallas_call(
        functools.partial(finish_kernel, p),
        out_shape=(
            sds((1, R, D), bf16), sds((F,), f32), sds((1, R, D), f32), sds((1, DF), f32),
            sds((DF, HC), f32), sds((DF, HC), f32), sds((DF, HC), f32), sds((HC, DF), f32),
            sds((1, DF), f32), sds((DF, FF), f32), sds((DF, FF), f32), sds((FF, DF), f32),
        ),
        in_specs=[vmem] * 4,
        out_specs=(vmem, pl.BlockSpec(memory_space=pltpu.SMEM)) + (vmem,) * 10,
        compiler_params=pltpu.CompilerParams(vmem_limit_bytes=40 * 2**20),
        name="finish",
    )(grad, gib, yb, loss)
    outs = list(outs)
    outs[3], outs[8] = outs[3].reshape(DF), outs[8].reshape(DF)
    return tuple(outs)


def solution(mesh):
    def run(*args):
        token, row, col = P("fsdp", "ctx", None), P("fsdp", "tp"), P("tp", "fsdp")
        pair = P("fsdp", "ctx")
        return jax.shard_map(
            functools.partial(shards, dict(mesh.shape), args[0].shape[1]),
            mesh=mesh,
            in_specs=(token, token, token, pair, pair, P(), row, row, row, col, P(), row, row, col),
            out_specs=(
                token, P(), token, P("fsdp"), row, row, row, col, P("fsdp"), row, row, col,
            ),
            check_vma=False,
        )(*args)

    return run
```

```python
import functools
from types import SimpleNamespace

import jax
import jax.numpy as jnp
from jax import lax
from jax.experimental import pallas as pl
from jax.experimental.pallas import tpu as pltpu
from jax.sharding import PartitionSpec as P

HEAD_DIM = 64
EPS = 1e-05
MESH = pl.DeviceIdType.MESH
NCHK = 4
SKEW = 3
f32, bf16 = jnp.float32, jnp.bfloat16


class Plan:
    def __init__(self, fsdp, ctx, rows, width, head_cols, hidden, seq_len):
        self.F, self.C, self.R, self.D = fsdp, ctx, rows, width
        self.HC, self.FF = head_cols, hidden
        self.DF = width // fsdp
        self.W = -(-(seq_len // 2) // rows)
        self.N = 3 * hidden + 4 * head_cols
        self.CH = next(
            k for k in range(16, self.N + 1, 16) if self.N % k == 0 and k * self.DF >= 32768
        )
        self.NCH = self.N // self.CH
        self.base, self.total = SimpleNamespace(), 0
        peers = fsdp - 1
        for name, count in dict(
            xz=self.W, sg=self.W, xy=self.W, xc=self.W, wd=10 * peers, wr=10 * peers,
            a=3 * NCHK, b=3 * NCHK, n2=NCHK, yb=1, dy=NCHK, dh=NCHK,
            lc=1, lr=ctx, ll=ctx, lx=peers, d1=self.W + 1, d2=self.W + 1, dz=self.W + 1,
            g1=1, g2=1, i1=1, i2=1, i3=1, gx=peers * (self.NCH + 1),
            zo=self.NCH + 1, zi=self.NCH + 1,
        ).items():
            setattr(self.base, name, self.total)
            self.total += count
        self.sends = 4 * self.W + 2 + 14 * peers + 9 + 3 + 2 * ctx + peers + 3 * self.W + 2 + 5 + peers + 2


def contract(left, right, dims):
    return lax.dot_general(left, right, ((dims[:1], dims[1:]), ((), ())), preferred_element_type=f32)


def total_of(v):
    return jnp.sum(jnp.sum(v, axis=1, keepdims=True), axis=0, keepdims=True)


def scratch_of(p):
    R, D, HC, FF, DF, F, C, W = p.R, p.D, p.HC, p.FF, p.DF, p.F, p.C, p.W
    HF, Q, KR, H = R // 2, R // 4, (p.W + 1) * p.R, p.HC // HEAD_DIM
    NG = p.N + 16
    return dict(
        XB=((KR, D), bf16), SG=((W + 1, 1, R), jnp.int32), N1=((KR, D), bf16),
        WQKV=((D, 3 * HC), bf16), WO=((HC, D), bf16), WG=((FF, D), bf16),
        WU=((FF, D), bf16), WD=((FF, D), bf16),
        QH=((H * R, HC), bf16), KB=((KR, HC), bf16), VB=((KR, HC), bf16), DOH=((H * R, HC), bf16),
        PM=((H * R, W * R), f32), S=((H * R, KR), f32), PB=((H * R, KR), bf16), DSB=((H * R, KR), bf16),
        BIAS=((R, W * R), f32), DQ=((R, HC), bf16), DKT=((HC, KR), bf16), DVT=((HC, KR), bf16),
        OB=((R, HC), bf16), VC=((R, 128), f32),
        H=((HF, D), f32), DY=((HF, D), f32), DH=((HF, D), f32), P32=((HF, D), f32),
        UP=((HF, D), bf16), TE=((HF, D), bf16),
        N2=((R, D), bf16), DYB=((R, D), bf16), DHB=((R, D), bf16),
        GB=((R, FF), bf16), UB=((R, FF), bf16), AB=((R, FF), bf16),
        DGB=((R, FF), bf16), DUB=((R, FF), bf16),
        D1S=((W + 1, HF, D), bf16), D1R=((W + 1, HF, D), bf16), D1O=((W + 1, HF, D), f32),
        D2S=((W + 1, Q, D), bf16), D2R=((W + 1, Q, D), bf16), DZR=((W + 1, Q, D), bf16),
        DZS=((W + 1, Q, D), bf16),
        GT=((3, 8, D), f32), GR=((2, 8, D), f32),
        LT=((2, 8, 128), f32), LB=((C, 8, 128), f32), LX=((F, C, 8, 128), f32),
        XS=((F, NG, DF), bf16), XR=((F - 1, NG, DF), bf16),
        ZO=((NG, DF), bf16), ZI=((NG, DF), bf16), GRAD=((NG, DF), bf16), GIB=((R, D), bf16),
        YB=((R, D), bf16), LOSS=((max(F, 8), 128), f32),
        S1=((3, HF, D), bf16), R1=((3, HF, D), bf16), S2=((3, HF, D), bf16), R2=((3, HF, D), bf16),
    )


def layer_kernel(p, names, *refs):
    v = SimpleNamespace(**dict(zip(names, refs[18:], strict=False)))
    (
        v.x, v.upstream, v.teacher, v.valid, v.segment, v.gain_one, v.wq, v.wk, v.wv, v.wo,
        v.gain_two, v.wg, v.wu, v.wd, v.grad_out, v.gi_out, v.y_out, v.loss_out,
    ) = refs[:18]
    ss, rs, ls = refs[-3:]
    R, D, HC, FF, DF, F, C, W, N, CH, NCH = (
        p.R, p.D, p.HC, p.FF, p.DF, p.F, p.C, p.W, p.N, p.CH, p.NCH
    )
    HF, Q, KR, H = R // 2, R // 4, (W + 1) * R, HC // HEAD_DIM
    RC = HF // NCHK
    base = p.base
    fs, z, t = lax.axis_index("fsdp"), lax.axis_index("ctx"), lax.axis_index("tp")
    core, yy, par = lax.rem(t, 2), t // 2, lax.rem(z, 2)
    to_core, to_y = {"tp": t + 1 - 2 * core}, {"tp": lax.rem(t + 2, 4)}
    to_next, to_prev = {"ctx": lax.rem(z + 1, C)}, {"ctx": lax.rem(z + C - 1, C)}
    to_pair = {"ctx": z + 1 - 2 * par}
    has_next, has_prev = z < C - 1, z > 0
    half = C // 2
    left_side = z < half
    hop = jnp.where(left_side, z, C - 1 - z)
    step_in = jnp.where(left_side, 1, -1)
    to_inner = {"ctx": z + step_in}
    to_outer = {"ctx": lax.rem(z - step_in + C, C)}
    is_outer, is_mid = hop == 0, hop == half - 1

    def owner(d):
        return lax.rem(fs + d, F)

    def rcopy(src, dst, sk, rk, dev):
        return pltpu.make_async_remote_copy(
            src_ref=src, dst_ref=dst, send_sem=ss.at[sk], recv_sem=rs.at[rk],
            device_id=dev, device_id_type=MESH,
        )

    unsent = []

    def outgoing(src, cond=None):
        unsent.append((src, cond))
        assert len(unsent) <= p.sends
        return len(unsent) - 1

    def send(src, dst, k, dev, cond=None, group=None):
        sk = outgoing(src, cond) if group is None else group
        if cond is None:
            rcopy(src, dst, sk, k, dev).start()
        else:
            pl.when(cond)(lambda: rcopy(src, dst, sk, k, dev).start())

    def got(dst, k):
        rcopy(dst, dst, 0, k, to_core).wait_recv()

    def hint(i, m):
        return pl.multiple_of(i, m)

    def rows(off, n, m=16):
        return pl.ds(hint(off, m), n)

    local = []

    def fetch(src, dst):
        cp = pltpu.make_async_copy(src, dst, ls.at[len(local)])
        cp.start()
        local.append(cp)
        return cp

    own_half = rows(core * HF, HF)
    x_copy = fetch(v.x, v.XB.at[pl.ds(0, R)])
    own_cols = pl.ds(hint(fs * DF, 128), DF)

    def by_row(dst, col0, cols):
        def region(who, off, n):
            return dst.at[rows(who * DF + off, n), pl.ds(col0, cols)]
        return region

    def by_col(dst):
        def region(who, off, n):
            return dst.at[rows(off, n), pl.ds(hint(who * DF, 128), DF)]
        return region

    weights = (
        (v.wq, by_row(v.WQKV, 0, HC), 1), (v.wk, by_row(v.WQKV, HC, HC), 1),
        (v.wv, by_row(v.WQKV, 2 * HC, HC), 1), (v.wo, by_col(v.WO), 1),
        (v.wg, by_col(v.WG), 2), (v.wu, by_col(v.WU), 2), (v.wd, by_col(v.WD), 2),
    )
    gathers = []
    count = 0
    for source, region, parts in weights:
        tall = source.shape[0]
        cut = tall // 2 // parts
        gathers.append((
            source, fetch(source, region(fs, 0, tall)),
            [(region, tall // 2, k * cut, cut, count + k) for k in range(parts)],
        ))
        count += parts
    wq, wk, wv, wo, wg, wu, wd = gathers
    te_copy = fetch(v.teacher.at[own_half], v.TE)
    up_copy = fetch(v.upstream.at[own_half], v.UP)

    barrier = pltpu.get_barrier_semaphore()

    def greet(dev):
        pl.semaphore_signal(barrier, inc=1, device_id=dev, device_id_type=MESH)

    greet(to_core)
    greet(to_y)
    for d in range(1, F):
        greet({"fsdp": owner(d)})
    pl.when(has_next)(lambda: greet(to_next))
    pl.when(has_prev)(lambda: greet(to_prev))
    pl.semaphore_wait(
        barrier, 2 + F - 1 + has_next.astype(jnp.int32) + has_prev.astype(jnp.int32)
    )

    def piece_index(kind, number, d):
        return kind + number * (F - 1) + d - 1

    for source, _, pieces in gathers:
        tall = source.shape[0] // 2
        for d in range(1, F):
            group = outgoing(source.at[rows(par * tall, tall)])
            for region, _, at, n, number in pieces:
                off = par * tall + at
                send(
                    source.at[rows(off, n)], region(fs, off, n), piece_index(base.wd, number, d),
                    {"fsdp": owner(d)}, None, group,
                )

    relays = {}

    def relay(weight, which):
        region, tall, at, n, number = weight[2][which]
        for d in range(1, F):
            if which == 0:
                relays[number, d] = outgoing(region(owner(F - d), par * tall, tall))
            part = region(owner(F - d), par * tall + at, n)
            got(part, piece_index(base.wd, number, d))
            send(
                part, part, piece_index(base.wr, number, d), to_pair, None, relays[number - which, d]
            )

    def relayed(weight):
        weight[1].wait()
        for region, tall, at, n, number in weight[2]:
            for d in range(1, F):
                got(region(owner(F - d), (1 - par) * tall + at, n), piece_index(base.wr, number, d))

    def x_half(j, which):
        return v.XB.at[rows(j * R + which * HF, HF)]

    def x_quarter(j, y):
        return v.XB.at[rows(j * R + core * HF + y * Q, Q)]

    send(v.x.at[rows(core * HF + yy * Q, Q)], x_quarter(1, yy), base.xz, to_next, has_next)
    v.SG[0] = v.segment[...]
    send(v.segment, v.SG.at[1], base.sg, to_next, has_next)
    for j in range(1, W + 1):
        @pl.when(z < j)
        def _(j=j):
            v.XB[pl.ds(j * R, R), :] = jnp.zeros((R, D), bf16)
            v.SG[j] = jnp.full((1, R), -1, jnp.int32)

    def x_pass(j):
        @pl.when(z >= j)
        def _():
            got(x_quarter(j, yy), base.xz + j - 1)
            got(v.SG.at[j], base.sg + j - 1)
        if j < W:
            both = (z >= j) & has_next
            send(x_quarter(j, yy), x_quarter(j + 1, yy), base.xz + j, to_next, both)
            send(v.SG.at[j], v.SG.at[j + 1], base.sg + j, to_next, both)
        send(x_quarter(j, yy), x_quarter(j, yy), base.xy + j - 1, to_y, z >= j)

    def x_join(j):
        pl.when(z >= j)(lambda: got(x_quarter(j, 1 - yy), base.xy + j - 1))
        send(x_half(j, core), x_half(j, core), base.xc + j - 1, to_core, z >= j)

    def x_done(j):
        pl.when(z >= j)(lambda: got(x_half(j, 1 - core), base.xc + j - 1))

    def norm_rows(j):
        def body(i, _):
            at = rows(j * R + i * RC, RC)
            xs = v.XB[at, :].astype(f32)
            r = lax.rsqrt(jnp.mean(xs * xs, axis=-1, keepdims=True) + EPS)
            v.N1[at, :] = (xs * r * v.gain_one[...]).astype(bf16)
            return 0
        lax.fori_loop(0, R // RC, body, 0)

    eye = lax.broadcasted_iota(jnp.int32, (R, R), 0) == lax.broadcasted_iota(jnp.int32, (R, R), 1)
    lower = lax.broadcasted_iota(jnp.int32, (R, R), 1) <= lax.broadcasted_iota(jnp.int32, (R, R), 0)

    def column(row):
        return jnp.sum(jnp.where(eye, row.astype(f32), 0.0), axis=1, keepdims=True)

    x_copy.wait()
    norm_rows(0)
    v.VC[...] = jnp.broadcast_to(column(v.valid[...]), (R, 128))
    relay(wq, 0)
    x_pass(1)
    relay(wk, 0)
    relay(wv, 0)
    x_join(1)
    x_done(1)
    norm_rows(1)
    for j in range(2, W + 1):
        x_pass(j)
        if j == 2:
            relay(wo, 0)
            relay(wg, 0)
        x_join(j)
        x_done(j)
        norm_rows(j)
    if W < 2:
        relay(wo, 0)
        relay(wg, 0)
    seg_col = column(v.SG[0])
    for j in range(W):
        seg_row = jnp.broadcast_to(v.SG[j].astype(f32), (R, R))
        if j == 0:
            seg_row = jnp.where(lower, seg_row, v.SG[W].astype(f32))
        v.BIAS[:, pl.ds(j * R, R)] = jnp.where(seg_col == seg_row, 0.0, -1e30)
    relayed(wq)
    lane_head = lax.broadcasted_iota(jnp.int32, (R, HC), 1) // HEAD_DIM

    def by_heads(ref, val):
        for h in range(H):
            ref[pl.ds(h * R, R), :] = jnp.where(lane_head == h, val, 0.0).astype(bf16)

    def from_heads(ref, other):
        mix = jnp.zeros((R, HC), f32)
        for h in range(H):
            part = jnp.dot(ref[pl.ds(h * R, R), :], other[...], preferred_element_type=f32)
            mix = jnp.where(lane_head == h, part, mix)
        return mix

    by_heads(
        v.QH,
        jnp.dot(v.N1[pl.ds(0, R), :], v.WQKV[:, pl.ds(0, HC)], preferred_element_type=f32),
    )
    relayed(wk)
    relayed(wv)
    for dst, col in ((v.KB, HC), (v.VB, 2 * HC)):
        dst[...] = jnp.dot(
            v.N1[...], v.WQKV[:, pl.ds(col, HC)], preferred_element_type=f32
        ).astype(bf16)
    relay(wg, 1)

    AR = 64 if R % 64 == 0 else R // 4
    WR = W * R

    def merged(i):
        at, inner = rows(i * AR, AR), rows(lax.rem(i, R // AR) * AR, AR)
        place = lax.broadcasted_iota(jnp.int32, (AR, R), 0) + lax.rem(i, R // AR) * AR
        low = lax.broadcasted_iota(jnp.int32, (AR, R), 1) <= place
        first = jnp.where(low, v.S[at, pl.ds(0, R)], v.S[at, pl.ds(WR, R)])
        if W > 1:
            first = jnp.concatenate([first, v.S[at, pl.ds(R, WR - R)]], axis=1)
        return first, at, inner, low

    def spread(ref, at, low, val):
        own = val[:, :R]
        ref[at, pl.ds(0, R)] = jnp.where(low, own, 0.0).astype(bf16)
        ref[at, pl.ds(WR, R)] = jnp.where(low, 0.0, own).astype(bf16)
        if W > 1:
            ref[at, pl.ds(R, WR - R)] = val[:, R:].astype(bf16)

    def soft(i, _):
        s, at, inner, low = merged(i)
        s = s * (HEAD_DIM**-0.5) + v.BIAS[inner, :]
        e = jnp.exp(s - jnp.max(s, axis=-1, keepdims=True))
        prob = e * (1.0 / jnp.sum(e, axis=-1, keepdims=True))
        v.PM[at, :] = prob
        spread(v.PB, at, low, prob)
        return 0

    for h in range(H):
        v.S[pl.ds(h * R, R), :] = contract(v.QH[pl.ds(h * R, R), :], v.KB[...], (1, 1))
    relay(wu, 0)
    lax.fori_loop(0, H * R // AR, soft, 0)
    v.OB[...] = from_heads(v.PB, v.VB).astype(bf16)

    def chunk(i):
        return pl.ds(i * RC, RC)

    def sum_begin(a, product):
        s1, r1, s2, r2 = v.S1.at[a], v.R1.at[a], v.S2.at[a], v.R2.at[a]
        s1[...] = product((1 - core) * HF).astype(bf16)
        first, second = outgoing(s1), outgoing(s2)
        for i in range(NCHK):
            send(s1.at[chunk(i)], r1.at[chunk(i)], base.a + a * NCHK + i, to_core, None, first)
        v.P32[...] = product(core * HF)
        for i in range(NCHK):
            got(r1.at[chunk(i)], base.a + a * NCHK + i)
            s2[chunk(i), :] = (v.P32[chunk(i), :] + r1[chunk(i), :].astype(f32)).astype(bf16)
            send(s2.at[chunk(i)], r2.at[chunk(i)], base.b + a * NCHK + i, to_y, None, second)

    def sum_end(a, i):
        s2, r2 = v.S2.at[a], v.R2.at[a]
        got(r2.at[chunk(i)], base.b + a * NCHK + i)
        return s2[chunk(i), :].astype(f32) + r2[chunk(i), :].astype(f32)

    def my_rows(i):
        return rows(core * HF + i * RC, RC)

    def their_rows(i):
        return rows((1 - core) * HF + i * RC, RC)

    def share(ref, flow, i):
        if i == 0:
            relays[flow] = outgoing(ref.at[own_half])
        send(ref.at[my_rows(i)], ref.at[my_rows(i)], flow + i, to_core, None, relays[flow])

    def shared(ref, flow):
        for i in range(NCHK):
            got(ref.at[their_rows(i)], flow + i)

    relayed(wo)
    sum_begin(
        0,
        lambda off: jnp.dot(v.OB[rows(off, HF), :], v.WO[...], preferred_element_type=f32),
    )
    relay(wu, 1)
    for i in range(NCHK):
        h_now = v.XB[my_rows(i), :].astype(f32) + sum_end(0, i)
        v.H[chunk(i), :] = h_now
        r = lax.rsqrt(jnp.mean(h_now * h_now, axis=-1, keepdims=True) + EPS)
        v.N2[my_rows(i), :] = (h_now * r * v.gain_two[...]).astype(bf16)
        share(v.N2, base.n2, i)
    relay(wd, 0)
    relay(wd, 1)
    shared(v.N2, base.n2)

    relayed(wg)
    v.GB[...] = contract(v.N2[...], v.WG[...], (1, 1)).astype(bf16)
    relayed(wu)
    v.UB[...] = contract(v.N2[...], v.WU[...], (1, 1)).astype(bf16)

    def activate(i, _):
        at = rows(i * RC, RC)
        g, u = v.GB[at, :].astype(f32), v.UB[at, :].astype(f32)
        v.AB[at, :] = (g / (1.0 + jnp.exp(-g)) * u).astype(bf16)
        return 0

    lax.fori_loop(0, R // RC, activate, 0)
    relayed(wd)
    sum_begin(
        1,
        lambda off: jnp.dot(v.AB[rows(off, HF), :], v.WD[...], preferred_element_type=f32),
    )
    te_copy.wait()
    up_copy.wait()
    squares, counted = jnp.zeros((1, 1), f32), jnp.zeros((1, 1), f32)
    for i in range(NCHK):
        y_now = v.H[chunk(i), :] + sum_end(1, i)
        v.YB[my_rows(i), :] = y_now.astype(bf16)
        weighting = v.VC[my_rows(i), pl.ds(0, 1)]
        differ = y_now - v.TE[chunk(i), :].astype(f32)
        squares = squares + total_of(weighting * differ * differ)
        counted = counted + total_of(weighting)
        dy = v.UP[chunk(i), :].astype(f32) + weighting * differ
        v.DY[chunk(i), :] = dy
        v.DYB[my_rows(i), :] = dy.astype(bf16)
        share(v.DYB, base.dy, i)
    tile_row = lax.broadcasted_iota(jnp.int32, (8, 128), 0)
    v.LT[0] = jnp.where(
        tile_row == 0, jnp.broadcast_to(squares, (8, 128)), jnp.broadcast_to(counted, (8, 128))
    )
    send(v.LT.at[0], v.LT.at[1], base.lc, to_core)
    y_half = v.YB.at[own_half]
    send(y_half, y_half, base.yb, to_core)
    grads_out = [outgoing(v.XS.at[owner(d)]) for d in range(1, F)]
    group_in, group_out = outgoing(v.XS.at[fs]), outgoing(v.GRAD, jnp.logical_not(is_outer))
    shared(v.DYB, base.dy)

    sent, own_done = [0], [0]

    def weight_grad(left, right, at, d, flipped=False):
        who = owner(d)
        tokens = left.shape[1 if flipped else 0]
        n = left.shape[0 if flipped else 1]
        if d == 0:
            own_done[0] = at + n
        rhs = right[pl.ds(0, tokens), pl.ds(hint(who * DF, 128), DF)]
        v.XS[who, pl.ds(at, n), :] = contract(left[...], rhs, (1 if flipped else 0, 0)).astype(bf16)

    def grad_index(d, j):
        return base.gx + (d - 1) * (NCH + 1) + j

    def grad_send(d, at, j):
        rcopy(
            v.XS.at[owner(d), at], v.XR.at[d - 1, at], grads_out[d - 1], grad_index(d, j),
            {"fsdp": owner(d)},
        ).start()

    def grads_ready(upto):
        first, last = sent[0], upto // CH
        sent[0] = last

        def body(j, _):
            for d in range(1, F):
                grad_send(d, rows(j * CH, CH), j)
            return 0

        if last > first:
            lax.fori_loop(first, last, body, 0)

    def inward(at, j):
        for d in range(1, F):
            got(v.XR.at[d - 1, at], grad_index(d, j))
        acc = v.XS[fs, at, :].astype(f32)
        for d in range(1, F):
            acc = acc + v.XR[d - 1, at, :].astype(f32)
        v.XS[fs, at, :] = acc.astype(bf16)

        @pl.when(jnp.logical_not(is_outer))
        def _():
            got(v.ZO.at[at], base.zo + j)
            v.XS[fs, at, :] = (acc + v.ZO[at, :].astype(f32)).astype(bf16)

        @pl.when(is_mid)
        def _():
            rcopy(v.XS.at[fs, at], v.ZI.at[at], group_in, base.zi + j, to_inner).start()

        @pl.when(jnp.logical_not(is_mid))
        def _():
            rcopy(v.XS.at[fs, at], v.ZO.at[at], group_in, base.zo + j, to_inner).start()

    def outward(at, j):
        got(v.ZI.at[at], base.zi + j)

        @pl.when(is_mid)
        def _():
            whole = v.XS[fs, at, :].astype(f32) + v.ZI[at, :].astype(f32)
            v.GRAD[at, :] = whole.astype(bf16)

        @pl.when(jnp.logical_not(is_mid))
        def _():
            v.GRAD[at, :] = v.ZI[at, :]

        @pl.when(jnp.logical_not(is_outer))
        def _():
            rcopy(v.GRAD.at[at], v.ZI.at[at], group_out, base.zi + j, to_outer).start()

        pltpu.make_async_copy(v.GRAD.at[at], v.grad_out.at[at], ls.at[10]).start()

    lag_in, lag_out = SKEW * hop, SKEW * (2 * half - 1 - hop)
    LAST = NCH + SKEW * (2 * half - 1)

    def pump(first, last):
        def body(i, _):
            ja, jb = i - lag_in, i - lag_out
            pl.when((ja >= 0) & (ja < NCH))(lambda: inward(rows(ja * CH, CH), ja))
            pl.when((jb >= 0) & (jb < NCH))(lambda: outward(rows(jb * CH, CH), jb))
            return 0

        if last > first:
            lax.fori_loop(first, last, body, 0)

    pumped = [0]

    def pump_to(last):
        ready = min(sent[0], own_done[0] // CH)
        last = min(last if NCH > 40 else last * NCH // 49, ready if ready < NCH else LAST)
        if last > pumped[0]:
            pump(pumped[0], last)
            pumped[0] = last

    peers = range(1, F)
    for d in peers:
        weight_grad(v.AB, v.DYB, 0, d)
    grads_ready(FF)
    v.S[pl.ds(0, R), pl.ds(0, FF)] = contract(v.DYB[...], v.WD[...], (1, 1))

    def activate_back(i, _):
        at = rows(i * RC, RC)
        g, u, da = v.GB[at, :].astype(f32), v.UB[at, :].astype(f32), v.S[at, pl.ds(0, FF)]
        sig = 1.0 / (1.0 + jnp.exp(-g))
        v.DGB[at, :] = (da * u * (sig * (1.0 + g * (1.0 - sig)))).astype(bf16)
        v.DUB[at, :] = (da * (g * sig)).astype(bf16)
        return 0

    lax.fori_loop(0, R // RC, activate_back, 0)
    sum_begin(
        2,
        lambda off: jnp.dot(v.DGB[rows(off, HF), :], v.WG[...], preferred_element_type=f32)
        + jnp.dot(v.DUB[rows(off, HF), :], v.WU[...], preferred_element_type=f32),
    )
    weight_grad(v.AB, v.DYB, 0, 0)
    for d in peers:
        weight_grad(v.DGB, v.N2, FF, d)
    grads_ready(2 * FF)
    for d in peers:
        weight_grad(v.DUB, v.N2, 2 * FF, d)
    grads_ready(3 * FF)
    weight_grad(v.DGB, v.N2, FF, 0)
    weight_grad(v.DUB, v.N2, 2 * FF, 0)
    pump_to(2)
    v.GT[0] = jnp.zeros((8, D), f32)
    for i in range(NCHK):
        dn2 = sum_end(2, i)
        h_now = v.H[chunk(i), :]
        r = lax.rsqrt(jnp.mean(h_now * h_now, axis=-1, keepdims=True) + EPS)
        gd = v.gain_two[...] * dn2
        dh = v.DY[chunk(i), :] + r * gd - h_now * (
            r * r * r * jnp.mean(gd * h_now, axis=-1, keepdims=True)
        )
        v.DH[chunk(i), :] = dh
        v.DHB[my_rows(i), :] = dh.astype(bf16)
        share(v.DHB, base.dh, i)
        part = jnp.sum(dn2 * h_now * r, axis=0, keepdims=True)
        part = jnp.where(yy == i // (NCHK // 2), part, 0.0)
        v.GT[0, pl.ds(0, 1), :] = v.GT[0, pl.ds(0, 1), :] + part
        pump_to(3 + i)
    shared(v.DHB, base.dh)

    by_heads(v.DOH, contract(v.DHB[...], v.WO[...], (1, 1)))
    pump_to(7)
    for h in range(H):
        v.S[pl.ds(h * R, R), :] = contract(v.DOH[pl.ds(h * R, R), :], v.VB[...], (1, 1))
    for d in peers:
        weight_grad(v.OB, v.DHB, 3 * FF, d)
    grads_ready(3 * FF + HC)
    weight_grad(v.OB, v.DHB, 3 * FF, 0)
    pump_to(8)

    def soft_back(i, _):
        dp, at, _, low = merged(i)
        prob = v.PM[at, :]
        spread(v.DSB, at, low, prob * (dp - jnp.sum(prob * dp, axis=-1, keepdims=True)))
        return 0

    lax.fori_loop(0, H * R // AR, soft_back, 0)
    pump_to(9)
    scale = HEAD_DIM**-0.5
    v.DVT[...] = contract(v.DOH[...], v.PB[...], (0, 0)).astype(bf16)
    v.DKT[...] = (contract(v.QH[...], v.DSB[...], (0, 0)) * scale).astype(bf16)
    v.DQ[...] = (from_heads(v.DSB, v.KB) * scale).astype(bf16)
    pump_to(11)

    def dn1_product(j, which):
        at = pl.ds(hint(j * R + which * HF, 128), HF)
        out = contract(v.DKT[:, at], v.WQKV[:, pl.ds(HC, HC)], (0, 1))
        out = out + contract(v.DVT[:, at], v.WQKV[:, pl.ds(2 * HC, HC)], (0, 1))
        if j == 0:
            out = out + contract(v.DQ[rows(which * HF, HF), :], v.WQKV[:, pl.ds(0, HC)], (1, 1))
        return out

    for j in range(W, -1, -1):
        v.D1S[j] = dn1_product(j, 1 - core).astype(bf16)
        send(v.D1S.at[j], v.D1R.at[j], base.d1 + j, to_core)
        v.D1O[j] = dn1_product(j, core)
    for d in list(peers) + [0]:
        at = 3 * FF + HC
        weight_grad(v.DQ, v.N1, at, d)
        weight_grad(v.DKT, v.N1, at + HC, d, True)
        weight_grad(v.DVT, v.N1, at + 2 * HC, d, True)
        if d == F - 1:
            grads_ready(N)
    pump_to(13)
    for j in range(W, -1, -1):
        got(v.D1R.at[j], base.d1 + j)
        there = rows((1 - yy) * Q, Q)
        v.D2S[j] = (v.D1O[j, there, :] + v.D1R[j, there, :].astype(f32)).astype(bf16)
        send(v.D2S.at[j], v.D2R.at[j], base.d2 + j, to_y)
    pump_to(16)
    here = rows(yy * Q, Q)
    for j in range(W, 0, -1):
        got(v.D2R.at[j], base.d2 + j)
        own = v.D1O[j, here, :] + v.D1R[j, here, :].astype(f32) + v.D2R[j].astype(f32)
        v.DZS[j] = own.astype(bf16)
        if j < W:
            @pl.when(has_next & (z >= j))
            def _(j=j, own=own):
                got(v.DZR.at[j + 1], base.dz + j + 1)
                v.DZS[j] = (own + v.DZR[j + 1].astype(f32)).astype(bf16)
        send(v.DZS.at[j], v.DZR.at[j], base.dz + j, to_prev, z >= j)
        pump_to(19 + 2 * (W - j))

    got(v.LT.at[1], base.lc)
    v.LB[z] = v.LT[0] + v.LT[1]
    for s in range(C - 1):
        left_tile, right_tile = z - s, z + s
        send(v.LB.at[jnp.maximum(left_tile, 0)], v.LB.at[jnp.maximum(left_tile, 0)],
             base.lr + s, to_next, has_next & (left_tile >= 0))
        send(v.LB.at[jnp.minimum(right_tile, C - 1)], v.LB.at[jnp.minimum(right_tile, C - 1)],
             base.ll + s, to_prev, has_prev & (right_tile <= C - 1))
        if s == 0:
            pump_to(23)
        pl.when(left_tile - 1 >= 0)(
            lambda i=left_tile - 1, s=s: got(v.LB.at[jnp.maximum(i, 0)], base.lr + s)
        )
        pl.when(right_tile + 1 <= C - 1)(
            lambda i=right_tile + 1, s=s: got(v.LB.at[jnp.minimum(i, C - 1)], base.ll + s)
        )
    v.LX[fs] = v.LB[...]
    for d in peers:
        send(v.LB, v.LX.at[fs], base.lx + d - 1, {"fsdp": owner(d)})

    pump_to(26)
    got(v.D2R.at[0], base.d2)
    v.P32[pl.ds(0, Q), :] = (
        v.D1O[0, here, :] + v.D1R[0, here, :].astype(f32) + v.D2R[0].astype(f32)
    )

    @pl.when(has_next)
    def _():
        got(v.DZR.at[1], base.dz + 1)
        v.P32[pl.ds(0, Q), :] = v.P32[pl.ds(0, Q), :] + v.DZR[1].astype(f32)

    quarter = rows(core * HF + yy * Q, Q)
    dn1 = v.P32[pl.ds(0, Q), :]
    x_now = v.XB[quarter, :].astype(f32)
    r = lax.rsqrt(jnp.mean(x_now * x_now, axis=-1, keepdims=True) + EPS)
    gd = v.gain_one[...] * dn1
    gi = v.DH[here, :] + r * gd - x_now * (
        r * r * r * jnp.mean(gd * x_now, axis=-1, keepdims=True)
    )
    v.GIB[quarter, :] = gi.astype(bf16)
    mine = v.GIB.at[quarter]
    send(mine, mine, base.i1, to_y)
    send(mine, mine, base.i2, to_core)
    v.GT[0, pl.ds(1, 1), :] = jnp.sum(dn1 * x_now * r, axis=0, keepdims=True)
    send(v.GT.at[0], v.GR.at[0], base.g1, to_core)
    pump_to(28)
    got(v.GR.at[0], base.g1)
    v.GT[1] = v.GT[0] + v.GR[0]
    send(v.GT.at[1], v.GR.at[1], base.g2, to_y)
    from_y = v.GIB.at[rows(core * HF + (1 - yy) * Q, Q)]
    got(from_y, base.i1)
    send(from_y, from_y, base.i3, to_core)
    pump_to(32)
    got(v.GR.at[1], base.g2)
    v.GT[2] = v.GT[1] + v.GR[1]
    for d in list(peers) + [0]:
        tile = v.GT[2, :, pl.ds(hint(owner(d) * DF, 128), DF)]
        v.XS[owner(d), pl.ds(N, 16), :] = jnp.concatenate([tile, jnp.zeros_like(tile)], 0).astype(bf16)
        if d:
            grad_send(d, pl.ds(N, 16), NCH)

    for d in peers:
        got(v.LX.at[owner(F - d)], base.lx + d - 1)
    sums = [sum(v.LX[s, c] for c in range(C)) for s in range(F)]
    counted = sum(s[1:2, :] for s in sums)
    for s in range(F):
        v.LOSS[pl.ds(s, 1), :] = sums[s][0:1, :] * F / (counted * D)

    pump_to(LAST - SKEW * (2 * half - 1))
    gain_rows = pl.ds(N, 16)
    inward(gain_rows, NCH)
    pump_to(LAST)
    outward(gain_rows, NCH)
    got(v.YB.at[rows((1 - core) * HF, HF)], base.yb)
    got(v.GIB.at[rows((1 - core) * HF + yy * Q, Q)], base.i2)
    got(v.GIB.at[rows((1 - core) * HF + (1 - yy) * Q, Q)], base.i3)
    results = (
        pltpu.make_async_copy(v.YB, v.y_out, ls.at[0]),
        pltpu.make_async_copy(v.GIB, v.gi_out, ls.at[1]),
        pltpu.make_async_copy(v.LOSS, v.loss_out, ls.at[2]),
    )
    for cp in results:
        cp.start()

    for k, (src, cond) in enumerate(unsent):
        def left(src=src, k=k):
            rcopy(src, src, k, 0, to_core).wait_send()
        if cond is None:
            left()
        else:
            pl.when(cond)(left)
    for cp in results:
        cp.wait()
    pltpu.make_async_copy(v.GRAD, v.grad_out, ls.at[10]).wait()


def finish_kernel(p, grad, gib, yb, loss, *refs):
    (y_out, loss_out, gi_out, one, gq, gk, gv, go, two, gg, gu, gd) = refs[:12]
    g_buf, i_buf, y_buf, l_buf, g_wide, i_wide, q_wide, sem_in, sem_out = refs[12:]
    FF, HC, N = p.FF, p.HC, p.N
    at = 3 * FF
    plain, flip = [], []
    for ref, first in ((gd, 0), (gg, FF), (gu, 2 * FF)):
        plain += [(ref, first, 0, FF // 2), (ref, first + FF // 2, FF // 2, FF // 2)]
    plain.append((go, at, 0, HC))
    flip = [(gq, at + HC), (gk, at + 2 * HC), (gv, at + 3 * HC)]
    loads = []

    def load(src, dst):
        cp = pltpu.make_async_copy(src, dst, sem_in.at[len(loads)])
        cp.start()
        loads.append(cp)
        return cp

    stores = []

    def store(src, dst):
        cp = pltpu.make_async_copy(src, dst, sem_out.at[len(stores)])
        cp.start()
        stores.append(cp)

    plain_in = [load(grad.at[pl.ds(f, n)], g_buf.at[pl.ds(f, n)]) for _, f, _, n in plain]
    flip_in = [load(grad.at[pl.ds(f, HC)], g_buf.at[pl.ds(f, HC)]) for _, f in flip]
    gi_in = load(gib, i_buf)
    y_in = load(yb, y_buf)
    gain_in = load(grad.at[pl.ds(N, 16)], g_buf.at[pl.ds(N, 16)])
    loss_in = load(loss, l_buf)
    for (ref, first, row, n), cp in zip(plain, plain_in):
        cp.wait()
        g_wide[pl.ds(first, n), :] = g_buf[pl.ds(first, n), :].astype(f32)
        store(g_wide.at[pl.ds(first, n)], ref.at[pl.ds(row, n)])
    for k, ((ref, first), cp) in enumerate(zip(flip, flip_in)):
        cp.wait()
        for c in range(0, HC, 128):
            w = min(128, HC - c)
            q_wide[k, :, pl.ds(c, w)] = g_buf[pl.ds(first + c, w), :].astype(f32).T
        store(q_wide.at[k], ref)
    gi_in.wait()
    i_wide[...] = i_buf[...].astype(f32)
    store(i_wide, gi_out.at[0])
    y_in.wait()
    store(y_buf, y_out.at[0])
    gain_in.wait()
    gains = g_buf[pl.ds(N, 16), :].astype(f32)
    two[...] = gains[0:1, :]
    one[...] = gains[1:2, :]
    loss_in.wait()
    for s in range(p.F):
        loss_out[s] = jnp.max(l_buf[pl.ds(s, 1), :])
    for cp in stores:
        cp.wait()


def shards(mesh_shape, seq_len, *args):
    (inputs, upstream, teacher, valid, segment, gain_one, wq, wk, wv, wo, gain_two, wg, wu, wd) = args
    _, rows_here, width = inputs.shape
    p = Plan(
        mesh_shape["fsdp"], mesh_shape["ctx"], rows_here, width, wq.shape[1], wg.shape[1], seq_len
    )
    R, D, DF, HC, FF, F = p.R, p.D, p.DF, p.HC, p.FF, p.F
    NG = p.N + 16
    scratch = scratch_of(p)
    vmem = pl.BlockSpec(memory_space=pltpu.VMEM)
    anywhere = pl.BlockSpec(memory_space=pl.ANY)
    in_specs = [anywhere] * 3 + [vmem] * 3 + [anywhere] * 4 + [vmem] + [anywhere] * 3
    sds = jax.ShapeDtypeStruct
    grad, gib, yb, loss = pl.pallas_call(
        functools.partial(layer_kernel, p, tuple(scratch)),
        out_shape=(
            sds((NG, DF), bf16), sds((R, D), bf16), sds((R, D), bf16), sds((max(F, 8), 128), f32),
        ),
        in_specs=in_specs,
        out_specs=(anywhere,) * 4,
        scratch_shapes=[pltpu.VMEM(s, dt) for s, dt in scratch.values()]
        + [
            pltpu.SemaphoreType.DMA((p.sends,)), pltpu.SemaphoreType.DMA((p.total,)),
            pltpu.SemaphoreType.DMA((11,)),
        ],
        compiler_params=pltpu.CompilerParams(
            collective_id=0, has_side_effects=True, vmem_limit_bytes=67043328
        ),
        name="layer",
    )(
        inputs.reshape(R, D), upstream.reshape(R, D), teacher.reshape(R, D), valid, segment,
        gain_one.reshape(1, D), wq, wk, wv, wo, gain_two.reshape(1, D), wg.T, wu.T, wd,
    )
    outs = pl.pallas_call(
        functools.partial(finish_kernel, p),
        out_shape=(
            sds((1, R, D), bf16), sds((F,), f32), sds((1, R, D), f32), sds((1, DF), f32),
            sds((DF, HC), f32), sds((DF, HC), f32), sds((DF, HC), f32), sds((HC, DF), f32),
            sds((1, DF), f32), sds((FF, DF), f32), sds((FF, DF), f32), sds((FF, DF), f32),
        ),
        in_specs=[anywhere] * 4,
        out_specs=(anywhere, pl.BlockSpec(memory_space=pltpu.SMEM), anywhere, vmem)
        + (anywhere,) * 4 + (vmem,) + (anywhere,) * 3,
        scratch_shapes=[
            pltpu.VMEM((NG, DF), bf16), pltpu.VMEM((R, D), bf16), pltpu.VMEM((R, D), bf16),
            pltpu.VMEM((max(F, 8), 128), f32), pltpu.VMEM((3 * FF + HC, DF), f32),
            pltpu.VMEM((R, D), f32), pltpu.VMEM((3, DF, HC), f32),
            pltpu.SemaphoreType.DMA((14,)), pltpu.SemaphoreType.DMA((12,)),
        ],
        compiler_params=pltpu.CompilerParams(vmem_limit_bytes=40 * 2**20),
        name="finish",
    )(grad, gib, yb, loss)
    outs = list(outs)
    outs[3], outs[8] = outs[3].reshape(DF), outs[8].reshape(DF)
    outs[9], outs[10] = outs[9].T, outs[10].T
    return tuple(outs)


def solution(mesh):
    def run(*args):
        token, row, col = P("fsdp", "ctx", None), P("fsdp", "tp"), P("tp", "fsdp")
        pair = P("fsdp", "ctx")
        return jax.shard_map(
            functools.partial(shards, dict(mesh.shape), args[0].shape[1]),
            mesh=mesh,
            in_specs=(token, token, token, pair, pair, P(), row, row, row, col, P(), row, row, col),
            out_specs=(
                token, P(), token, P("fsdp"), row, row, row, col, P("fsdp"), row, row, col,
            ),
            check_vma=False,
        )(*args)

    return run
```

```python
import functools
from types import SimpleNamespace

import jax
import jax.numpy as jnp
from jax import lax
from jax.experimental import pallas as pl
from jax.experimental.pallas import tpu as pltpu
from jax.sharding import PartitionSpec as P

HEAD_DIM = 64
EPS = 1e-05
MESH = pl.DeviceIdType.MESH
NCHK = 4
SKEW = 2
f32, bf16 = jnp.float32, jnp.bfloat16


class Plan:
    def __init__(self, fsdp, ctx, rows, width, head_cols, hidden, seq_len):
        self.F, self.C, self.R, self.D = fsdp, ctx, rows, width
        self.HC, self.FF = head_cols, hidden
        self.DF = width // fsdp
        self.W = -(-(seq_len // 2) // rows)
        self.N = 3 * hidden + 4 * head_cols
        self.CH = next(
            k for k in range(16, self.N + 1, 16) if self.N % k == 0 and k * self.DF >= 57344
        )
        self.NCH = self.N // self.CH
        self.base, self.total = SimpleNamespace(), 0
        peers = fsdp - 1
        for name, count in dict(
            xz=self.W, sg=self.W, xy=self.W, xc=self.W, wd=10 * peers, wr=10 * peers,
            a=3 * NCHK, b=3 * NCHK, n2=NCHK, yb=1, dy=NCHK, dh=NCHK,
            lc=1, ll=ctx - 1, lx=peers, d1=self.W + 1, d2=self.W + 1, dz=self.W + 1,
            g1=1, g2=1, i1=1, i2=1, i3=1, gx=peers * (self.NCH + 1),
            zo=self.NCH + 1, zi=self.NCH + 1,
        ).items():
            setattr(self.base, name, self.total)
            self.total += count
        self.sends = 4 * self.W + 2 + 14 * peers + 9 + 3 + 2 * ctx + peers + 3 * self.W + 2 + 5 + peers + 2


def contract(left, right, dims):
    return lax.dot_general(left, right, ((dims[:1], dims[1:]), ((), ())), preferred_element_type=f32)


def total_of(v):
    return jnp.sum(jnp.sum(v, axis=1, keepdims=True), axis=0, keepdims=True)


def scratch_of(p):
    R, D, HC, FF, DF, F, C, W = p.R, p.D, p.HC, p.FF, p.DF, p.F, p.C, p.W
    HF, Q, KR, H = R // 2, R // 4, (p.W + 1) * p.R, p.HC // HEAD_DIM
    NG = p.N + 16
    return dict(
        XB=((KR, D), bf16), SG=((W + 1, 1, R), jnp.int32), N1=((KR, D), bf16),
        WQKV=((D, 3 * HC), bf16), WO=((HC, D), bf16), WG=((FF, D), bf16),
        WU=((FF, D), bf16), WD=((FF, D), bf16),
        QH=((H * R, HC), bf16), KB=((KR, HC), bf16), VB=((KR, HC), bf16), DOH=((H * R, HC), bf16),
        PM=((H * R, W * R), f32), S=((H * R, KR), f32), PB=((H * R, KR), bf16), DSB=((H * R, KR), bf16),
        BIAS=((R, W * R), f32), DQ=((R, HC), bf16), DKT=((HC, KR), bf16), DVT=((HC, KR), bf16),
        OB=((R, HC), bf16), VC=((R, 128), f32),
        H=((HF, D), f32), DY=((HF, D), f32), DH=((HF, D), f32), P32=((HF, D), f32),
        UP=((HF, D), bf16), TE=((HF, D), bf16),
        N2=((R, D), bf16), DYB=((R, D), bf16), DHB=((R, D), bf16),
        GB=((R, FF), bf16), UB=((R, FF), bf16), AB=((R, FF), bf16),
        DGB=((R, FF), bf16), DUB=((R, FF), bf16),
        D1S=((W + 1, HF, D), bf16), D1R=((W + 1, HF, D), bf16), D1O=((W + 1, HF, D), f32),
        D2S=((W + 1, Q, D), bf16), D2R=((W + 1, Q, D), bf16), DZR=((W + 1, Q, D), bf16),
        DZS=((W + 1, Q, D), bf16),
        GT=((3, 8, D), f32), GR=((2, 8, D), f32),
        LT=((8, 128), f32), LX=((F, 8, 128), f32), LC=((F, 8, 128), f32), LB=((C, F, 8, 128), f32),
        XS=((F, NG, DF), bf16), XR=((F - 1, NG, DF), bf16),
        ZO=((NG, DF), bf16), ZI=((NG, DF), bf16), GRAD=((NG, DF), bf16), GIB=((R, D), bf16),
        YB=((R, D), bf16), LOSS=((max(F, 8), 128), f32),
        S1=((3, HF, D), bf16), R1=((3, HF, D), bf16), S2=((3, HF, D), bf16), R2=((3, HF, D), bf16),
    )


def layer_kernel(p, names, *refs):
    v = SimpleNamespace(**dict(zip(names, refs[18:], strict=False)))
    (
        v.x, v.upstream, v.teacher, v.valid, v.segment, v.gain_one, v.wq, v.wk, v.wv, v.wo,
        v.gain_two, v.wg, v.wu, v.wd, v.grad_out, v.gi_out, v.y_out, v.loss_out,
    ) = refs[:18]
    ss, rs, ls = refs[-3:]
    R, D, HC, FF, DF, F, C, W, N, CH, NCH = (
        p.R, p.D, p.HC, p.FF, p.DF, p.F, p.C, p.W, p.N, p.CH, p.NCH
    )
    HF, Q, KR, H = R // 2, R // 4, (W + 1) * R, HC // HEAD_DIM
    RC = HF // NCHK
    base = p.base
    fs, z, t = lax.axis_index("fsdp"), lax.axis_index("ctx"), lax.axis_index("tp")
    core, yy, par = lax.rem(t, 2), t // 2, lax.rem(z, 2)
    to_core, to_y = {"tp": t + 1 - 2 * core}, {"tp": lax.rem(t + 2, 4)}
    to_next, to_prev = {"ctx": lax.rem(z + 1, C)}, {"ctx": lax.rem(z + C - 1, C)}
    to_pair = {"ctx": z + 1 - 2 * par}
    has_next, has_prev = z < C - 1, z > 0
    half = C // 2
    left_side = z < half
    hop = jnp.where(left_side, z, C - 1 - z)
    step_in = jnp.where(left_side, 1, -1)
    to_inner = {"ctx": z + step_in}
    to_outer = {"ctx": lax.rem(z - step_in + C, C)}
    is_outer, is_mid = hop == 0, hop == half - 1

    def owner(d):
        return lax.rem(fs + d, F)

    def rcopy(src, dst, sk, rk, dev):
        return pltpu.make_async_remote_copy(
            src_ref=src, dst_ref=dst, send_sem=ss.at[sk], recv_sem=rs.at[rk],
            device_id=dev, device_id_type=MESH,
        )

    unsent = []

    def outgoing(src, cond=None):
        unsent.append((src, cond))
        assert len(unsent) <= p.sends
        return len(unsent) - 1

    def send(src, dst, k, dev, cond=None, group=None):
        sk = outgoing(src, cond) if group is None else group
        if cond is None:
            rcopy(src, dst, sk, k, dev).start()
        else:
            pl.when(cond)(lambda: rcopy(src, dst, sk, k, dev).start())

    def got(dst, k):
        rcopy(dst, dst, 0, k, to_core).wait_recv()

    def hint(i, m):
        return pl.multiple_of(i, m)

    def rows(off, n, m=16):
        return pl.ds(hint(off, m), n)

    local = []

    def fetch(src, dst):
        cp = pltpu.make_async_copy(src, dst, ls.at[len(local)])
        cp.start()
        local.append(cp)
        return cp

    own_half = rows(core * HF, HF)
    x_copy = fetch(v.x, v.XB.at[pl.ds(0, R)])
    own_cols = pl.ds(hint(fs * DF, 128), DF)

    def by_row(dst, col0, cols):
        def region(who, off, n):
            return dst.at[rows(who * DF + off, n), pl.ds(col0, cols)]
        return region

    def by_col(dst):
        def region(who, off, n):
            return dst.at[rows(off, n), pl.ds(hint(who * DF, 128), DF)]
        return region

    weights = (
        (v.wq, by_row(v.WQKV, 0, HC), 1), (v.wk, by_row(v.WQKV, HC, HC), 1),
        (v.wv, by_row(v.WQKV, 2 * HC, HC), 1), (v.wo, by_col(v.WO), 1),
        (v.wg, by_col(v.WG), 2), (v.wu, by_col(v.WU), 2), (v.wd, by_col(v.WD), 2),
    )
    gathers = []
    count = 0
    for source, region, parts in weights:
        tall = source.shape[0]
        cut = tall // 2 // parts
        gathers.append((
            source, fetch(source, region(fs, 0, tall)),
            [(region, tall // 2, k * cut, cut, count + k) for k in range(parts)],
        ))
        count += parts
    wq, wk, wv, wo, wg, wu, wd = gathers
    te_copy = fetch(v.teacher.at[own_half], v.TE)
    up_copy = fetch(v.upstream.at[own_half], v.UP)

    barrier = pltpu.get_barrier_semaphore()

    def greet(dev):
        pl.semaphore_signal(barrier, inc=1, device_id=dev, device_id_type=MESH)

    greet(to_core)
    greet(to_y)
    for d in range(1, F):
        greet({"fsdp": owner(d)})
    for k in range(1, C):
        greet({"ctx": lax.rem(z + k, C)})
    pl.semaphore_wait(barrier, F + C)

    def piece_index(kind, number, d):
        return kind + number * (F - 1) + d - 1

    for source, _, pieces in gathers:
        tall = source.shape[0] // 2
        for d in range(1, F):
            group = outgoing(source.at[rows(par * tall, tall)])
            for region, _, at, n, number in pieces:
                off = par * tall + at
                send(
                    source.at[rows(off, n)], region(fs, off, n), piece_index(base.wd, number, d),
                    {"fsdp": owner(d)}, None, group,
                )

    relays = {}

    def relay(weight, which):
        region, tall, at, n, number = weight[2][which]
        for d in range(1, F):
            if which == 0:
                relays[number, d] = outgoing(region(owner(F - d), par * tall, tall))
            part = region(owner(F - d), par * tall + at, n)
            got(part, piece_index(base.wd, number, d))
            send(
                part, part, piece_index(base.wr, number, d), to_pair, None, relays[number - which, d]
            )

    def relayed(weight):
        weight[1].wait()
        for region, tall, at, n, number in weight[2]:
            for d in range(1, F):
                got(region(owner(F - d), (1 - par) * tall + at, n), piece_index(base.wr, number, d))

    def x_half(j, which):
        return v.XB.at[rows(j * R + which * HF, HF)]

    def x_quarter(j, y):
        return v.XB.at[rows(j * R + core * HF + y * Q, Q)]

    send(v.x.at[rows(core * HF + yy * Q, Q)], x_quarter(1, yy), base.xz, to_next, has_next)
    v.SG[0] = v.segment[...]
    send(v.segment, v.SG.at[1], base.sg, to_next, has_next)
    for j in range(1, W + 1):
        @pl.when(z < j)
        def _(j=j):
            v.XB[pl.ds(j * R, R), :] = jnp.zeros((R, D), bf16)
            v.SG[j] = jnp.full((1, R), -1, jnp.int32)

    def x_pass(j):
        @pl.when(z >= j)
        def _():
            got(x_quarter(j, yy), base.xz + j - 1)
            got(v.SG.at[j], base.sg + j - 1)
        if j < W:
            both = (z >= j) & has_next
            send(x_quarter(j, yy), x_quarter(j + 1, yy), base.xz + j, to_next, both)
            send(v.SG.at[j], v.SG.at[j + 1], base.sg + j, to_next, both)
        send(x_quarter(j, yy), x_quarter(j, yy), base.xy + j - 1, to_y, z >= j)

    def x_join(j):
        pl.when(z >= j)(lambda: got(x_quarter(j, 1 - yy), base.xy + j - 1))
        send(x_half(j, core), x_half(j, core), base.xc + j - 1, to_core, z >= j)

    def x_done(j):
        pl.when(z >= j)(lambda: got(x_half(j, 1 - core), base.xc + j - 1))

    def norm_rows(j):
        def body(i, _):
            at = rows(j * R + i * RC, RC)
            xs = v.XB[at, :].astype(f32)
            r = lax.rsqrt(jnp.mean(xs * xs, axis=-1, keepdims=True) + EPS)
            v.N1[at, :] = (xs * r * v.gain_one[...]).astype(bf16)
            return 0
        lax.fori_loop(0, R // RC, body, 0)

    eye = lax.broadcasted_iota(jnp.int32, (R, R), 0) == lax.broadcasted_iota(jnp.int32, (R, R), 1)
    lower = lax.broadcasted_iota(jnp.int32, (R, R), 1) <= lax.broadcasted_iota(jnp.int32, (R, R), 0)

    def column(row):
        return jnp.sum(jnp.where(eye, row.astype(f32), 0.0), axis=1, keepdims=True)

    x_copy.wait()
    norm_rows(0)
    v.VC[...] = jnp.broadcast_to(column(v.valid[...]), (R, 128))
    relay(wq, 0)
    x_pass(1)
    relay(wk, 0)
    relay(wv, 0)
    x_join(1)
    x_done(1)
    norm_rows(1)
    for j in range(2, W + 1):
        x_pass(j)
        if j == 2:
            relay(wo, 0)
            relay(wg, 0)
        x_join(j)
        x_done(j)
        norm_rows(j)
    if W < 2:
        relay(wo, 0)
        relay(wg, 0)
    seg_col = column(v.SG[0])
    for j in range(W):
        seg_row = jnp.broadcast_to(v.SG[j].astype(f32), (R, R))
        if j == 0:
            seg_row = jnp.where(lower, seg_row, v.SG[W].astype(f32))
        v.BIAS[:, pl.ds(j * R, R)] = jnp.where(seg_col == seg_row, 0.0, -1e30)
    relayed(wq)
    lane_head = lax.broadcasted_iota(jnp.int32, (R, HC), 1) // HEAD_DIM

    def by_heads(ref, val):
        for h in range(H):
            ref[pl.ds(h * R, R), :] = jnp.where(lane_head == h, val, 0.0).astype(bf16)

    def from_heads(ref, other):
        mix = jnp.zeros((R, HC), f32)
        for h in range(H):
            part = jnp.dot(ref[pl.ds(h * R, R), :], other[...], preferred_element_type=f32)
            mix = jnp.where(lane_head == h, part, mix)
        return mix

    by_heads(
        v.QH,
        jnp.dot(v.N1[pl.ds(0, R), :], v.WQKV[:, pl.ds(0, HC)], preferred_element_type=f32),
    )
    relayed(wk)
    relayed(wv)
    for dst, col in ((v.KB, HC), (v.VB, 2 * HC)):
        dst[...] = jnp.dot(
            v.N1[...], v.WQKV[:, pl.ds(col, HC)], preferred_element_type=f32
        ).astype(bf16)
    relay(wg, 1)

    AR = 64 if R % 64 == 0 else R // 4
    WR = W * R

    def merged(i):
        at, inner = rows(i * AR, AR), rows(lax.rem(i, R // AR) * AR, AR)
        place = lax.broadcasted_iota(jnp.int32, (AR, R), 0) + lax.rem(i, R // AR) * AR
        low = lax.broadcasted_iota(jnp.int32, (AR, R), 1) <= place
        first = jnp.where(low, v.S[at, pl.ds(0, R)], v.S[at, pl.ds(WR, R)])
        if W > 1:
            first = jnp.concatenate([first, v.S[at, pl.ds(R, WR - R)]], axis=1)
        return first, at, inner, low

    def spread(ref, at, low, val):
        own = val[:, :R]
        ref[at, pl.ds(0, R)] = jnp.where(low, own, 0.0).astype(bf16)
        ref[at, pl.ds(WR, R)] = jnp.where(low, 0.0, own).astype(bf16)
        if W > 1:
            ref[at, pl.ds(R, WR - R)] = val[:, R:].astype(bf16)

    def soft(i, _):
        s, at, inner, low = merged(i)
        s = s * (HEAD_DIM**-0.5) + v.BIAS[inner, :]
        e = jnp.exp(s - jnp.max(s, axis=-1, keepdims=True))
        prob = e * (1.0 / jnp.sum(e, axis=-1, keepdims=True))
        v.PM[at, :] = prob
        spread(v.PB, at, low, prob)
        return 0

    for h in range(H):
        v.S[pl.ds(h * R, R), :] = contract(v.QH[pl.ds(h * R, R), :], v.KB[...], (1, 1))
    relay(wu, 0)
    lax.fori_loop(0, H * R // AR, soft, 0)
    v.OB[...] = from_heads(v.PB, v.VB).astype(bf16)

    def chunk(i):
        return pl.ds(i * RC, RC)

    def sum_begin(a, product):
        s1, r1, s2, r2 = v.S1.at[a], v.R1.at[a], v.S2.at[a], v.R2.at[a]
        s1[...] = product((1 - core) * HF).astype(bf16)
        first, second = outgoing(s1), outgoing(s2)
        for i in range(NCHK):
            send(s1.at[chunk(i)], r1.at[chunk(i)], base.a + a * NCHK + i, to_core, None, first)
        v.P32[...] = product(core * HF)
        for i in range(NCHK):
            got(r1.at[chunk(i)], base.a + a * NCHK + i)
            s2[chunk(i), :] = (v.P32[chunk(i), :] + r1[chunk(i), :].astype(f32)).astype(bf16)
            send(s2.at[chunk(i)], r2.at[chunk(i)], base.b + a * NCHK + i, to_y, None, second)

    def sum_end(a, i):
        s2, r2 = v.S2.at[a], v.R2.at[a]
        got(r2.at[chunk(i)], base.b + a * NCHK + i)
        return s2[chunk(i), :].astype(f32) + r2[chunk(i), :].astype(f32)

    def my_rows(i):
        return rows(core * HF + i * RC, RC)

    def their_rows(i):
        return rows((1 - core) * HF + i * RC, RC)

    def share(ref, flow, i):
        if i == 0:
            relays[flow] = outgoing(ref.at[own_half])
        send(ref.at[my_rows(i)], ref.at[my_rows(i)], flow + i, to_core, None, relays[flow])

    def shared(ref, flow):
        for i in range(NCHK):
            got(ref.at[their_rows(i)], flow + i)

    relayed(wo)
    sum_begin(
        0,
        lambda off: jnp.dot(v.OB[rows(off, HF), :], v.WO[...], preferred_element_type=f32),
    )
    relay(wu, 1)
    for i in range(NCHK):
        h_now = v.XB[my_rows(i), :].astype(f32) + sum_end(0, i)
        v.H[chunk(i), :] = h_now
        r = lax.rsqrt(jnp.mean(h_now * h_now, axis=-1, keepdims=True) + EPS)
        v.N2[my_rows(i), :] = (h_now * r * v.gain_two[...]).astype(bf16)
        share(v.N2, base.n2, i)
    relay(wd, 0)
    relay(wd, 1)
    shared(v.N2, base.n2)

    relayed(wg)
    v.GB[...] = contract(v.N2[...], v.WG[...], (1, 1)).astype(bf16)
    relayed(wu)
    v.UB[...] = contract(v.N2[...], v.WU[...], (1, 1)).astype(bf16)

    def activate(i, _):
        at = rows(i * RC, RC)
        g, u = v.GB[at, :].astype(f32), v.UB[at, :].astype(f32)
        v.AB[at, :] = (g / (1.0 + jnp.exp(-g)) * u).astype(bf16)
        return 0

    lax.fori_loop(0, R // RC, activate, 0)
    relayed(wd)
    sum_begin(
        1,
        lambda off: jnp.dot(v.AB[rows(off, HF), :], v.WD[...], preferred_element_type=f32),
    )
    te_copy.wait()
    up_copy.wait()
    squares, counted = jnp.zeros((1, 1), f32), jnp.zeros((1, 1), f32)
    for i in range(NCHK):
        y_now = v.H[chunk(i), :] + sum_end(1, i)
        v.YB[my_rows(i), :] = y_now.astype(bf16)
        weighting = v.VC[my_rows(i), pl.ds(0, 1)]
        differ = y_now - v.TE[chunk(i), :].astype(f32)
        squares = squares + total_of(weighting * differ * differ)
        counted = counted + total_of(weighting)
        dy = v.UP[chunk(i), :].astype(f32) + weighting * differ
        v.DY[chunk(i), :] = dy
        v.DYB[my_rows(i), :] = dy.astype(bf16)
        share(v.DYB, base.dy, i)
    tile_row = lax.broadcasted_iota(jnp.int32, (8, 128), 0)
    tile = jnp.where(
        tile_row == 0, jnp.broadcast_to(squares, (8, 128)), jnp.broadcast_to(counted, (8, 128))
    )
    v.LT[...] = tile
    v.LX[fs] = tile
    for d in range(1, F):
        send(v.LT, v.LX.at[fs], base.lx + d - 1, {"fsdp": owner(d)})
    y_half = v.YB.at[own_half]
    send(y_half, y_half, base.yb, to_core)
    grads_out = [outgoing(v.XS.at[owner(d)]) for d in range(1, F)]
    group_in, group_out = outgoing(v.XS.at[fs]), outgoing(v.GRAD, jnp.logical_not(is_outer))
    shared(v.DYB, base.dy)

    sent, own_done = [0], [0]

    def weight_grad(left, right, at, d, flipped=False):
        who = owner(d)
        tokens = left.shape[1 if flipped else 0]
        n = left.shape[0 if flipped else 1]
        if d == 0:
            own_done[0] = at + n
        rhs = right[pl.ds(0, tokens), pl.ds(hint(who * DF, 128), DF)]
        v.XS[who, pl.ds(at, n), :] = contract(left[...], rhs, (1 if flipped else 0, 0)).astype(bf16)

    def grad_index(d, j):
        return base.gx + (d - 1) * (NCH + 1) + j

    def grad_send(d, at, j):
        rcopy(
            v.XS.at[owner(d), at], v.XR.at[d - 1, at], grads_out[d - 1], grad_index(d, j),
            {"fsdp": owner(d)},
        ).start()

    def grads_ready(upto):
        first, last = sent[0], upto // CH
        sent[0] = last

        def body(j, _):
            for d in range(1, F):
                grad_send(d, rows(j * CH, CH), j)
            return 0

        if last > first:
            lax.fori_loop(first, last, body, 0)

    def inward(at, j):
        for d in range(1, F):
            got(v.XR.at[d - 1, at], grad_index(d, j))
        acc = v.XS[fs, at, :].astype(f32)
        for d in range(1, F):
            acc = acc + v.XR[d - 1, at, :].astype(f32)
        v.XS[fs, at, :] = acc.astype(bf16)

        @pl.when(jnp.logical_not(is_outer))
        def _():
            got(v.ZO.at[at], base.zo + j)
            v.XS[fs, at, :] = (acc + v.ZO[at, :].astype(f32)).astype(bf16)

        @pl.when(is_mid)
        def _():
            rcopy(v.XS.at[fs, at], v.ZI.at[at], group_in, base.zi + j, to_inner).start()

        @pl.when(jnp.logical_not(is_mid))
        def _():
            rcopy(v.XS.at[fs, at], v.ZO.at[at], group_in, base.zo + j, to_inner).start()

    def outward(at, j):
        got(v.ZI.at[at], base.zi + j)

        @pl.when(is_mid)
        def _():
            whole = v.XS[fs, at, :].astype(f32) + v.ZI[at, :].astype(f32)
            v.GRAD[at, :] = whole.astype(bf16)

        @pl.when(jnp.logical_not(is_mid))
        def _():
            v.GRAD[at, :] = v.ZI[at, :]

        @pl.when(jnp.logical_not(is_outer))
        def _():
            rcopy(v.GRAD.at[at], v.ZI.at[at], group_out, base.zi + j, to_outer).start()

        pltpu.make_async_copy(v.GRAD.at[at], v.grad_out.at[at], ls.at[10]).start()

    lag_in, lag_out = SKEW * hop, SKEW * (2 * half - 1 - hop)
    LAST = NCH + SKEW * (2 * half - 1)

    def pump(first, last):
        def body(i, _):
            ja, jb = i - lag_in, i - lag_out
            pl.when((ja >= 0) & (ja < NCH))(lambda: inward(rows(ja * CH, CH), ja))
            pl.when((jb >= 0) & (jb < NCH))(lambda: outward(rows(jb * CH, CH), jb))
            return 0

        if last > first:
            lax.fori_loop(first, last, body, 0)

    pumped = [0]

    def pump_to(place):
        last = LAST if place > 49 else place * NCH // 49
        ready = min(sent[0], own_done[0] // CH)
        last = min(last, ready if ready < NCH else LAST)
        if last > pumped[0]:
            pump(pumped[0], last)
            pumped[0] = last

    peers = range(1, F)
    for d in peers:
        weight_grad(v.AB, v.DYB, 0, d)
    grads_ready(FF)
    v.S[pl.ds(0, R), pl.ds(0, FF)] = contract(v.DYB[...], v.WD[...], (1, 1))

    def activate_back(i, _):
        at = rows(i * RC, RC)
        g, u, da = v.GB[at, :].astype(f32), v.UB[at, :].astype(f32), v.S[at, pl.ds(0, FF)]
        sig = 1.0 / (1.0 + jnp.exp(-g))
        v.DGB[at, :] = (da * u * (sig * (1.0 + g * (1.0 - sig)))).astype(bf16)
        v.DUB[at, :] = (da * (g * sig)).astype(bf16)
        return 0

    lax.fori_loop(0, R // RC, activate_back, 0)
    sum_begin(
        2,
        lambda off: jnp.dot(v.DGB[rows(off, HF), :], v.WG[...], preferred_element_type=f32)
        + jnp.dot(v.DUB[rows(off, HF), :], v.WU[...], preferred_element_type=f32),
    )
    weight_grad(v.AB, v.DYB, 0, 0)
    for d in peers:
        got(v.LX.at[owner(F - d)], base.lx + d - 1)
    send(v.LX, v.LC, base.lc, to_core)
    for d in peers:
        weight_grad(v.DGB, v.N2, FF, d)
    grads_ready(2 * FF)
    for d in peers:
        weight_grad(v.DUB, v.N2, 2 * FF, d)
    grads_ready(3 * FF)
    weight_grad(v.DGB, v.N2, FF, 0)
    weight_grad(v.DUB, v.N2, 2 * FF, 0)
    pump_to(2)
    v.GT[0] = jnp.zeros((8, D), f32)
    for i in range(NCHK):
        dn2 = sum_end(2, i)
        h_now = v.H[chunk(i), :]
        r = lax.rsqrt(jnp.mean(h_now * h_now, axis=-1, keepdims=True) + EPS)
        gd = v.gain_two[...] * dn2
        dh = v.DY[chunk(i), :] + r * gd - h_now * (
            r * r * r * jnp.mean(gd * h_now, axis=-1, keepdims=True)
        )
        v.DH[chunk(i), :] = dh
        v.DHB[my_rows(i), :] = dh.astype(bf16)
        share(v.DHB, base.dh, i)
        part = jnp.sum(dn2 * h_now * r, axis=0, keepdims=True)
        part = jnp.where(yy == i // (NCHK // 2), part, 0.0)
        v.GT[0, pl.ds(0, 1), :] = v.GT[0, pl.ds(0, 1), :] + part
        pump_to(3 + i)
    shared(v.DHB, base.dh)
    got(v.LC, base.lc)
    v.LB[z] = v.LX[...] + v.LC[...]
    for k in range(1, C):
        send(v.LB.at[z], v.LB.at[z], base.ll + k - 1, {"ctx": lax.rem(z + k, C)})

    by_heads(v.DOH, contract(v.DHB[...], v.WO[...], (1, 1)))
    pump_to(7)
    for h in range(H):
        v.S[pl.ds(h * R, R), :] = contract(v.DOH[pl.ds(h * R, R), :], v.VB[...], (1, 1))
    for d in peers:
        weight_grad(v.OB, v.DHB, 3 * FF, d)
    grads_ready(3 * FF + HC)
    weight_grad(v.OB, v.DHB, 3 * FF, 0)
    pump_to(8)

    def soft_back(i, _):
        dp, at, _, low = merged(i)
        prob = v.PM[at, :]
        spread(v.DSB, at, low, prob * (dp - jnp.sum(prob * dp, axis=-1, keepdims=True)))
        return 0

    lax.fori_loop(0, H * R // AR, soft_back, 0)
    pump_to(9)
    scale = HEAD_DIM**-0.5
    v.DVT[...] = contract(v.DOH[...], v.PB[...], (0, 0)).astype(bf16)
    v.DKT[...] = (contract(v.QH[...], v.DSB[...], (0, 0)) * scale).astype(bf16)
    v.DQ[...] = (from_heads(v.DSB, v.KB) * scale).astype(bf16)
    pump_to(11)

    def dn1_product(j, which):
        at = pl.ds(hint(j * R + which * HF, 128), HF)
        out = contract(v.DKT[:, at], v.WQKV[:, pl.ds(HC, HC)], (0, 1))
        out = out + contract(v.DVT[:, at], v.WQKV[:, pl.ds(2 * HC, HC)], (0, 1))
        if j == 0:
            out = out + contract(v.DQ[rows(which * HF, HF), :], v.WQKV[:, pl.ds(0, HC)], (1, 1))
        return out

    for j in range(W, -1, -1):
        v.D1S[j] = dn1_product(j, 1 - core).astype(bf16)
        send(v.D1S.at[j], v.D1R.at[j], base.d1 + j, to_core)
        v.D1O[j] = dn1_product(j, core)
    for d in list(peers) + [0]:
        at = 3 * FF + HC
        weight_grad(v.DQ, v.N1, at, d)
        weight_grad(v.DKT, v.N1, at + HC, d, True)
        weight_grad(v.DVT, v.N1, at + 2 * HC, d, True)
        if d == F - 1:
            grads_ready(N)
    pump_to(13)
    for j in range(W, -1, -1):
        got(v.D1R.at[j], base.d1 + j)
        there = rows((1 - yy) * Q, Q)
        v.D2S[j] = (v.D1O[j, there, :] + v.D1R[j, there, :].astype(f32)).astype(bf16)
        send(v.D2S.at[j], v.D2R.at[j], base.d2 + j, to_y)
    pump_to(16)
    here = rows(yy * Q, Q)
    for j in range(W, 0, -1):
        got(v.D2R.at[j], base.d2 + j)
        own = v.D1O[j, here, :] + v.D1R[j, here, :].astype(f32) + v.D2R[j].astype(f32)
        v.DZS[j] = own.astype(bf16)
        if j < W:
            @pl.when(has_next & (z >= j))
            def _(j=j, own=own):
                got(v.DZR.at[j + 1], base.dz + j + 1)
                v.DZS[j] = (own + v.DZR[j + 1].astype(f32)).astype(bf16)
        send(v.DZS.at[j], v.DZR.at[j], base.dz + j, to_prev, z >= j)
        pump_to(19 + 2 * (W - j))

    pump_to(23)
    pump_to(26)
    got(v.D2R.at[0], base.d2)
    v.P32[pl.ds(0, Q), :] = (
        v.D1O[0, here, :] + v.D1R[0, here, :].astype(f32) + v.D2R[0].astype(f32)
    )

    @pl.when(has_next)
    def _():
        got(v.DZR.at[1], base.dz + 1)
        v.P32[pl.ds(0, Q), :] = v.P32[pl.ds(0, Q), :] + v.DZR[1].astype(f32)

    quarter = rows(core * HF + yy * Q, Q)
    dn1 = v.P32[pl.ds(0, Q), :]
    x_now = v.XB[quarter, :].astype(f32)
    r = lax.rsqrt(jnp.mean(x_now * x_now, axis=-1, keepdims=True) + EPS)
    gd = v.gain_one[...] * dn1
    gi = v.DH[here, :] + r * gd - x_now * (
        r * r * r * jnp.mean(gd * x_now, axis=-1, keepdims=True)
    )
    v.GIB[quarter, :] = gi.astype(bf16)
    mine = v.GIB.at[quarter]
    send(mine, mine, base.i1, to_y)
    send(mine, mine, base.i2, to_core)
    v.GT[0, pl.ds(1, 1), :] = jnp.sum(dn1 * x_now * r, axis=0, keepdims=True)
    send(v.GT.at[0], v.GR.at[0], base.g1, to_core)
    pump_to(28)
    got(v.GR.at[0], base.g1)
    v.GT[1] = v.GT[0] + v.GR[0]
    send(v.GT.at[1], v.GR.at[1], base.g2, to_y)
    from_y = v.GIB.at[rows(core * HF + (1 - yy) * Q, Q)]
    got(from_y, base.i1)
    send(from_y, from_y, base.i3, to_core)
    pump_to(32)
    got(v.GR.at[1], base.g2)
    v.GT[2] = v.GT[1] + v.GR[1]
    for d in list(peers) + [0]:
        tile = v.GT[2, :, pl.ds(hint(owner(d) * DF, 128), DF)]
        v.XS[owner(d), pl.ds(N, 16), :] = jnp.concatenate([tile, jnp.zeros_like(tile)], 0).astype(bf16)
        if d:
            grad_send(d, pl.ds(N, 16), NCH)

    pump_to(49)
    gain_rows = pl.ds(N, 16)
    inward(gain_rows, NCH)
    pump_to(50)
    outward(gain_rows, NCH)
    for k in range(1, C):
        got(v.LB.at[lax.rem(z + C - k, C)], base.ll + k - 1)
    sums = [sum(v.LB[c, s] for c in range(C)) for s in range(F)]
    counted = sum(s[1:2, :] for s in sums)
    for s in range(F):
        v.LOSS[pl.ds(s, 1), :] = sums[s][0:1, :] * F / (counted * D)
    got(v.YB.at[rows((1 - core) * HF, HF)], base.yb)
    got(v.GIB.at[rows((1 - core) * HF + yy * Q, Q)], base.i2)
    got(v.GIB.at[rows((1 - core) * HF + (1 - yy) * Q, Q)], base.i3)
    results = (
        pltpu.make_async_copy(v.YB, v.y_out, ls.at[0]),
        pltpu.make_async_copy(v.GIB, v.gi_out, ls.at[1]),
        pltpu.make_async_copy(v.LOSS, v.loss_out, ls.at[2]),
    )
    for cp in results:
        cp.start()

    for k, (src, cond) in enumerate(unsent):
        def left(src=src, k=k):
            rcopy(src, src, k, 0, to_core).wait_send()
        if cond is None:
            left()
        else:
            pl.when(cond)(left)
    for cp in results:
        cp.wait()
    pltpu.make_async_copy(v.GRAD, v.grad_out, ls.at[10]).wait()


def finish_kernel(p, grad, gib, yb, loss, *refs):
    (y_out, loss_out, gi_out, one, gq, gk, gv, go, two, gg, gu, gd) = refs[:12]
    g_buf, i_buf, y_buf, l_buf, g_wide, i_wide, q_wide, sem_in, sem_out = refs[12:]
    FF, HC, N = p.FF, p.HC, p.N
    at = 3 * FF
    plain, flip = [], []
    for ref, first in ((gd, 0), (gg, FF), (gu, 2 * FF)):
        plain += [(ref, first, 0, FF // 2), (ref, first + FF // 2, FF // 2, FF // 2)]
    plain.append((go, at, 0, HC))
    flip = [(gq, at + HC), (gk, at + 2 * HC), (gv, at + 3 * HC)]
    loads = []

    def load(src, dst):
        cp = pltpu.make_async_copy(src, dst, sem_in.at[len(loads)])
        cp.start()
        loads.append(cp)
        return cp

    stores = []

    def store(src, dst):
        cp = pltpu.make_async_copy(src, dst, sem_out.at[len(stores)])
        cp.start()
        stores.append(cp)

    plain_in = [load(grad.at[pl.ds(f, n)], g_buf.at[pl.ds(f, n)]) for _, f, _, n in plain]
    flip_in = [load(grad.at[pl.ds(f, HC)], g_buf.at[pl.ds(f, HC)]) for _, f in flip]
    gi_in = load(gib, i_buf)
    y_in = load(yb, y_buf)
    gain_in = load(grad.at[pl.ds(N, 16)], g_buf.at[pl.ds(N, 16)])
    loss_in = load(loss, l_buf)
    for (ref, first, row, n), cp in zip(plain, plain_in):
        cp.wait()
        g_wide[pl.ds(first, n), :] = g_buf[pl.ds(first, n), :].astype(f32)
        store(g_wide.at[pl.ds(first, n)], ref.at[pl.ds(row, n)])
    for k, ((ref, first), cp) in enumerate(zip(flip, flip_in)):
        cp.wait()
        for c in range(0, HC, 128):
            w = min(128, HC - c)
            q_wide[k, :, pl.ds(c, w)] = g_buf[pl.ds(first + c, w), :].astype(f32).T
        store(q_wide.at[k], ref)
    gi_in.wait()
    i_wide[...] = i_buf[...].astype(f32)
    store(i_wide, gi_out.at[0])
    y_in.wait()
    store(y_buf, y_out.at[0])
    gain_in.wait()
    gains = g_buf[pl.ds(N, 16), :].astype(f32)
    two[...] = gains[0:1, :]
    one[...] = gains[1:2, :]
    loss_in.wait()
    for s in range(p.F):
        loss_out[s] = jnp.max(l_buf[pl.ds(s, 1), :])
    for cp in stores:
        cp.wait()


def shards(mesh_shape, seq_len, *args):
    (inputs, upstream, teacher, valid, segment, gain_one, wq, wk, wv, wo, gain_two, wg, wu, wd) = args
    _, rows_here, width = inputs.shape
    p = Plan(
        mesh_shape["fsdp"], mesh_shape["ctx"], rows_here, width, wq.shape[1], wg.shape[1], seq_len
    )
    R, D, DF, HC, FF, F = p.R, p.D, p.DF, p.HC, p.FF, p.F
    NG = p.N + 16
    scratch = scratch_of(p)
    vmem = pl.BlockSpec(memory_space=pltpu.VMEM)
    anywhere = pl.BlockSpec(memory_space=pl.ANY)
    in_specs = [anywhere] * 3 + [vmem] * 3 + [anywhere] * 4 + [vmem] + [anywhere] * 3
    sds = jax.ShapeDtypeStruct
    grad, gib, yb, loss = pl.pallas_call(
        functools.partial(layer_kernel, p, tuple(scratch)),
        out_shape=(
            sds((NG, DF), bf16), sds((R, D), bf16), sds((R, D), bf16), sds((max(F, 8), 128), f32),
        ),
        in_specs=in_specs,
        out_specs=(anywhere,) * 4,
        scratch_shapes=[pltpu.VMEM(s, dt) for s, dt in scratch.values()]
        + [
            pltpu.SemaphoreType.DMA((p.sends,)), pltpu.SemaphoreType.DMA((p.total,)),
            pltpu.SemaphoreType.DMA((11,)),
        ],
        compiler_params=pltpu.CompilerParams(
            collective_id=0, has_side_effects=True, vmem_limit_bytes=67043328
        ),
        name="layer",
    )(
        inputs.reshape(R, D), upstream.reshape(R, D), teacher.reshape(R, D), valid, segment,
        gain_one.reshape(1, D), wq, wk, wv, wo, gain_two.reshape(1, D), wg.T, wu.T, wd,
    )
    outs = pl.pallas_call(
        functools.partial(finish_kernel, p),
        out_shape=(
            sds((1, R, D), bf16), sds((F,), f32), sds((1, R, D), f32), sds((1, DF), f32),
            sds((DF, HC), f32), sds((DF, HC), f32), sds((DF, HC), f32), sds((HC, DF), f32),
            sds((1, DF), f32), sds((FF, DF), f32), sds((FF, DF), f32), sds((FF, DF), f32),
        ),
        in_specs=[anywhere] * 4,
        out_specs=(anywhere, pl.BlockSpec(memory_space=pltpu.SMEM), anywhere, vmem)
        + (anywhere,) * 4 + (vmem,) + (anywhere,) * 3,
        scratch_shapes=[
            pltpu.VMEM((NG, DF), bf16), pltpu.VMEM((R, D), bf16), pltpu.VMEM((R, D), bf16),
            pltpu.VMEM((max(F, 8), 128), f32), pltpu.VMEM((3 * FF + HC, DF), f32),
            pltpu.VMEM((R, D), f32), pltpu.VMEM((3, DF, HC), f32),
            pltpu.SemaphoreType.DMA((14,)), pltpu.SemaphoreType.DMA((12,)),
        ],
        compiler_params=pltpu.CompilerParams(vmem_limit_bytes=40 * 2**20),
        name="finish",
    )(grad, gib, yb, loss)
    outs = list(outs)
    outs[3], outs[8] = outs[3].reshape(DF), outs[8].reshape(DF)
    outs[9], outs[10] = outs[9].T, outs[10].T
    return tuple(outs)


def solution(mesh):
    def run(*args):
        token, row, col = P("fsdp", "ctx", None), P("fsdp", "tp"), P("tp", "fsdp")
        pair = P("fsdp", "ctx")
        return jax.shard_map(
            functools.partial(shards, dict(mesh.shape), args[0].shape[1]),
            mesh=mesh,
            in_specs=(token, token, token, pair, pair, P(), row, row, row, col, P(), row, row, col),
            out_specs=(
                token, P(), token, P("fsdp"), row, row, row, col, P("fsdp"), row, row, col,
            ),
            check_vma=False,
        )(*args)

    return run
```

```python
import functools
from types import SimpleNamespace

import jax
import jax.numpy as jnp
from jax import lax
from jax.experimental import pallas as pl
from jax.experimental.pallas import tpu as pltpu
from jax.sharding import PartitionSpec as P

HEAD_DIM = 64
EPS = 1e-05
MESH = pl.DeviceIdType.MESH
NCHK = 4
YROWS = 2
SKEW = 2
f32, bf16 = jnp.float32, jnp.bfloat16


class Plan:
    def __init__(self, fsdp, ctx, rows, width, head_cols, hidden, seq_len):
        self.F, self.C, self.R, self.D = fsdp, ctx, rows, width
        self.HC, self.FF = head_cols, hidden
        self.DF = width // fsdp
        self.W = -(-(seq_len // 2) // rows)
        self.N = 3 * hidden + 4 * head_cols
        self.CH = next(
            k for k in range(16, self.N + 1, 16) if self.N % k == 0 and k * self.DF >= 57344
        )
        self.NCH = self.N // self.CH
        self.base, self.total = SimpleNamespace(), 0
        peers = fsdp - 1
        for name, count in dict(
            ya=YROWS * fsdp, ys=YROWS * fsdp, xz=self.W, sg=self.W, xy=self.W, xc=self.W, wd=11 * peers, wr=11 * peers,
            a=3 * NCHK, b=3 * NCHK, n2=NCHK, yb=1, dy=YROWS * fsdp, dh=NCHK,
            lc=1, ll=ctx - 1, lx=peers, d1=self.W + 1, d2=self.W + 1, dz=self.W + 1,
            g1=1, g2=1, i1=1, i2=1, i3=1, gx=peers * (self.NCH + 1),
            zo=self.NCH + 1, zi=self.NCH + 1,
        ).items():
            setattr(self.base, name, self.total)
            self.total += count
        self.sends = 4 * self.W + 2 + 14 * peers + 9 + 3 + 2 * ctx + peers + 3 * self.W + 2 + 5 + peers + 2


def contract(left, right, dims):
    return lax.dot_general(left, right, ((dims[:1], dims[1:]), ((), ())), preferred_element_type=f32)


def total_of(v):
    return jnp.sum(jnp.sum(v, axis=1, keepdims=True), axis=0, keepdims=True)


def scratch_of(p):
    R, D, HC, FF, DF, F, C, W = p.R, p.D, p.HC, p.FF, p.DF, p.F, p.C, p.W
    HF, Q, KR, H = R // 2, R // 4, (p.W + 1) * p.R, p.HC // HEAD_DIM
    NG = p.N + 16
    return dict(
        XB=((KR, D), bf16), SG=((W + 1, 1, R), jnp.int32), N1=((KR, D), bf16),
        WQKV=((D, 3 * HC), bf16), WO=((HC, D), bf16), WG=((FF, D), bf16),
        WU=((FF, D), bf16), WD=((FF, D), bf16),
        QH=((H * R, HC), bf16), KB=((KR, HC), bf16), VB=((KR, HC), bf16), DOH=((H * R, HC), bf16),
        PM=((H * R, W * R), f32), S=((H * R, KR), f32), PB=((H * R, KR), bf16), DSB=((H * R, KR), bf16),
        BIAS=((R, W * R), f32), DQ=((R, HC), bf16), DKT=((HC, KR), bf16), DVT=((HC, KR), bf16),
        OB=((R, HC), bf16), VC=((R, 128), f32),
        H=((HF, D), f32), DY=((HF, D), f32), DH=((HF, D), f32), P32=((HF, D), f32),
        UP=((HF, D), bf16), TE=((HF, D), bf16),
        N2=((R, D), bf16), DYB=((R, D), bf16), DHB=((R, D), bf16),
        GB=((R, FF), bf16), UB=((R, FF), bf16), AB=((R, FF), bf16),
        DGB=((R, FF), bf16), DUB=((R, FF), bf16),
        D1S=((W + 1, HF, D), bf16), D1R=((W + 1, HF, D), bf16), D1O=((W + 1, HF, D), f32),
        D2S=((W + 1, Q, D), bf16), D2R=((W + 1, Q, D), bf16), DZR=((W + 1, Q, D), bf16),
        DZS=((W + 1, Q, D), bf16),
        GT=((3, 8, D), f32), GR=((2, 8, D), f32),
        LT=((8, 128), f32), LX=((F, 8, 128), f32), LC=((F, 8, 128), f32), LB=((C, F, 8, 128), f32),
        XS=((F, NG, DF), bf16), XR=((F - 1, NG, DF), bf16),
        ZO=((NG, DF), bf16), ZI=((NG, DF), bf16), GRAD=((NG, DF), bf16), GIB=((R, D), bf16),
        YB=((R, D), bf16), LOSS=((max(F, 8), 128), f32),
        S1=((3, HF, D), bf16), R1=((3, HF, D), bf16), S2=((3, HF, D), bf16), R2=((3, HF, D), bf16),
    )


def layer_kernel(p, names, *refs):
    v = SimpleNamespace(**dict(zip(names, refs[18:], strict=False)))
    (
        v.x, v.upstream, v.teacher, v.valid, v.segment, v.gain_one, v.wq, v.wk, v.wv, v.wo,
        v.gain_two, v.wg, v.wu, v.wd, v.grad_out, v.gi_out, v.y_out, v.loss_out,
    ) = refs[:18]
    ss, rs, ls = refs[-3:]
    R, D, HC, FF, DF, F, C, W, N, CH, NCH = (
        p.R, p.D, p.HC, p.FF, p.DF, p.F, p.C, p.W, p.N, p.CH, p.NCH
    )
    HF, Q, KR, H = R // 2, R // 4, (W + 1) * R, HC // HEAD_DIM
    RC = HF // NCHK
    base = p.base
    fs, z, t = lax.axis_index("fsdp"), lax.axis_index("ctx"), lax.axis_index("tp")
    core, yy, par = lax.rem(t, 2), t // 2, lax.rem(z, 2)
    to_core, to_y = {"tp": t + 1 - 2 * core}, {"tp": lax.rem(t + 2, 4)}
    to_next, to_prev = {"ctx": lax.rem(z + 1, C)}, {"ctx": lax.rem(z + C - 1, C)}
    to_pair = {"ctx": z + 1 - 2 * par}
    has_next, has_prev = z < C - 1, z > 0
    half = C // 2
    left_side = z < half
    hop = jnp.where(left_side, z, C - 1 - z)
    step_in = jnp.where(left_side, 1, -1)
    to_inner = {"ctx": z + step_in}
    to_outer = {"ctx": lax.rem(z - step_in + C, C)}
    is_outer, is_mid = hop == 0, hop == half - 1

    def owner(d):
        return lax.rem(fs + d, F)

    def rcopy(src, dst, sk, rk, dev):
        return pltpu.make_async_remote_copy(
            src_ref=src, dst_ref=dst, send_sem=ss.at[sk], recv_sem=rs.at[rk],
            device_id=dev, device_id_type=MESH,
        )

    unsent = []

    def outgoing(src, cond=None):
        unsent.append((src, cond))
        assert len(unsent) <= p.sends
        return len(unsent) - 1

    def send(src, dst, k, dev, cond=None, group=None):
        sk = outgoing(src, cond) if group is None else group
        if cond is None:
            rcopy(src, dst, sk, k, dev).start()
        else:
            pl.when(cond)(lambda: rcopy(src, dst, sk, k, dev).start())

    def got(dst, k):
        rcopy(dst, dst, 0, k, to_core).wait_recv()

    def hint(i, m):
        return pl.multiple_of(i, m)

    def rows(off, n, m=16):
        return pl.ds(hint(off, m), n)

    barrier = pltpu.get_barrier_semaphore()

    def greet(dev):
        pl.semaphore_signal(barrier, inc=1, device_id=dev, device_id_type=MESH)

    greet(to_core)
    greet(to_y)
    for d in range(1, F):
        greet({"fsdp": owner(d)})
    for k in range(1, C):
        greet({"ctx": lax.rem(z + k, C)})

    local = []

    def fetch(src, dst):
        cp = pltpu.make_async_copy(src, dst, ls.at[len(local)])
        cp.start()
        local.append(cp)
        return cp

    own_half = rows(core * HF, HF)
    x_copy = fetch(v.x, v.XB.at[pl.ds(0, R)])
    own_cols = pl.ds(hint(fs * DF, 128), DF)

    def by_row(dst, col0, cols):
        def region(who, off, n):
            return dst.at[rows(who * DF + off, n), pl.ds(col0, cols)]
        return region

    def by_col(dst):
        def region(who, off, n):
            return dst.at[rows(off, n), pl.ds(hint(who * DF, 128), DF)]
        return region

    weights = (
        (v.wq, by_row(v.WQKV, 0, HC), 1), (v.wk, by_row(v.WQKV, HC, HC), 1),
        (v.wv, by_row(v.WQKV, 2 * HC, HC), 1), (v.wo, by_col(v.WO), 1),
        (v.wg, by_col(v.WG), 2), (v.wu, by_col(v.WU), 2), (v.wd, by_col(v.WD), 3),
    )
    gathers = []
    count = 0
    for source, region, parts in weights:
        tall = source.shape[0]
        cuts = [0, tall // 2]
        for _ in range(parts - 1):
            cuts.insert(-1, (cuts[-2] + cuts[-1] + 31) // 32 * 16)
        gathers.append((
            source, fetch(source, region(fs, 0, tall)),
            [(region, tall // 2, cuts[k], cuts[k + 1] - cuts[k], count + k) for k in range(parts)],
        ))
        count += parts
    wq, wk, wv, wo, wg, wu, wd = gathers
    te_copy = fetch(v.teacher.at[own_half], v.TE)
    up_copy = fetch(v.upstream.at[own_half], v.UP)

    pl.semaphore_wait(barrier, F + C)

    def piece_index(kind, number, d):
        return kind + number * (F - 1) + d - 1

    for source, _, pieces in gathers:
        tall = source.shape[0] // 2
        for d in range(1, F):
            group = outgoing(source.at[rows(par * tall, tall)])
            for region, _, at, n, number in pieces:
                off = par * tall + at
                send(
                    source.at[rows(off, n)], region(fs, off, n), piece_index(base.wd, number, d),
                    {"fsdp": owner(d)}, None, group,
                )

    relays = {}

    def relay(weight, which):
        region, tall, at, n, number = weight[2][which]
        for d in range(1, F):
            if which == 0:
                relays[number, d] = outgoing(region(owner(F - d), par * tall, tall))
            part = region(owner(F - d), par * tall + at, n)
            got(part, piece_index(base.wd, number, d))
            send(
                part, part, piece_index(base.wr, number, d), to_pair, None, relays[number - which, d]
            )

    def relayed(weight, with_own=True):
        if with_own:
            weight[1].wait()
        for region, tall, at, n, number in weight[2]:
            for d in range(1, F):
                got(region(owner(F - d), (1 - par) * tall + at, n), piece_index(base.wr, number, d))

    def x_half(j, which):
        return v.XB.at[rows(j * R + which * HF, HF)]

    def x_quarter(j, y):
        return v.XB.at[rows(j * R + core * HF + y * Q, Q)]

    send(v.x.at[rows(core * HF + yy * Q, Q)], x_quarter(1, yy), base.xz, to_next, has_next)
    v.SG[0] = v.segment[...]
    send(v.segment, v.SG.at[1], base.sg, to_next, has_next)
    for j in range(1, W + 1):
        @pl.when(z < j)
        def _(j=j):
            v.XB[pl.ds(j * R, R), :] = jnp.zeros((R, D), bf16)
            v.SG[j] = jnp.full((1, R), -1, jnp.int32)

    def x_pass(j):
        @pl.when(z >= j)
        def _():
            got(x_quarter(j, yy), base.xz + j - 1)
            got(v.SG.at[j], base.sg + j - 1)
        if j < W:
            both = (z >= j) & has_next
            send(x_quarter(j, yy), x_quarter(j + 1, yy), base.xz + j, to_next, both)
            send(v.SG.at[j], v.SG.at[j + 1], base.sg + j, to_next, both)
        send(x_quarter(j, yy), x_quarter(j, yy), base.xy + j - 1, to_y, z >= j)

    def x_join(j):
        pl.when(z >= j)(lambda: got(x_quarter(j, 1 - yy), base.xy + j - 1))
        send(x_half(j, core), x_half(j, core), base.xc + j - 1, to_core, z >= j)

    def x_done(j):
        pl.when(z >= j)(lambda: got(x_half(j, 1 - core), base.xc + j - 1))

    def norm_rows(j):
        def body(i, _):
            at = rows(j * R + i * RC, RC)
            xs = v.XB[at, :].astype(f32)
            r = lax.rsqrt(jnp.mean(xs * xs, axis=-1, keepdims=True) + EPS)
            v.N1[at, :] = (xs * r * v.gain_one[...]).astype(bf16)
            return 0
        lax.fori_loop(0, R // RC, body, 0)

    eye = lax.broadcasted_iota(jnp.int32, (R, R), 0) == lax.broadcasted_iota(jnp.int32, (R, R), 1)
    lower = lax.broadcasted_iota(jnp.int32, (R, R), 1) <= lax.broadcasted_iota(jnp.int32, (R, R), 0)

    def column(row):
        return jnp.sum(jnp.where(eye, row.astype(f32), 0.0), axis=1, keepdims=True)

    x_copy.wait()
    norm_rows(0)
    v.VC[...] = jnp.broadcast_to(column(v.valid[...]), (R, 128))
    relay(wq, 0)
    x_pass(1)
    relay(wk, 0)
    relay(wv, 0)
    for j in range(1, W + 1):
        if j < W:
            x_pass(j + 1)
        x_join(j)
        if j == 1:
            relay(wo, 0)
        if j == W:
            relay(wg, 0)
        x_done(j)
        norm_rows(j)
    seg_col = column(v.SG[0])
    for j in range(W):
        seg_row = jnp.broadcast_to(v.SG[j].astype(f32), (R, R))
        if j == 0:
            seg_row = jnp.where(lower, seg_row, v.SG[W].astype(f32))
        v.BIAS[:, pl.ds(j * R, R)] = jnp.where(seg_col == seg_row, 0.0, -1e30)
    relayed(wq)
    lane_head = lax.broadcasted_iota(jnp.int32, (R, HC), 1) // HEAD_DIM

    def by_heads(ref, val):
        for h in range(H):
            ref[pl.ds(h * R, R), :] = jnp.where(lane_head == h, val, 0.0).astype(bf16)

    def from_heads(ref, other):
        mix = jnp.zeros((R, HC), f32)
        for h in range(H):
            part = jnp.dot(ref[pl.ds(h * R, R), :], other[...], preferred_element_type=f32)
            mix = jnp.where(lane_head == h, part, mix)
        return mix

    by_heads(
        v.QH,
        jnp.dot(v.N1[pl.ds(0, R), :], v.WQKV[:, pl.ds(0, HC)], preferred_element_type=f32),
    )
    relayed(wk)
    relayed(wv)
    for dst, col in ((v.KB, HC), (v.VB, 2 * HC)):
        dst[...] = jnp.dot(
            v.N1[...], v.WQKV[:, pl.ds(col, HC)], preferred_element_type=f32
        ).astype(bf16)
    relay(wg, 1)

    AR = 64 if R % 64 == 0 else R // 4
    WR = W * R

    def merged(i):
        at, inner = rows(i * AR, AR), rows(lax.rem(i, R // AR) * AR, AR)
        place = lax.broadcasted_iota(jnp.int32, (AR, R), 0) + lax.rem(i, R // AR) * AR
        low = lax.broadcasted_iota(jnp.int32, (AR, R), 1) <= place
        first = jnp.where(low, v.S[at, pl.ds(0, R)], v.S[at, pl.ds(WR, R)])
        if W > 1:
            first = jnp.concatenate([first, v.S[at, pl.ds(R, WR - R)]], axis=1)
        return first, at, inner, low

    def spread(ref, at, low, val):
        own = val[:, :R]
        ref[at, pl.ds(0, R)] = jnp.where(low, own, 0.0).astype(bf16)
        ref[at, pl.ds(WR, R)] = jnp.where(low, 0.0, own).astype(bf16)
        if W > 1:
            ref[at, pl.ds(R, WR - R)] = val[:, R:].astype(bf16)

    def soft(i, _):
        s, at, inner, low = merged(i)
        s = s * (HEAD_DIM**-0.5) + v.BIAS[inner, :]
        e = jnp.exp(s - jnp.max(s, axis=-1, keepdims=True))
        prob = e * (1.0 / jnp.sum(e, axis=-1, keepdims=True))
        v.PM[at, :] = prob
        spread(v.PB, at, low, prob)
        return 0

    for h in range(H):
        v.S[pl.ds(h * R, R), :] = contract(v.QH[pl.ds(h * R, R), :], v.KB[...], (1, 1))
    relay(wu, 0)
    lax.fori_loop(0, H * R // AR, soft, 0)
    v.OB[...] = from_heads(v.PB, v.VB).astype(bf16)

    def chunk(i):
        return pl.ds(i * RC, RC)

    def sum_begin(a, product):
        s1, r1, s2, r2 = v.S1.at[a], v.R1.at[a], v.S2.at[a], v.R2.at[a]
        s1[...] = product((1 - core) * HF).astype(bf16)
        first, second = outgoing(s1), outgoing(s2)
        for i in range(NCHK):
            send(s1.at[chunk(i)], r1.at[chunk(i)], base.a + a * NCHK + i, to_core, None, first)
        v.P32[...] = product(core * HF)
        for i in range(NCHK):
            got(r1.at[chunk(i)], base.a + a * NCHK + i)
            s2[chunk(i), :] = (v.P32[chunk(i), :] + r1[chunk(i), :].astype(f32)).astype(bf16)
            send(s2.at[chunk(i)], r2.at[chunk(i)], base.b + a * NCHK + i, to_y, None, second)

    def sum_end(a, i):
        s2, r2 = v.S2.at[a], v.R2.at[a]
        got(r2.at[chunk(i)], base.b + a * NCHK + i)
        return s2[chunk(i), :].astype(f32) + r2[chunk(i), :].astype(f32)

    def my_rows(i):
        return rows(core * HF + i * RC, RC)

    def their_rows(i):
        return rows((1 - core) * HF + i * RC, RC)

    def share(ref, flow, i):
        if i == 0:
            relays[flow] = outgoing(ref.at[own_half])
        send(ref.at[my_rows(i)], ref.at[my_rows(i)], flow + i, to_core, None, relays[flow])

    def shared(ref, flow):
        for i in range(NCHK):
            got(ref.at[their_rows(i)], flow + i)

    relayed(wo)
    sum_begin(
        0,
        lambda off: jnp.dot(v.OB[rows(off, HF), :], v.WO[...], preferred_element_type=f32),
    )
    relay(wu, 1)
    relay(wd, 0)
    for i in range(NCHK):
        h_now = v.XB[my_rows(i), :].astype(f32) + sum_end(0, i)
        v.H[chunk(i), :] = h_now
        r = lax.rsqrt(jnp.mean(h_now * h_now, axis=-1, keepdims=True) + EPS)
        v.N2[my_rows(i), :] = (h_now * r * v.gain_two[...]).astype(bf16)
        share(v.N2, base.n2, i)
        if i == 1:
            relay(wd, 1)
    relay(wd, 2)
    shared(v.N2, base.n2)

    relayed(wg)
    v.GB[...] = contract(v.N2[...], v.WG[...], (1, 1)).astype(bf16)
    relayed(wu)
    v.UB[...] = contract(v.N2[...], v.WU[...], (1, 1)).astype(bf16)

    def activate(i, _):
        at = rows(i * RC, RC)
        g, u = v.GB[at, :].astype(f32), v.UB[at, :].astype(f32)
        v.AB[at, :] = (g / (1.0 + jnp.exp(-g)) * u).astype(bf16)
        return 0

    lax.fori_loop(0, R // RC, activate, 0)
    YR = HF // YROWS
    s1, r1, s2, r2 = v.S1.at[1], v.R1.at[1], v.S2.at[1], v.R2.at[1]
    first, second, to_share = outgoing(s1), outgoing(s2), outgoing(v.DYB.at[own_half])

    def col_block(d):
        return pl.ds(hint(owner(d) * DF, 128), DF)

    def y_parts(d):
        return [(d * YROWS + k, k * YR) for k in range(YROWS)]

    def y_begin(d):
        cols = col_block(d)
        s1[:, cols] = jnp.dot(
            v.AB[rows((1 - core) * HF, HF), :], v.WD[:, cols], preferred_element_type=f32
        ).astype(bf16)
        for i, off in y_parts(d):
            at = s1.at[pl.ds(off, YR), cols]
            send(at, r1.at[pl.ds(off, YR), cols], base.ya + i, to_core, None, first)
        v.P32[:, cols] = jnp.dot(v.AB[own_half, :], v.WD[:, cols], preferred_element_type=f32)
        for i, off in y_parts(d):
            part = pl.ds(off, YR)
            got(r1.at[part, cols], base.ya + i)
            s2[part, cols] = (v.P32[part, cols] + r1[part, cols].astype(f32)).astype(bf16)
            send(s2.at[part, cols], r2.at[part, cols], base.ys + i, to_y, None, second)

    wd[1].wait()
    y_begin(0)
    relayed(wd, False)
    for d in range(1, F):
        y_begin(d)
    te_copy.wait()
    up_copy.wait()
    squares, counted = jnp.zeros((1, 1), f32), jnp.zeros((1, 1), f32)
    for d in range(F):
        cols = col_block(d)
        for i, off in y_parts(d):
            part, mine = pl.ds(off, YR), rows(core * HF + off, YR)
            got(r2.at[part, cols], base.ys + i)
            y_now = v.H[part, cols] + s2[part, cols].astype(f32) + r2[part, cols].astype(f32)
            v.YB[mine, cols] = y_now.astype(bf16)
            weighting = v.VC[mine, pl.ds(0, 1)]
            differ = y_now - v.TE[part, cols].astype(f32)
            squares = squares + total_of(weighting * differ * differ)
            if d == 0:
                counted = counted + total_of(weighting)
            dy = v.UP[part, cols].astype(f32) + weighting * differ
            v.DY[part, cols] = dy
            v.DYB[mine, cols] = dy.astype(bf16)
            at = v.DYB.at[mine, cols]
            send(at, at, base.dy + i, to_core, None, to_share)
    tile_row = lax.broadcasted_iota(jnp.int32, (8, 128), 0)
    tile = jnp.where(
        tile_row == 0, jnp.broadcast_to(squares, (8, 128)), jnp.broadcast_to(counted, (8, 128))
    )
    v.LT[...] = tile
    v.LX[fs] = tile
    for d in range(1, F):
        send(v.LT, v.LX.at[fs], base.lx + d - 1, {"fsdp": owner(d)})
    y_half = v.YB.at[own_half]
    send(y_half, y_half, base.yb, to_core)
    grads_out = [outgoing(v.XS.at[owner(d)]) for d in range(1, F)]
    group_in, group_out = outgoing(v.XS.at[fs]), outgoing(v.GRAD, jnp.logical_not(is_outer))
    for d in range(F):
        for i, off in y_parts(d):
            got(v.DYB.at[rows((1 - core) * HF + off, YR), col_block(d)], base.dy + i)

    sent, own_done = [0], [0]

    def weight_grad(left, right, at, d, flipped=False):
        who = owner(d)
        tokens = left.shape[1 if flipped else 0]
        n = left.shape[0 if flipped else 1]
        if d == 0:
            own_done[0] = at + n
        rhs = right[pl.ds(0, tokens), pl.ds(hint(who * DF, 128), DF)]
        v.XS[who, pl.ds(at, n), :] = contract(left[...], rhs, (1 if flipped else 0, 0)).astype(bf16)

    def grad_index(d, j):
        return base.gx + (d - 1) * (NCH + 1) + j

    def grad_send(d, at, j):
        rcopy(
            v.XS.at[owner(d), at], v.XR.at[d - 1, at], grads_out[d - 1], grad_index(d, j),
            {"fsdp": owner(d)},
        ).start()

    def grads_ready(upto):
        first, last = sent[0], upto // CH
        sent[0] = last

        def body(j, _):
            for d in range(1, F):
                grad_send(d, rows(j * CH, CH), j)
            return 0

        if last > first:
            lax.fori_loop(first, last, body, 0)

    def inward(at, j):
        for d in range(1, F):
            got(v.XR.at[d - 1, at], grad_index(d, j))
        acc = v.XS[fs, at, :].astype(f32)
        for d in range(1, F):
            acc = acc + v.XR[d - 1, at, :].astype(f32)
        v.XS[fs, at, :] = acc.astype(bf16)

        @pl.when(jnp.logical_not(is_outer))
        def _():
            got(v.ZO.at[at], base.zo + j)
            v.XS[fs, at, :] = (acc + v.ZO[at, :].astype(f32)).astype(bf16)

        @pl.when(is_mid)
        def _():
            rcopy(v.XS.at[fs, at], v.ZI.at[at], group_in, base.zi + j, to_inner).start()

        @pl.when(jnp.logical_not(is_mid))
        def _():
            rcopy(v.XS.at[fs, at], v.ZO.at[at], group_in, base.zo + j, to_inner).start()

    def outward(at, j):
        got(v.ZI.at[at], base.zi + j)

        @pl.when(is_mid)
        def _():
            whole = v.XS[fs, at, :].astype(f32) + v.ZI[at, :].astype(f32)
            v.GRAD[at, :] = whole.astype(bf16)

        @pl.when(jnp.logical_not(is_mid))
        def _():
            v.GRAD[at, :] = v.ZI[at, :]

        @pl.when(jnp.logical_not(is_outer))
        def _():
            rcopy(v.GRAD.at[at], v.ZI.at[at], group_out, base.zi + j, to_outer).start()

        pltpu.make_async_copy(v.GRAD.at[at], v.grad_out.at[at], ls.at[10]).start()

    lag_in, lag_out = SKEW * hop, SKEW * (2 * half - 1 - hop)
    LAST = NCH + SKEW * (2 * half - 1)

    def pump(first, last):
        def body(i, _):
            ja, jb = i - lag_in, i - lag_out
            pl.when((ja >= 0) & (ja < NCH))(lambda: inward(rows(ja * CH, CH), ja))
            pl.when((jb >= 0) & (jb < NCH))(lambda: outward(rows(jb * CH, CH), jb))
            return 0

        if last > first:
            lax.fori_loop(first, last, body, 0)

    pumped = [0]

    def pump_to(place):
        last = LAST if place > 49 else place * NCH // 49
        ready = min(sent[0], own_done[0] // CH)
        last = min(last, ready if ready < NCH else LAST)
        if last > pumped[0]:
            pump(pumped[0], last)
            pumped[0] = last

    peers = range(1, F)
    for d in peers:
        weight_grad(v.AB, v.DYB, 0, d)
    grads_ready(FF)
    v.S[pl.ds(0, R), pl.ds(0, FF)] = contract(v.DYB[...], v.WD[...], (1, 1))

    def activate_back(i, _):
        at = rows(i * RC, RC)
        g, u, da = v.GB[at, :].astype(f32), v.UB[at, :].astype(f32), v.S[at, pl.ds(0, FF)]
        sig = 1.0 / (1.0 + jnp.exp(-g))
        v.DGB[at, :] = (da * u * (sig * (1.0 + g * (1.0 - sig)))).astype(bf16)
        v.DUB[at, :] = (da * (g * sig)).astype(bf16)
        return 0

    lax.fori_loop(0, R // RC, activate_back, 0)
    sum_begin(
        2,
        lambda off: jnp.dot(v.DGB[rows(off, HF), :], v.WG[...], preferred_element_type=f32)
        + jnp.dot(v.DUB[rows(off, HF), :], v.WU[...], preferred_element_type=f32),
    )
    weight_grad(v.AB, v.DYB, 0, 0)
    for d in peers:
        got(v.LX.at[owner(F - d)], base.lx + d - 1)
    send(v.LX, v.LC, base.lc, to_core)
    for d in peers:
        weight_grad(v.DGB, v.N2, FF, d)
    grads_ready(2 * FF)
    for d in peers:
        weight_grad(v.DUB, v.N2, 2 * FF, d)
    grads_ready(3 * FF)
    weight_grad(v.DGB, v.N2, FF, 0)
    weight_grad(v.DUB, v.N2, 2 * FF, 0)
    pump_to(2)
    v.GT[0] = jnp.zeros((8, D), f32)
    for i in range(NCHK):
        dn2 = sum_end(2, i)
        h_now = v.H[chunk(i), :]
        r = lax.rsqrt(jnp.mean(h_now * h_now, axis=-1, keepdims=True) + EPS)
        gd = v.gain_two[...] * dn2
        dh = v.DY[chunk(i), :] + r * gd - h_now * (
            r * r * r * jnp.mean(gd * h_now, axis=-1, keepdims=True)
        )
        v.DH[chunk(i), :] = dh
        v.DHB[my_rows(i), :] = dh.astype(bf16)
        share(v.DHB, base.dh, i)
        part = jnp.sum(dn2 * h_now * r, axis=0, keepdims=True)
        part = jnp.where(yy == i // (NCHK // 2), part, 0.0)
        v.GT[0, pl.ds(0, 1), :] = v.GT[0, pl.ds(0, 1), :] + part
        pump_to(3 + i)
    shared(v.DHB, base.dh)
    got(v.LC, base.lc)
    v.LB[z] = v.LX[...] + v.LC[...]
    for k in range(1, C):
        send(v.LB.at[z], v.LB.at[z], base.ll + k - 1, {"ctx": lax.rem(z + k, C)})

    by_heads(v.DOH, contract(v.DHB[...], v.WO[...], (1, 1)))
    pump_to(7)
    for h in range(H):
        v.S[pl.ds(h * R, R), :] = contract(v.DOH[pl.ds(h * R, R), :], v.VB[...], (1, 1))
    for d in peers:
        weight_grad(v.OB, v.DHB, 3 * FF, d)
    grads_ready(3 * FF + HC)
    weight_grad(v.OB, v.DHB, 3 * FF, 0)
    pump_to(8)

    def soft_back(i, _):
        dp, at, _, low = merged(i)
        prob = v.PM[at, :]
        spread(v.DSB, at, low, prob * (dp - jnp.sum(prob * dp, axis=-1, keepdims=True)))
        return 0

    lax.fori_loop(0, H * R // AR, soft_back, 0)
    pump_to(9)
    scale = HEAD_DIM**-0.5
    v.DVT[...] = contract(v.DOH[...], v.PB[...], (0, 0)).astype(bf16)
    v.DKT[...] = (contract(v.QH[...], v.DSB[...], (0, 0)) * scale).astype(bf16)
    v.DQ[...] = (from_heads(v.DSB, v.KB) * scale).astype(bf16)
    pump_to(11)

    def dn1_product(j, which):
        at = pl.ds(hint(j * R + which * HF, 128), HF)
        out = contract(v.DKT[:, at], v.WQKV[:, pl.ds(HC, HC)], (0, 1))
        out = out + contract(v.DVT[:, at], v.WQKV[:, pl.ds(2 * HC, HC)], (0, 1))
        if j == 0:
            out = out + contract(v.DQ[rows(which * HF, HF), :], v.WQKV[:, pl.ds(0, HC)], (1, 1))
        return out

    for j in range(W, -1, -1):
        v.D1S[j] = dn1_product(j, 1 - core).astype(bf16)
        send(v.D1S.at[j], v.D1R.at[j], base.d1 + j, to_core)
        v.D1O[j] = dn1_product(j, core)
    for d in list(peers) + [0]:
        at = 3 * FF + HC
        weight_grad(v.DQ, v.N1, at, d)
        weight_grad(v.DKT, v.N1, at + HC, d, True)
        weight_grad(v.DVT, v.N1, at + 2 * HC, d, True)
        if d == F - 1:
            grads_ready(N)
    pump_to(13)
    for j in range(W, -1, -1):
        got(v.D1R.at[j], base.d1 + j)
        there = rows((1 - yy) * Q, Q)
        v.D2S[j] = (v.D1O[j, there, :] + v.D1R[j, there, :].astype(f32)).astype(bf16)
        send(v.D2S.at[j], v.D2R.at[j], base.d2 + j, to_y)
    pump_to(16)
    here = rows(yy * Q, Q)
    for j in range(W, 0, -1):
        got(v.D2R.at[j], base.d2 + j)
        own = v.D1O[j, here, :] + v.D1R[j, here, :].astype(f32) + v.D2R[j].astype(f32)
        v.DZS[j] = own.astype(bf16)
        if j < W:
            @pl.when(has_next & (z >= j))
            def _(j=j, own=own):
                got(v.DZR.at[j + 1], base.dz + j + 1)
                v.DZS[j] = (own + v.DZR[j + 1].astype(f32)).astype(bf16)
        send(v.DZS.at[j], v.DZR.at[j], base.dz + j, to_prev, z >= j)
        pump_to(19 + 2 * (W - j))

    pump_to(23)
    pump_to(26)
    got(v.D2R.at[0], base.d2)
    v.P32[pl.ds(0, Q), :] = (
        v.D1O[0, here, :] + v.D1R[0, here, :].astype(f32) + v.D2R[0].astype(f32)
    )

    @pl.when(has_next)
    def _():
        got(v.DZR.at[1], base.dz + 1)
        v.P32[pl.ds(0, Q), :] = v.P32[pl.ds(0, Q), :] + v.DZR[1].astype(f32)

    quarter = rows(core * HF + yy * Q, Q)
    dn1 = v.P32[pl.ds(0, Q), :]
    x_now = v.XB[quarter, :].astype(f32)
    r = lax.rsqrt(jnp.mean(x_now * x_now, axis=-1, keepdims=True) + EPS)
    gd = v.gain_one[...] * dn1
    gi = v.DH[here, :] + r * gd - x_now * (
        r * r * r * jnp.mean(gd * x_now, axis=-1, keepdims=True)
    )
    v.GIB[quarter, :] = gi.astype(bf16)
    mine = v.GIB.at[quarter]
    send(mine, mine, base.i1, to_y)
    send(mine, mine, base.i2, to_core)
    v.GT[0, pl.ds(1, 1), :] = jnp.sum(dn1 * x_now * r, axis=0, keepdims=True)
    send(v.GT.at[0], v.GR.at[0], base.g1, to_core)
    pump_to(28)
    got(v.GR.at[0], base.g1)
    v.GT[1] = v.GT[0] + v.GR[0]
    send(v.GT.at[1], v.GR.at[1], base.g2, to_y)
    from_y = v.GIB.at[rows(core * HF + (1 - yy) * Q, Q)]
    got(from_y, base.i1)
    send(from_y, from_y, base.i3, to_core)
    pump_to(32)
    got(v.GR.at[1], base.g2)
    v.GT[2] = v.GT[1] + v.GR[1]
    for d in list(peers) + [0]:
        tile = v.GT[2, :, pl.ds(hint(owner(d) * DF, 128), DF)]
        v.XS[owner(d), pl.ds(N, 16), :] = jnp.concatenate([tile, jnp.zeros_like(tile)], 0).astype(bf16)
        if d:
            grad_send(d, pl.ds(N, 16), NCH)

    pump_to(49)
    gain_rows = pl.ds(N, 16)
    inward(gain_rows, NCH)
    for k in range(1, C):
        got(v.LB.at[lax.rem(z + C - k, C)], base.ll + k - 1)
    sums = [sum(v.LB[c, s] for c in range(C)) for s in range(F)]
    counted = sum(s[1:2, :] for s in sums)
    for s in range(F):
        v.LOSS[pl.ds(s, 1), :] = sums[s][0:1, :] * F / (counted * D)
    got(v.YB.at[rows((1 - core) * HF, HF)], base.yb)
    got(v.GIB.at[rows((1 - core) * HF + yy * Q, Q)], base.i2)
    got(v.GIB.at[rows((1 - core) * HF + (1 - yy) * Q, Q)], base.i3)
    results = (
        pltpu.make_async_copy(v.YB, v.y_out, ls.at[0]),
        pltpu.make_async_copy(v.GIB, v.gi_out, ls.at[1]),
        pltpu.make_async_copy(v.LOSS, v.loss_out, ls.at[2]),
    )
    for cp in results:
        cp.start()

    streams = grads_out + [group_in, group_out]

    def all_left(k):
        src, cond = unsent[k]

        def left():
            rcopy(src, src, k, 0, to_core).wait_send()

        if cond is None:
            left()
        else:
            pl.when(cond)(left)

    for k in range(len(unsent)):
        if k not in streams:
            all_left(k)
    pump_to(50)
    outward(gain_rows, NCH)
    for k in streams:
        all_left(k)
    for cp in results:
        cp.wait()
    pltpu.make_async_copy(v.GRAD, v.grad_out, ls.at[10]).wait()


def finish_kernel(p, grad, gib, yb, loss, *refs):
    (y_out, loss_out, gi_out, one, gq, gk, gv, go, two, gg, gu, gd) = refs[:12]
    g_buf, i_buf, y_buf, l_buf, g_wide, i_wide, q_wide, sem_in, sem_out = refs[12:]
    FF, HC, N = p.FF, p.HC, p.N
    at = 3 * FF
    plain, flip = [], []
    for ref, first in ((gd, 0), (gg, FF), (gu, 2 * FF)):
        plain += [(ref, first, 0, FF // 2), (ref, first + FF // 2, FF // 2, FF // 2)]
    plain.append((go, at, 0, HC))
    flip = [(gq, at + HC), (gk, at + 2 * HC), (gv, at + 3 * HC)]
    loads = []

    def load(src, dst):
        cp = pltpu.make_async_copy(src, dst, sem_in.at[len(loads)])
        cp.start()
        loads.append(cp)
        return cp

    stores = []

    def store(src, dst):
        cp = pltpu.make_async_copy(src, dst, sem_out.at[len(stores)])
        cp.start()
        stores.append(cp)

    plain_in = [load(grad.at[pl.ds(f, n)], g_buf.at[pl.ds(f, n)]) for _, f, _, n in plain]
    flip_in = [load(grad.at[pl.ds(f, HC)], g_buf.at[pl.ds(f, HC)]) for _, f in flip]
    gi_in = load(gib, i_buf)
    y_in = load(yb, y_buf)
    gain_in = load(grad.at[pl.ds(N, 16)], g_buf.at[pl.ds(N, 16)])
    loss_in = load(loss, l_buf)
    for (ref, first, row, n), cp in zip(plain, plain_in):
        cp.wait()
        g_wide[pl.ds(first, n), :] = g_buf[pl.ds(first, n), :].astype(f32)
        store(g_wide.at[pl.ds(first, n)], ref.at[pl.ds(row, n)])
    for k, ((ref, first), cp) in enumerate(zip(flip, flip_in)):
        cp.wait()
        for c in range(0, HC, 128):
            w = min(128, HC - c)
            q_wide[k, :, pl.ds(c, w)] = g_buf[pl.ds(first + c, w), :].astype(f32).T
        store(q_wide.at[k], ref)
    gi_in.wait()
    i_wide[...] = i_buf[...].astype(f32)
    store(i_wide, gi_out.at[0])
    y_in.wait()
    store(y_buf, y_out.at[0])
    gain_in.wait()
    gains = g_buf[pl.ds(N, 16), :].astype(f32)
    two[...] = gains[0:1, :]
    one[...] = gains[1:2, :]
    loss_in.wait()
    for s in range(p.F):
        loss_out[s] = jnp.max(l_buf[pl.ds(s, 1), :])
    for cp in stores:
        cp.wait()


def shards(mesh_shape, seq_len, *args):
    (inputs, upstream, teacher, valid, segment, gain_one, wq, wk, wv, wo, gain_two, wg, wu, wd) = args
    _, rows_here, width = inputs.shape
    p = Plan(
        mesh_shape["fsdp"], mesh_shape["ctx"], rows_here, width, wq.shape[1], wg.shape[1], seq_len
    )
    R, D, DF, HC, FF, F = p.R, p.D, p.DF, p.HC, p.FF, p.F
    NG = p.N + 16
    scratch = scratch_of(p)
    vmem = pl.BlockSpec(memory_space=pltpu.VMEM)
    anywhere = pl.BlockSpec(memory_space=pl.ANY)
    in_specs = [anywhere] * 3 + [vmem] * 3 + [anywhere] * 4 + [vmem] + [anywhere] * 3
    sds = jax.ShapeDtypeStruct
    grad, gib, yb, loss = pl.pallas_call(
        functools.partial(layer_kernel, p, tuple(scratch)),
        out_shape=(
            sds((NG, DF), bf16), sds((R, D), bf16), sds((R, D), bf16), sds((max(F, 8), 128), f32),
        ),
        in_specs=in_specs,
        out_specs=(anywhere,) * 4,
        scratch_shapes=[pltpu.VMEM(s, dt) for s, dt in scratch.values()]
        + [
            pltpu.SemaphoreType.DMA((p.sends,)), pltpu.SemaphoreType.DMA((p.total,)),
            pltpu.SemaphoreType.DMA((11,)),
        ],
        compiler_params=pltpu.CompilerParams(
            collective_id=0, has_side_effects=True, vmem_limit_bytes=67043328
        ),
        name="layer",
    )(
        inputs.reshape(R, D), upstream.reshape(R, D), teacher.reshape(R, D), valid, segment,
        gain_one.reshape(1, D), wq, wk, wv, wo, gain_two.reshape(1, D), wg.T, wu.T, wd,
    )
    outs = pl.pallas_call(
        functools.partial(finish_kernel, p),
        out_shape=(
            sds((1, R, D), bf16), sds((F,), f32), sds((1, R, D), f32), sds((1, DF), f32),
            sds((DF, HC), f32), sds((DF, HC), f32), sds((DF, HC), f32), sds((HC, DF), f32),
            sds((1, DF), f32), sds((FF, DF), f32), sds((FF, DF), f32), sds((FF, DF), f32),
        ),
        in_specs=[anywhere] * 4,
        out_specs=(anywhere, pl.BlockSpec(memory_space=pltpu.SMEM), anywhere, vmem)
        + (anywhere,) * 4 + (vmem,) + (anywhere,) * 3,
        scratch_shapes=[
            pltpu.VMEM((NG, DF), bf16), pltpu.VMEM((R, D), bf16), pltpu.VMEM((R, D), bf16),
            pltpu.VMEM((max(F, 8), 128), f32), pltpu.VMEM((3 * FF + HC, DF), f32),
            pltpu.VMEM((R, D), f32), pltpu.VMEM((3, DF, HC), f32),
            pltpu.SemaphoreType.DMA((14,)), pltpu.SemaphoreType.DMA((12,)),
        ],
        compiler_params=pltpu.CompilerParams(vmem_limit_bytes=67043328),
        name="finish",
    )(grad, gib, yb, loss)
    outs = list(outs)
    outs[3], outs[8] = outs[3].reshape(DF), outs[8].reshape(DF)
    outs[9], outs[10] = outs[9].T, outs[10].T
    return tuple(outs)


def solution(mesh):
    def run(*args):
        token, row, col = P("fsdp", "ctx", None), P("fsdp", "tp"), P("tp", "fsdp")
        pair = P("fsdp", "ctx")
        return jax.shard_map(
            functools.partial(shards, dict(mesh.shape), args[0].shape[1]),
            mesh=mesh,
            in_specs=(token, token, token, pair, pair, P(), row, row, row, col, P(), row, row, col),
            out_specs=(
                token, P(), token, P("fsdp"), row, row, row, col, P("fsdp"), row, row, col,
            ),
            check_vma=False,
        )(*args)

    return run
```

```python
import functools
from types import SimpleNamespace

import jax
import jax.numpy as jnp
from jax import lax
from jax.experimental import pallas as pl
from jax.experimental.pallas import tpu as pltpu
from jax.sharding import PartitionSpec as P

HEAD_DIM = 64
EPS = 1e-05
MESH = pl.DeviceIdType.MESH
NCHK = 4
YROWS = 2
SKEW = 2
f32, bf16 = jnp.float32, jnp.bfloat16


class Plan:
    def __init__(self, fsdp, ctx, rows, width, head_cols, hidden, seq_len):
        self.F, self.C, self.R, self.D = fsdp, ctx, rows, width
        self.HC, self.FF = head_cols, hidden
        self.DF = width // fsdp
        self.W = -(-(seq_len // 2) // rows)
        self.N = 3 * hidden + 4 * head_cols
        self.CH = next(
            k for k in range(16, self.N + 1, 16) if self.N % k == 0 and k * self.DF >= 57344
        )
        self.NCH = self.N // self.CH
        self.base, self.total = SimpleNamespace(), 0
        peers = fsdp - 1
        for name, count in dict(
            ya=YROWS * fsdp, ys=YROWS * fsdp, xz=2 * self.W, sg=self.W, xy=2 * self.W, xc=self.W, wd=11 * peers, wr=11 * peers,
            a=3 * NCHK, b=3 * NCHK, n2=NCHK, yb=1, dy=YROWS * fsdp, dh=NCHK,
            lc=1, ll=ctx - 1, lx=peers, d1=self.W + 1, d2=self.W + 1, dz=self.W + 1,
            g1=1, g2=1, i1=1, i2=1, i3=1, gx=peers * (self.NCH + 1),
            zo=self.NCH + 1, zi=self.NCH + 1,
        ).items():
            setattr(self.base, name, self.total)
            self.total += count
        self.sends = 4 * self.W + 2 + 14 * peers + 9 + 3 + 2 * ctx + peers + 3 * self.W + 2 + 5 + peers + 2


def contract(left, right, dims):
    return lax.dot_general(left, right, ((dims[:1], dims[1:]), ((), ())), preferred_element_type=f32)


def total_of(v):
    return jnp.sum(jnp.sum(v, axis=1, keepdims=True), axis=0, keepdims=True)


def scratch_of(p):
    R, D, HC, FF, DF, F, C, W = p.R, p.D, p.HC, p.FF, p.DF, p.F, p.C, p.W
    HF, Q, KR, H = R // 2, R // 4, (p.W + 1) * p.R, p.HC // HEAD_DIM
    NG = p.N + 16
    return dict(
        XB=((KR, D), bf16), SG=((W + 1, 1, R), jnp.int32), N1=((KR, D), bf16),
        WQKV=((D, 3 * HC), bf16), WO=((HC, D), bf16), WG=((FF, D), bf16),
        WU=((FF, D), bf16), WD=((FF, D), bf16),
        QH=((H * R, HC), bf16), KB=((KR, HC), bf16), VB=((KR, HC), bf16), DOH=((H * R, HC), bf16),
        PM=((H * R, W * R), f32), S=((H * R, KR), f32), PB=((H * R, KR), bf16), DSB=((H * R, KR), bf16),
        BIAS=((R, W * R), f32), DQ=((R, HC), bf16), DKT=((HC, KR), bf16), DVT=((HC, KR), bf16),
        OB=((R, HC), bf16), VC=((R, 128), f32),
        H=((HF, D), f32), DY=((HF, D), f32), DH=((HF, D), f32), P32=((HF, D), f32),
        UP=((HF, D), bf16), TE=((HF, D), bf16),
        N2=((R, D), bf16), DYB=((R, D), bf16), DHB=((R, D), bf16),
        GB=((R, FF), bf16), UB=((R, FF), bf16), AB=((R, FF), bf16),
        DGB=((R, FF), bf16), DUB=((R, FF), bf16),
        D1S=((W + 1, HF, D), bf16), D1R=((W + 1, HF, D), bf16), D1O=((W + 1, HF, D), f32),
        D2S=((W + 1, Q, D), bf16), D2R=((W + 1, Q, D), bf16), DZR=((W + 1, Q, D), bf16),
        DZS=((W + 1, Q, D), bf16),
        GT=((3, 8, D), f32), GR=((2, 8, D), f32),
        LT=((8, 128), f32), LX=((F, 8, 128), f32), LC=((F, 8, 128), f32), LB=((C, F, 8, 128), f32),
        XS=((F, NG, DF), bf16), XR=((F - 1, NG, DF), bf16),
        ZO=((NG, DF), bf16), ZI=((NG, DF), bf16), GRAD=((NG, DF), bf16), GIB=((R, D), bf16),
        YB=((R, D), bf16), LOSS=((max(F, 8), 128), f32),
        S1=((3, HF, D), bf16), R1=((3, HF, D), bf16), S2=((3, HF, D), bf16), R2=((3, HF, D), bf16),
    )


def layer_kernel(p, names, *refs):
    v = SimpleNamespace(**dict(zip(names, refs[18:], strict=False)))
    (
        v.x, v.upstream, v.teacher, v.valid, v.segment, v.gain_one, v.wq, v.wk, v.wv, v.wo,
        v.gain_two, v.wg, v.wu, v.wd, v.grad_out, v.gi_out, v.y_out, v.loss_out,
    ) = refs[:18]
    ss, rs, ls = refs[-3:]
    R, D, HC, FF, DF, F, C, W, N, CH, NCH = (
        p.R, p.D, p.HC, p.FF, p.DF, p.F, p.C, p.W, p.N, p.CH, p.NCH
    )
    HF, Q, KR, H = R // 2, R // 4, (W + 1) * R, HC // HEAD_DIM
    RC = HF // NCHK
    base = p.base
    fs, z, t = lax.axis_index("fsdp"), lax.axis_index("ctx"), lax.axis_index("tp")
    core, yy, par = lax.rem(t, 2), t // 2, lax.rem(z, 2)
    to_core, to_y = {"tp": t + 1 - 2 * core}, {"tp": lax.rem(t + 2, 4)}
    to_next, to_prev = {"ctx": lax.rem(z + 1, C)}, {"ctx": lax.rem(z + C - 1, C)}
    to_pair = {"ctx": z + 1 - 2 * par}
    has_next, has_prev = z < C - 1, z > 0
    half = C // 2
    left_side = z < half
    hop = jnp.where(left_side, z, C - 1 - z)
    step_in = jnp.where(left_side, 1, -1)
    to_inner = {"ctx": z + step_in}
    to_outer = {"ctx": lax.rem(z - step_in + C, C)}
    is_outer, is_mid = hop == 0, hop == half - 1

    def owner(d):
        return lax.rem(fs + d, F)

    def rcopy(src, dst, sk, rk, dev):
        return pltpu.make_async_remote_copy(
            src_ref=src, dst_ref=dst, send_sem=ss.at[sk], recv_sem=rs.at[rk],
            device_id=dev, device_id_type=MESH,
        )

    unsent = []

    def outgoing(src, cond=None):
        unsent.append((src, cond))
        assert len(unsent) <= p.sends
        return len(unsent) - 1

    def send(src, dst, k, dev, cond=None, group=None):
        sk = outgoing(src, cond) if group is None else group
        if cond is None:
            rcopy(src, dst, sk, k, dev).start()
        else:
            pl.when(cond)(lambda: rcopy(src, dst, sk, k, dev).start())

    def got(dst, k):
        rcopy(dst, dst, 0, k, to_core).wait_recv()

    def hint(i, m):
        return pl.multiple_of(i, m)

    def rows(off, n, m=16):
        return pl.ds(hint(off, m), n)

    barrier = pltpu.get_barrier_semaphore()

    def greet(dev):
        pl.semaphore_signal(barrier, inc=1, device_id=dev, device_id_type=MESH)

    greet(to_core)
    greet(to_y)
    for d in range(1, F):
        greet({"fsdp": owner(d)})
    for k in range(1, C):
        greet({"ctx": lax.rem(z + k, C)})

    local = []

    def fetch(src, dst):
        cp = pltpu.make_async_copy(src, dst, ls.at[len(local)])
        cp.start()
        local.append(cp)
        return cp

    own_half = rows(core * HF, HF)
    x_copy = fetch(v.x, v.XB.at[pl.ds(0, R)])
    own_cols = pl.ds(hint(fs * DF, 128), DF)

    def by_row(dst, col0, cols):
        def region(who, off, n):
            return dst.at[rows(who * DF + off, n), pl.ds(col0, cols)]
        return region

    def by_col(dst):
        def region(who, off, n):
            return dst.at[rows(off, n), pl.ds(hint(who * DF, 128), DF)]
        return region

    weights = (
        (v.wq, by_row(v.WQKV, 0, HC), 1), (v.wk, by_row(v.WQKV, HC, HC), 1),
        (v.wv, by_row(v.WQKV, 2 * HC, HC), 1), (v.wo, by_col(v.WO), 1),
        (v.wg, by_col(v.WG), 2), (v.wu, by_col(v.WU), 2), (v.wd, by_col(v.WD), 3),
    )
    gathers = []
    count = 0
    for source, region, parts in weights:
        tall = source.shape[0]
        cuts = [0, tall // 2] if parts == 1 else [0, tall // 4, tall // 2]
        if parts == 3:
            cuts.insert(2, tall // 3 // 16 * 16)
        gathers.append((
            source, fetch(source, region(fs, 0, tall)),
            [
                (region, cuts[min(parts, 2)], tall // 2, cuts[k], cuts[k + 1] - cuts[k], count + k)
                for k in range(parts)
            ],
        ))
        count += parts
    wq, wk, wv, wo, wg, wu, wd = gathers
    te_copy = fetch(v.teacher.at[own_half], v.TE)
    up_copy = fetch(v.upstream.at[own_half], v.UP)

    pl.semaphore_wait(barrier, F + C)

    def piece_index(kind, number, d):
        return kind + number * (F - 1) + d - 1

    for source, _, pieces in gathers:
        tall = source.shape[0] // 2
        for d in range(1, F):
            group = outgoing(source.at[rows(par * tall, tall)])
            for region, passed, _, at, n, number in pieces:
                off = par * tall + at
                send(
                    source.at[rows(off, n)], region(fs, off, n), piece_index(base.wd, number, d),
                    {"fsdp": owner(d)}, None, group,
                )
                if at >= passed:
                    off = (1 - par) * tall + at
                    send(
                        source.at[rows(off, n)], region(fs, off, n),
                        piece_index(base.wr, number, d), {"fsdp": owner(d)},
                    )

    relays = {}

    def relay(weight, which):
        region, passed, tall, at, n, number = weight[2][which]
        for d in range(1, F):
            if which == 0:
                relays[number, d] = outgoing(region(owner(F - d), par * tall, passed))
            part = region(owner(F - d), par * tall + at, n)
            got(part, piece_index(base.wd, number, d))
            send(
                part, part, piece_index(base.wr, number, d), to_pair, None, relays[number - which, d]
            )

    def relayed(weight, with_own=True):
        if with_own:
            weight[1].wait()
        for region, passed, tall, at, n, number in weight[2]:
            for d in range(1, F):
                if at >= passed:
                    got(region(owner(F - d), par * tall + at, n), piece_index(base.wd, number, d))
                got(region(owner(F - d), (1 - par) * tall + at, n), piece_index(base.wr, number, d))

    def x_half(j, which):
        return v.XB.at[rows(j * R + which * HF, HF)]

    def x_eighth(j, y, k):
        return v.XB.at[rows(j * R + core * HF + y * Q + k * (Q // 2), Q // 2)]

    def x_quarter(j, y):
        return v.XB.at[rows(j * R + core * HF + y * Q, Q)]

    x_group = outgoing(x_quarter(0, yy), has_next)
    for k in range(2):
        send(
            v.x.at[rows(core * HF + yy * Q + k * (Q // 2), Q // 2)], x_eighth(1, yy, k), base.xz + k,
            to_next, has_next, x_group,
        )
    v.SG[0] = v.segment[...]
    send(v.segment, v.SG.at[1], base.sg, to_next, has_next)
    for j in range(1, W + 1):
        @pl.when(z < j)
        def _(j=j):
            v.XB[pl.ds(j * R, R), :] = jnp.zeros((R, D), bf16)
            v.SG[j] = jnp.full((1, R), -1, jnp.int32)

    def x_pass(j):
        both = (z >= j) & has_next
        onward = outgoing(x_quarter(j, yy), both) if j < W else None
        across = outgoing(x_quarter(j, yy), z >= j)
        for k in range(2):
            part = x_eighth(j, yy, k)
            pl.when(z >= j)(lambda part=part, k=k: got(part, base.xz + 2 * (j - 1) + k))
            if j < W:
                send(part, x_eighth(j + 1, yy, k), base.xz + 2 * j + k, to_next, both, onward)
            send(part, part, base.xy + 2 * (j - 1) + k, to_y, z >= j, across)
        pl.when(z >= j)(lambda: got(v.SG.at[j], base.sg + j - 1))
        if j < W:
            send(v.SG.at[j], v.SG.at[j + 1], base.sg + j, to_next, both)

    def x_join(j):
        for k in range(2):
            pl.when(z >= j)(
                lambda k=k: got(x_eighth(j, 1 - yy, k), base.xy + 2 * (j - 1) + k)
            )
        send(x_half(j, core), x_half(j, core), base.xc + j - 1, to_core, z >= j)

    def x_done(j):
        pl.when(z >= j)(lambda: got(x_half(j, 1 - core), base.xc + j - 1))

    def norm_rows(j):
        def body(i, _):
            at = rows(j * R + i * RC, RC)
            xs = v.XB[at, :].astype(f32)
            r = lax.rsqrt(jnp.mean(xs * xs, axis=-1, keepdims=True) + EPS)
            v.N1[at, :] = (xs * r * v.gain_one[...]).astype(bf16)
            return 0
        lax.fori_loop(0, R // RC, body, 0)

    eye = lax.broadcasted_iota(jnp.int32, (R, R), 0) == lax.broadcasted_iota(jnp.int32, (R, R), 1)
    lower = lax.broadcasted_iota(jnp.int32, (R, R), 1) <= lax.broadcasted_iota(jnp.int32, (R, R), 0)

    def column(row):
        return jnp.sum(jnp.where(eye, row.astype(f32), 0.0), axis=1, keepdims=True)

    x_copy.wait()
    norm_rows(0)
    v.VC[...] = jnp.broadcast_to(column(v.valid[...]), (R, 128))
    x_pass(1)
    relay(wq, 0)
    relay(wk, 0)
    relay(wv, 0)
    for j in range(1, W + 1):
        if j < W:
            x_pass(j + 1)
        x_join(j)
        if j == 1:
            relay(wo, 0)
        if j == W:
            relay(wg, 0)
        x_done(j)
        norm_rows(j)
    seg_col = column(v.SG[0])
    for j in range(W):
        seg_row = jnp.broadcast_to(v.SG[j].astype(f32), (R, R))
        if j == 0:
            seg_row = jnp.where(lower, seg_row, v.SG[W].astype(f32))
        v.BIAS[:, pl.ds(j * R, R)] = jnp.where(seg_col == seg_row, 0.0, -1e30)
    relayed(wq)
    lane_head = lax.broadcasted_iota(jnp.int32, (R, HC), 1) // HEAD_DIM

    def by_heads(ref, val):
        for h in range(H):
            ref[pl.ds(h * R, R), :] = jnp.where(lane_head == h, val, 0.0).astype(bf16)

    def from_heads(ref, other):
        mix = jnp.zeros((R, HC), f32)
        for h in range(H):
            part = jnp.dot(ref[pl.ds(h * R, R), :], other[...], preferred_element_type=f32)
            mix = jnp.where(lane_head == h, part, mix)
        return mix

    by_heads(
        v.QH,
        jnp.dot(v.N1[pl.ds(0, R), :], v.WQKV[:, pl.ds(0, HC)], preferred_element_type=f32),
    )
    relayed(wk)
    relayed(wv)
    for dst, col in ((v.KB, HC), (v.VB, 2 * HC)):
        dst[...] = jnp.dot(
            v.N1[...], v.WQKV[:, pl.ds(col, HC)], preferred_element_type=f32
        ).astype(bf16)
    relay(wg, 1)

    AR = 64 if R % 64 == 0 else R // 4
    WR = W * R

    def merged(i):
        at, inner = rows(i * AR, AR), rows(lax.rem(i, R // AR) * AR, AR)
        place = lax.broadcasted_iota(jnp.int32, (AR, R), 0) + lax.rem(i, R // AR) * AR
        low = lax.broadcasted_iota(jnp.int32, (AR, R), 1) <= place
        first = jnp.where(low, v.S[at, pl.ds(0, R)], v.S[at, pl.ds(WR, R)])
        if W > 1:
            first = jnp.concatenate([first, v.S[at, pl.ds(R, WR - R)]], axis=1)
        return first, at, inner, low

    def spread(ref, at, low, val):
        own = val[:, :R]
        ref[at, pl.ds(0, R)] = jnp.where(low, own, 0.0).astype(bf16)
        ref[at, pl.ds(WR, R)] = jnp.where(low, 0.0, own).astype(bf16)
        if W > 1:
            ref[at, pl.ds(R, WR - R)] = val[:, R:].astype(bf16)

    def soft(i, _):
        s, at, inner, low = merged(i)
        s = s * (HEAD_DIM**-0.5) + v.BIAS[inner, :]
        e = jnp.exp(s - jnp.max(s, axis=-1, keepdims=True))
        prob = e * (1.0 / jnp.sum(e, axis=-1, keepdims=True))
        v.PM[at, :] = prob
        spread(v.PB, at, low, prob)
        return 0

    for h in range(H):
        v.S[pl.ds(h * R, R), :] = contract(v.QH[pl.ds(h * R, R), :], v.KB[...], (1, 1))
    lax.fori_loop(0, H * R // AR, soft, 0)
    relay(wu, 0)
    v.OB[...] = from_heads(v.PB, v.VB).astype(bf16)

    def chunk(i):
        return pl.ds(i * RC, RC)

    def sum_begin(a, product):
        s1, r1, s2, r2 = v.S1.at[a], v.R1.at[a], v.S2.at[a], v.R2.at[a]
        s1[...] = product((1 - core) * HF).astype(bf16)
        first, second = outgoing(s1), outgoing(s2)
        for i in range(NCHK):
            send(s1.at[chunk(i)], r1.at[chunk(i)], base.a + a * NCHK + i, to_core, None, first)
        v.P32[...] = product(core * HF)
        for i in range(NCHK):
            got(r1.at[chunk(i)], base.a + a * NCHK + i)
            s2[chunk(i), :] = (v.P32[chunk(i), :] + r1[chunk(i), :].astype(f32)).astype(bf16)
            send(s2.at[chunk(i)], r2.at[chunk(i)], base.b + a * NCHK + i, to_y, None, second)

    def sum_end(a, i):
        s2, r2 = v.S2.at[a], v.R2.at[a]
        got(r2.at[chunk(i)], base.b + a * NCHK + i)
        return s2[chunk(i), :].astype(f32) + r2[chunk(i), :].astype(f32)

    def my_rows(i):
        return rows(core * HF + i * RC, RC)

    def their_rows(i):
        return rows((1 - core) * HF + i * RC, RC)

    def share(ref, flow, i):
        if i == 0:
            relays[flow] = outgoing(ref.at[own_half])
        send(ref.at[my_rows(i)], ref.at[my_rows(i)], flow + i, to_core, None, relays[flow])

    def shared(ref, flow):
        for i in range(NCHK):
            got(ref.at[their_rows(i)], flow + i)

    relayed(wo)
    sum_begin(
        0,
        lambda off: jnp.dot(v.OB[rows(off, HF), :], v.WO[...], preferred_element_type=f32),
    )
    relay(wu, 1)
    relay(wd, 0)
    for i in range(NCHK):
        h_now = v.XB[my_rows(i), :].astype(f32) + sum_end(0, i)
        v.H[chunk(i), :] = h_now
        r = lax.rsqrt(jnp.mean(h_now * h_now, axis=-1, keepdims=True) + EPS)
        v.N2[my_rows(i), :] = (h_now * r * v.gain_two[...]).astype(bf16)
        share(v.N2, base.n2, i)
        if i == 1:
            relay(wd, 1)
    shared(v.N2, base.n2)

    relayed(wg)
    v.GB[...] = contract(v.N2[...], v.WG[...], (1, 1)).astype(bf16)
    relayed(wu)
    v.UB[...] = contract(v.N2[...], v.WU[...], (1, 1)).astype(bf16)

    def activate(i, _):
        at = rows(i * RC, RC)
        g, u = v.GB[at, :].astype(f32), v.UB[at, :].astype(f32)
        v.AB[at, :] = (g / (1.0 + jnp.exp(-g)) * u).astype(bf16)
        return 0

    lax.fori_loop(0, R // RC, activate, 0)
    YR = HF // YROWS
    s1, r1, s2, r2 = v.S1.at[1], v.R1.at[1], v.S2.at[1], v.R2.at[1]
    first, second, to_share = outgoing(s1), outgoing(s2), outgoing(v.DYB.at[own_half])

    def col_block(d):
        return pl.ds(hint(owner(d) * DF, 128), DF)

    def y_parts(d):
        return [(d * YROWS + k, k * YR) for k in range(YROWS)]

    def y_begin(d):
        cols = col_block(d)
        s1[:, cols] = jnp.dot(
            v.AB[rows((1 - core) * HF, HF), :], v.WD[:, cols], preferred_element_type=f32
        ).astype(bf16)
        for i, off in y_parts(d):
            at = s1.at[pl.ds(off, YR), cols]
            send(at, r1.at[pl.ds(off, YR), cols], base.ya + i, to_core, None, first)
        v.P32[:, cols] = jnp.dot(v.AB[own_half, :], v.WD[:, cols], preferred_element_type=f32)

    def y_pass(d):
        cols = col_block(d)
        for i, off in y_parts(d):
            part = pl.ds(off, YR)
            got(r1.at[part, cols], base.ya + i)
            s2[part, cols] = (v.P32[part, cols] + r1[part, cols].astype(f32)).astype(bf16)
            send(s2.at[part, cols], r2.at[part, cols], base.ys + i, to_y, None, second)

    wd[1].wait()
    y_begin(0)
    relayed(wd, False)
    for d in range(1, F):
        y_begin(d)
    for d in range(F):
        y_pass(d)
    te_copy.wait()
    up_copy.wait()
    squares, counted = jnp.zeros((1, 1), f32), jnp.zeros((1, 1), f32)
    for d in range(F):
        cols = col_block(d)
        for i, off in y_parts(d):
            part, mine = pl.ds(off, YR), rows(core * HF + off, YR)
            got(r2.at[part, cols], base.ys + i)
            y_now = v.H[part, cols] + s2[part, cols].astype(f32) + r2[part, cols].astype(f32)
            v.YB[mine, cols] = y_now.astype(bf16)
            weighting = v.VC[mine, pl.ds(0, 1)]
            differ = y_now - v.TE[part, cols].astype(f32)
            squares = squares + total_of(weighting * differ * differ)
            if d == 0:
                counted = counted + total_of(weighting)
            dy = v.UP[part, cols].astype(f32) + weighting * differ
            v.DY[part, cols] = dy
            v.DYB[mine, cols] = dy.astype(bf16)
            at = v.DYB.at[mine, cols]
            send(at, at, base.dy + i, to_core, None, to_share)
    tile_row = lax.broadcasted_iota(jnp.int32, (8, 128), 0)
    tile = jnp.where(
        tile_row == 0, jnp.broadcast_to(squares, (8, 128)), jnp.broadcast_to(counted, (8, 128))
    )
    v.LT[...] = tile
    v.LX[fs] = tile
    for d in range(1, F):
        send(v.LT, v.LX.at[fs], base.lx + d - 1, {"fsdp": owner(d)})
    y_half = v.YB.at[own_half]
    send(y_half, y_half, base.yb, to_core)
    grads_out = [outgoing(v.XS.at[owner(d)]) for d in range(1, F)]
    group_in, group_out = outgoing(v.XS.at[fs]), outgoing(v.GRAD, jnp.logical_not(is_outer))
    for d in range(F):
        for i, off in y_parts(d):
            got(v.DYB.at[rows((1 - core) * HF + off, YR), col_block(d)], base.dy + i)

    sent, own_done = [0], [0]

    def weight_grad(left, right, at, d, flipped=False):
        who = owner(d)
        tokens = left.shape[1 if flipped else 0]
        n = left.shape[0 if flipped else 1]
        if d == 0:
            own_done[0] = at + n
        rhs = right[pl.ds(0, tokens), pl.ds(hint(who * DF, 128), DF)]
        v.XS[who, pl.ds(at, n), :] = contract(left[...], rhs, (1 if flipped else 0, 0)).astype(bf16)

    def grad_index(d, j):
        return base.gx + (d - 1) * (NCH + 1) + j

    def grad_send(d, at, j):
        rcopy(
            v.XS.at[owner(d), at], v.XR.at[d - 1, at], grads_out[d - 1], grad_index(d, j),
            {"fsdp": owner(d)},
        ).start()

    def grads_ready(upto):
        first, last = sent[0], upto // CH
        sent[0] = last

        def body(j, _):
            for d in range(1, F):
                grad_send(d, rows(j * CH, CH), j)
            return 0

        if last > first:
            lax.fori_loop(first, last, body, 0)

    def inward(at, j):
        for d in range(1, F):
            got(v.XR.at[d - 1, at], grad_index(d, j))
        acc = v.XS[fs, at, :].astype(f32)
        for d in range(1, F):
            acc = acc + v.XR[d - 1, at, :].astype(f32)
        v.XS[fs, at, :] = acc.astype(bf16)

        @pl.when(jnp.logical_not(is_outer))
        def _():
            got(v.ZO.at[at], base.zo + j)
            v.XS[fs, at, :] = (acc + v.ZO[at, :].astype(f32)).astype(bf16)

        @pl.when(is_mid)
        def _():
            rcopy(v.XS.at[fs, at], v.ZI.at[at], group_in, base.zi + j, to_inner).start()

        @pl.when(jnp.logical_not(is_mid))
        def _():
            rcopy(v.XS.at[fs, at], v.ZO.at[at], group_in, base.zo + j, to_inner).start()

    def outward(at, j):
        got(v.ZI.at[at], base.zi + j)

        @pl.when(is_mid)
        def _():
            whole = v.XS[fs, at, :].astype(f32) + v.ZI[at, :].astype(f32)
            v.GRAD[at, :] = whole.astype(bf16)

        @pl.when(jnp.logical_not(is_mid))
        def _():
            v.GRAD[at, :] = v.ZI[at, :]

        @pl.when(jnp.logical_not(is_outer))
        def _():
            rcopy(v.GRAD.at[at], v.ZI.at[at], group_out, base.zi + j, to_outer).start()

        pltpu.make_async_copy(v.GRAD.at[at], v.grad_out.at[at], ls.at[10]).start()

    lag_in, lag_out = SKEW * hop, SKEW * (2 * half - 1 - hop)
    LAST = NCH + SKEW * (2 * half - 1)

    def pump(first, last):
        def body(i, _):
            ja, jb = i - lag_in, i - lag_out
            pl.when((ja >= 0) & (ja < NCH))(lambda: inward(rows(ja * CH, CH), ja))
            pl.when((jb >= 0) & (jb < NCH))(lambda: outward(rows(jb * CH, CH), jb))
            return 0

        if last > first:
            lax.fori_loop(first, last, body, 0)

    pumped = [0]

    def pump_to(place):
        last = LAST if place > 49 else place * NCH // 49
        ready = min(sent[0], own_done[0] // CH)
        last = min(last, ready if ready < NCH else LAST)
        if last > pumped[0]:
            pump(pumped[0], last)
            pumped[0] = last

    peers = range(1, F)
    for d in peers:
        weight_grad(v.AB, v.DYB, 0, d)
    grads_ready(FF)
    v.S[pl.ds(0, R), pl.ds(0, FF)] = contract(v.DYB[...], v.WD[...], (1, 1))

    def activate_back(i, _):
        at = rows(i * RC, RC)
        g, u, da = v.GB[at, :].astype(f32), v.UB[at, :].astype(f32), v.S[at, pl.ds(0, FF)]
        sig = 1.0 / (1.0 + jnp.exp(-g))
        v.DGB[at, :] = (da * u * (sig * (1.0 + g * (1.0 - sig)))).astype(bf16)
        v.DUB[at, :] = (da * (g * sig)).astype(bf16)
        return 0

    lax.fori_loop(0, R // RC, activate_back, 0)
    sum_begin(
        2,
        lambda off: jnp.dot(v.DGB[rows(off, HF), :], v.WG[...], preferred_element_type=f32)
        + jnp.dot(v.DUB[rows(off, HF), :], v.WU[...], preferred_element_type=f32),
    )
    weight_grad(v.AB, v.DYB, 0, 0)
    for d in peers:
        got(v.LX.at[owner(F - d)], base.lx + d - 1)
    send(v.LX, v.LC, base.lc, to_core)
    for d in peers:
        weight_grad(v.DGB, v.N2, FF, d)
    grads_ready(2 * FF)
    for d in peers:
        weight_grad(v.DUB, v.N2, 2 * FF, d)
    grads_ready(3 * FF)
    weight_grad(v.DGB, v.N2, FF, 0)
    weight_grad(v.DUB, v.N2, 2 * FF, 0)
    pump_to(2)
    v.GT[0] = jnp.zeros((8, D), f32)
    for i in range(NCHK):
        dn2 = sum_end(2, i)
        h_now = v.H[chunk(i), :]
        r = lax.rsqrt(jnp.mean(h_now * h_now, axis=-1, keepdims=True) + EPS)
        gd = v.gain_two[...] * dn2
        dh = v.DY[chunk(i), :] + r * gd - h_now * (
            r * r * r * jnp.mean(gd * h_now, axis=-1, keepdims=True)
        )
        v.DH[chunk(i), :] = dh
        v.DHB[my_rows(i), :] = dh.astype(bf16)
        share(v.DHB, base.dh, i)
        part = jnp.sum(dn2 * h_now * r, axis=0, keepdims=True)
        part = jnp.where(yy == i // (NCHK // 2), part, 0.0)
        v.GT[0, pl.ds(0, 1), :] = v.GT[0, pl.ds(0, 1), :] + part
        pump_to(3 + i)
    shared(v.DHB, base.dh)
    got(v.LC, base.lc)
    v.LB[z] = v.LX[...] + v.LC[...]
    for k in range(1, C):
        send(v.LB.at[z], v.LB.at[z], base.ll + k - 1, {"ctx": lax.rem(z + k, C)})

    by_heads(v.DOH, contract(v.DHB[...], v.WO[...], (1, 1)))
    pump_to(7)
    for h in range(H):
        v.S[pl.ds(h * R, R), :] = contract(v.DOH[pl.ds(h * R, R), :], v.VB[...], (1, 1))
    for d in peers:
        weight_grad(v.OB, v.DHB, 3 * FF, d)
    grads_ready(3 * FF + HC)
    weight_grad(v.OB, v.DHB, 3 * FF, 0)
    pump_to(8)

    def soft_back(i, _):
        dp, at, _, low = merged(i)
        prob = v.PM[at, :]
        spread(v.DSB, at, low, prob * (dp - jnp.sum(prob * dp, axis=-1, keepdims=True)))
        return 0

    lax.fori_loop(0, H * R // AR, soft_back, 0)
    pump_to(9)
    scale = HEAD_DIM**-0.5
    v.DVT[...] = contract(v.DOH[...], v.PB[...], (0, 0)).astype(bf16)
    v.DKT[...] = (contract(v.QH[...], v.DSB[...], (0, 0)) * scale).astype(bf16)
    v.DQ[...] = (from_heads(v.DSB, v.KB) * scale).astype(bf16)
    pump_to(11)

    def dn1_product(j, which):
        at = pl.ds(hint(j * R + which * HF, 128), HF)
        out = contract(v.DKT[:, at], v.WQKV[:, pl.ds(HC, HC)], (0, 1))
        out = out + contract(v.DVT[:, at], v.WQKV[:, pl.ds(2 * HC, HC)], (0, 1))
        if j == 0:
            out = out + contract(v.DQ[rows(which * HF, HF), :], v.WQKV[:, pl.ds(0, HC)], (1, 1))
        return out

    for j in range(W, -1, -1):
        v.D1S[j] = dn1_product(j, 1 - core).astype(bf16)
        send(v.D1S.at[j], v.D1R.at[j], base.d1 + j, to_core)
        v.D1O[j] = dn1_product(j, core)
    for d in list(peers) + [0]:
        at = 3 * FF + HC
        weight_grad(v.DQ, v.N1, at, d)
        weight_grad(v.DKT, v.N1, at + HC, d, True)
        weight_grad(v.DVT, v.N1, at + 2 * HC, d, True)
        if d == F - 1:
            grads_ready(N)
    pump_to(13)
    for j in range(W, -1, -1):
        got(v.D1R.at[j], base.d1 + j)
        there = rows((1 - yy) * Q, Q)
        v.D2S[j] = (v.D1O[j, there, :] + v.D1R[j, there, :].astype(f32)).astype(bf16)
        send(v.D2S.at[j], v.D2R.at[j], base.d2 + j, to_y)
    pump_to(16)
    here = rows(yy * Q, Q)
    for j in range(W, 0, -1):
        got(v.D2R.at[j], base.d2 + j)
        own = v.D1O[j, here, :] + v.D1R[j, here, :].astype(f32) + v.D2R[j].astype(f32)
        v.DZS[j] = own.astype(bf16)
        if j < W:
            @pl.when(has_next & (z >= j))
            def _(j=j, own=own):
                got(v.DZR.at[j + 1], base.dz + j + 1)
                v.DZS[j] = (own + v.DZR[j + 1].astype(f32)).astype(bf16)
        send(v.DZS.at[j], v.DZR.at[j], base.dz + j, to_prev, z >= j)
        pump_to(19 + 2 * (W - j))

    pump_to(23)
    pump_to(26)
    got(v.D2R.at[0], base.d2)
    v.P32[pl.ds(0, Q), :] = (
        v.D1O[0, here, :] + v.D1R[0, here, :].astype(f32) + v.D2R[0].astype(f32)
    )

    @pl.when(has_next)
    def _():
        got(v.DZR.at[1], base.dz + 1)
        v.P32[pl.ds(0, Q), :] = v.P32[pl.ds(0, Q), :] + v.DZR[1].astype(f32)

    quarter = rows(core * HF + yy * Q, Q)
    dn1 = v.P32[pl.ds(0, Q), :]
    x_now = v.XB[quarter, :].astype(f32)
    r = lax.rsqrt(jnp.mean(x_now * x_now, axis=-1, keepdims=True) + EPS)
    gd = v.gain_one[...] * dn1
    gi = v.DH[here, :] + r * gd - x_now * (
        r * r * r * jnp.mean(gd * x_now, axis=-1, keepdims=True)
    )
    v.GIB[quarter, :] = gi.astype(bf16)
    mine = v.GIB.at[quarter]
    send(mine, mine, base.i1, to_y)
    send(mine, mine, base.i2, to_core)
    v.GT[0, pl.ds(1, 1), :] = jnp.sum(dn1 * x_now * r, axis=0, keepdims=True)
    send(v.GT.at[0], v.GR.at[0], base.g1, to_core)
    pump_to(28)
    got(v.GR.at[0], base.g1)
    v.GT[1] = v.GT[0] + v.GR[0]
    send(v.GT.at[1], v.GR.at[1], base.g2, to_y)
    from_y = v.GIB.at[rows(core * HF + (1 - yy) * Q, Q)]
    got(from_y, base.i1)
    send(from_y, from_y, base.i3, to_core)
    pump_to(32)
    got(v.GR.at[1], base.g2)
    v.GT[2] = v.GT[1] + v.GR[1]
    for d in list(peers) + [0]:
        tile = v.GT[2, :, pl.ds(hint(owner(d) * DF, 128), DF)]
        v.XS[owner(d), pl.ds(N, 16), :] = jnp.concatenate([tile, jnp.zeros_like(tile)], 0).astype(bf16)
        if d:
            grad_send(d, pl.ds(N, 16), NCH)

    pump_to(49)
    gain_rows = pl.ds(N, 16)
    inward(gain_rows, NCH)
    for k in range(1, C):
        got(v.LB.at[lax.rem(z + C - k, C)], base.ll + k - 1)
    sums = [sum(v.LB[c, s] for c in range(C)) for s in range(F)]
    counted = sum(s[1:2, :] for s in sums)
    for s in range(F):
        v.LOSS[pl.ds(s, 1), :] = sums[s][0:1, :] * F / (counted * D)
    got(v.YB.at[rows((1 - core) * HF, HF)], base.yb)
    got(v.GIB.at[rows((1 - core) * HF + yy * Q, Q)], base.i2)
    got(v.GIB.at[rows((1 - core) * HF + (1 - yy) * Q, Q)], base.i3)
    results = (
        pltpu.make_async_copy(v.YB, v.y_out, ls.at[0]),
        pltpu.make_async_copy(v.GIB, v.gi_out, ls.at[1]),
        pltpu.make_async_copy(v.LOSS, v.loss_out, ls.at[2]),
    )
    for cp in results:
        cp.start()

    streams = grads_out + [group_in, group_out]

    def all_left(k):
        src, cond = unsent[k]

        def left():
            rcopy(src, src, k, 0, to_core).wait_send()

        if cond is None:
            left()
        else:
            pl.when(cond)(left)

    for k in range(len(unsent)):
        if k not in streams:
            all_left(k)
    pump_to(50)
    outward(gain_rows, NCH)
    for k in streams:
        all_left(k)
    for cp in results:
        cp.wait()
    pltpu.make_async_copy(v.GRAD, v.grad_out, ls.at[10]).wait()


def finish_kernel(p, grad, gib, yb, loss, *refs):
    (y_out, loss_out, gi_out, one, gq, gk, gv, go, two, gg, gu, gd) = refs[:12]
    g_buf, i_buf, y_buf, l_buf, g_wide, i_wide, q_wide, sem_in, sem_out = refs[12:]
    FF, HC, N = p.FF, p.HC, p.N
    at = 3 * FF
    plain, flip = [], []
    for ref, first in ((gd, 0), (gg, FF), (gu, 2 * FF)):
        plain += [(ref, first, 0, FF // 2), (ref, first + FF // 2, FF // 2, FF // 2)]
    plain.append((go, at, 0, HC))
    flip = [(gq, at + HC), (gk, at + 2 * HC), (gv, at + 3 * HC)]
    loads = []

    def load(src, dst):
        cp = pltpu.make_async_copy(src, dst, sem_in.at[len(loads)])
        cp.start()
        loads.append(cp)
        return cp

    stores = []

    def store(src, dst):
        cp = pltpu.make_async_copy(src, dst, sem_out.at[len(stores)])
        cp.start()
        stores.append(cp)

    plain_in = [load(grad.at[pl.ds(f, n)], g_buf.at[pl.ds(f, n)]) for _, f, _, n in plain]
    flip_in = [load(grad.at[pl.ds(f, HC)], g_buf.at[pl.ds(f, HC)]) for _, f in flip]
    gi_in = load(gib, i_buf)
    y_in = load(yb, y_buf)
    gain_in = load(grad.at[pl.ds(N, 16)], g_buf.at[pl.ds(N, 16)])
    loss_in = load(loss, l_buf)
    for (ref, first, row, n), cp in zip(plain, plain_in):
        cp.wait()
        g_wide[pl.ds(first, n), :] = g_buf[pl.ds(first, n), :].astype(f32)
        store(g_wide.at[pl.ds(first, n)], ref.at[pl.ds(row, n)])
    for k, ((ref, first), cp) in enumerate(zip(flip, flip_in)):
        cp.wait()
        for c in range(0, HC, 128):
            w = min(128, HC - c)
            q_wide[k, :, pl.ds(c, w)] = g_buf[pl.ds(first + c, w), :].astype(f32).T
        store(q_wide.at[k], ref)
    gi_in.wait()
    i_wide[...] = i_buf[...].astype(f32)
    store(i_wide, gi_out.at[0])
    y_in.wait()
    store(y_buf, y_out.at[0])
    gain_in.wait()
    gains = g_buf[pl.ds(N, 16), :].astype(f32)
    two[...] = gains[0:1, :]
    one[...] = gains[1:2, :]
    loss_in.wait()
    for s in range(p.F):
        loss_out[s] = jnp.max(l_buf[pl.ds(s, 1), :])
    for cp in stores:
        cp.wait()


def shards(mesh_shape, seq_len, *args):
    (inputs, upstream, teacher, valid, segment, gain_one, wq, wk, wv, wo, gain_two, wg, wu, wd) = args
    _, rows_here, width = inputs.shape
    p = Plan(
        mesh_shape["fsdp"], mesh_shape["ctx"], rows_here, width, wq.shape[1], wg.shape[1], seq_len
    )
    R, D, DF, HC, FF, F = p.R, p.D, p.DF, p.HC, p.FF, p.F
    NG = p.N + 16
    scratch = scratch_of(p)
    vmem = pl.BlockSpec(memory_space=pltpu.VMEM)
    anywhere = pl.BlockSpec(memory_space=pl.ANY)
    in_specs = [anywhere] * 3 + [vmem] * 3 + [anywhere] * 4 + [vmem] + [anywhere] * 3
    sds = jax.ShapeDtypeStruct
    grad, gib, yb, loss = pl.pallas_call(
        functools.partial(layer_kernel, p, tuple(scratch)),
        out_shape=(
            sds((NG, DF), bf16), sds((R, D), bf16), sds((R, D), bf16), sds((max(F, 8), 128), f32),
        ),
        in_specs=in_specs,
        out_specs=(anywhere,) * 4,
        scratch_shapes=[pltpu.VMEM(s, dt) for s, dt in scratch.values()]
        + [
            pltpu.SemaphoreType.DMA((p.sends,)), pltpu.SemaphoreType.DMA((p.total,)),
            pltpu.SemaphoreType.DMA((11,)),
        ],
        compiler_params=pltpu.CompilerParams(
            collective_id=0, has_side_effects=True, vmem_limit_bytes=67043328
        ),
        name="layer",
    )(
        inputs.reshape(R, D), upstream.reshape(R, D), teacher.reshape(R, D), valid, segment,
        gain_one.reshape(1, D), wq, wk, wv, wo, gain_two.reshape(1, D), wg.T, wu.T, wd,
    )
    outs = pl.pallas_call(
        functools.partial(finish_kernel, p),
        out_shape=(
            sds((1, R, D), bf16), sds((F,), f32), sds((1, R, D), f32), sds((1, DF), f32),
            sds((DF, HC), f32), sds((DF, HC), f32), sds((DF, HC), f32), sds((HC, DF), f32),
            sds((1, DF), f32), sds((FF, DF), f32), sds((FF, DF), f32), sds((FF, DF), f32),
        ),
        in_specs=[anywhere] * 4,
        out_specs=(anywhere, pl.BlockSpec(memory_space=pltpu.SMEM), anywhere, vmem)
        + (anywhere,) * 4 + (vmem,) + (anywhere,) * 3,
        scratch_shapes=[
            pltpu.VMEM((NG, DF), bf16), pltpu.VMEM((R, D), bf16), pltpu.VMEM((R, D), bf16),
            pltpu.VMEM((max(F, 8), 128), f32), pltpu.VMEM((3 * FF + HC, DF), f32),
            pltpu.VMEM((R, D), f32), pltpu.VMEM((3, DF, HC), f32),
            pltpu.SemaphoreType.DMA((14,)), pltpu.SemaphoreType.DMA((12,)),
        ],
        compiler_params=pltpu.CompilerParams(vmem_limit_bytes=67043328),
        name="finish",
    )(grad, gib, yb, loss)
    outs = list(outs)
    outs[3], outs[8] = outs[3].reshape(DF), outs[8].reshape(DF)
    outs[9], outs[10] = outs[9].T, outs[10].T
    return tuple(outs)


def solution(mesh):
    def run(*args):
        token, row, col = P("fsdp", "ctx", None), P("fsdp", "tp"), P("tp", "fsdp")
        pair = P("fsdp", "ctx")
        return jax.shard_map(
            functools.partial(shards, dict(mesh.shape), args[0].shape[1]),
            mesh=mesh,
            in_specs=(token, token, token, pair, pair, P(), row, row, row, col, P(), row, row, col),
            out_specs=(
                token, P(), token, P("fsdp"), row, row, row, col, P("fsdp"), row, row, col,
            ),
            check_vma=False,
        )(*args)

    return run
```

```python
import functools
from types import SimpleNamespace

import jax
import jax.numpy as jnp
from jax import lax
from jax.experimental import pallas as pl
from jax.experimental.pallas import tpu as pltpu
from jax.sharding import PartitionSpec as P

HEAD_DIM = 64
EPS = 1e-05
MESH = pl.DeviceIdType.MESH
NCHK = 4
YROWS = 2
SKEW = 2
f32, bf16 = jnp.float32, jnp.bfloat16


class Plan:
    def __init__(self, fsdp, ctx, rows, width, head_cols, hidden, seq_len):
        self.F, self.C, self.R, self.D = fsdp, ctx, rows, width
        self.HC, self.FF = head_cols, hidden
        self.DF = width // fsdp
        self.W = -(-(seq_len // 2) // rows)
        self.N = 3 * hidden + 4 * head_cols
        self.CH = next(
            k for k in range(16, self.N + 1, 16) if self.N % k == 0 and k * self.DF >= 57344
        )
        self.NCH = self.N // self.CH
        self.NB = self.NCH - max(1, 224 // self.CH)
        rest = self.N + 16 - self.NB * self.CH
        self.CS = next(k for k in (48, 64, 80, 32, 16) if rest % k == 0)
        self.NK = self.NB + rest // self.CS
        self.base, self.total = SimpleNamespace(), 0
        peers = fsdp - 1
        for name, count in dict(
            ya=YROWS * fsdp, ys=YROWS * fsdp, xz=2 * self.W, sg=self.W, xy=2 * self.W, xc=self.W, wd=11 * peers, wr=11 * peers,
            a=3 * NCHK, b=3 * NCHK, n2=NCHK, yb=1, dy=YROWS * fsdp, dh=NCHK,
            lc=1, ll=ctx - 1, lx=peers, d1=self.W + 1, d2=self.W + 1, dz=self.W + 1,
            g1=1, g2=1, i1=1, i2=1, i3=1, gx=peers * self.NK, zo=self.NK, zi=self.NK,
        ).items():
            setattr(self.base, name, self.total)
            self.total += count
        self.sends = 4 * self.W + 2 + 14 * peers + 9 + 3 + 2 * ctx + peers + 3 * self.W + 2 + 5 + peers + 2


def contract(left, right, dims):
    return lax.dot_general(left, right, ((dims[:1], dims[1:]), ((), ())), preferred_element_type=f32)


def total_of(v):
    return jnp.sum(jnp.sum(v, axis=1, keepdims=True), axis=0, keepdims=True)


def scratch_of(p):
    R, D, HC, FF, DF, F, C, W = p.R, p.D, p.HC, p.FF, p.DF, p.F, p.C, p.W
    HF, Q, KR, H = R // 2, R // 4, (p.W + 1) * p.R, p.HC // HEAD_DIM
    NG = p.N + 16
    return dict(
        XB=((KR, D), bf16), SG=((W + 1, 1, R), jnp.int32), N1=((KR, D), bf16),
        WQKV=((D, 3 * HC), bf16), WO=((HC, D), bf16), WG=((FF, D), bf16),
        WU=((FF, D), bf16), WD=((FF, D), bf16),
        QH=((H * R, HC), bf16), KB=((KR, HC), bf16), VB=((KR, HC), bf16), DOH=((H * R, HC), bf16),
        PM=((H * R, W * R), f32), S=((H * R, KR), f32), PB=((H * R, KR), bf16), DSB=((H * R, KR), bf16),
        BIAS=((R, W * R), f32), DQ=((R, HC), bf16), DKT=((HC, KR), bf16), DVT=((HC, KR), bf16),
        OB=((R, HC), bf16), VC=((R, 128), f32),
        H=((HF, D), f32), DY=((HF, D), f32), DH=((HF, D), f32), P32=((HF, D), f32),
        UP=((HF, D), bf16), TE=((HF, D), bf16),
        N2=((R, D), bf16), DYB=((R, D), bf16), DHB=((R, D), bf16),
        GB=((R, FF), bf16), UB=((R, FF), bf16), AB=((R, FF), bf16),
        DGB=((R, FF), bf16), DUB=((R, FF), bf16),
        D1S=((W + 1, HF, D), bf16), D1R=((W + 1, HF, D), bf16), D1O=((W + 1, HF, D), f32),
        D2S=((W + 1, Q, D), bf16), D2R=((W + 1, Q, D), bf16), DZR=((W + 1, Q, D), bf16),
        DZS=((W + 1, Q, D), bf16),
        GT=((3, 8, D), f32), GR=((2, 8, D), f32),
        LT=((8, 128), f32), LX=((F, 8, 128), f32), LC=((F, 8, 128), f32), LB=((C, F, 8, 128), f32),
        XS=((F, NG, DF), bf16), XR=((F - 1, NG, DF), bf16),
        ZO=((NG, DF), bf16), ZI=((NG, DF), bf16), GRAD=((NG, DF), bf16), GIB=((R, D), bf16),
        YB=((R, D), bf16), LOSS=((max(F, 8), 128), f32),
        S1=((3, HF, D), bf16), R1=((3, HF, D), bf16), S2=((3, HF, D), bf16), R2=((3, HF, D), bf16),
    )


def layer_kernel(p, names, *refs):
    v = SimpleNamespace(**dict(zip(names, refs[18:], strict=False)))
    (
        v.x, v.upstream, v.teacher, v.valid, v.segment, v.gain_one, v.wq, v.wk, v.wv, v.wo,
        v.gain_two, v.wg, v.wu, v.wd, v.grad_out, v.gi_out, v.y_out, v.loss_out,
    ) = refs[:18]
    ss, rs, ls = refs[-3:]
    R, D, HC, FF, DF, F, C, W, N, CH, NCH, CS, NB, NK = (
        p.R, p.D, p.HC, p.FF, p.DF, p.F, p.C, p.W, p.N, p.CH, p.NCH, p.CS, p.NB, p.NK
    )
    HF, Q, KR, H = R // 2, R // 4, (W + 1) * R, HC // HEAD_DIM
    RC = HF // NCHK
    base = p.base
    fs, z, t = lax.axis_index("fsdp"), lax.axis_index("ctx"), lax.axis_index("tp")
    core, yy, par = lax.rem(t, 2), t // 2, lax.rem(z, 2)
    to_core, to_y = {"tp": t + 1 - 2 * core}, {"tp": lax.rem(t + 2, 4)}
    to_next, to_prev = {"ctx": lax.rem(z + 1, C)}, {"ctx": lax.rem(z + C - 1, C)}
    to_pair = {"ctx": z + 1 - 2 * par}
    has_next, has_prev = z < C - 1, z > 0
    half = C // 2
    left_side = z < half
    hop = jnp.where(left_side, z, C - 1 - z)
    step_in = jnp.where(left_side, 1, -1)
    to_inner = {"ctx": z + step_in}
    to_outer = {"ctx": lax.rem(z - step_in + C, C)}
    is_outer, is_mid = hop == 0, hop == half - 1

    def owner(d):
        return lax.rem(fs + d, F)

    def rcopy(src, dst, sk, rk, dev):
        return pltpu.make_async_remote_copy(
            src_ref=src, dst_ref=dst, send_sem=ss.at[sk], recv_sem=rs.at[rk],
            device_id=dev, device_id_type=MESH,
        )

    unsent = []

    def outgoing(src, cond=None):
        unsent.append((src, cond))
        assert len(unsent) <= p.sends
        return len(unsent) - 1

    def send(src, dst, k, dev, cond=None, group=None):
        sk = outgoing(src, cond) if group is None else group
        if cond is None:
            rcopy(src, dst, sk, k, dev).start()
        else:
            pl.when(cond)(lambda: rcopy(src, dst, sk, k, dev).start())

    def got(dst, k):
        rcopy(dst, dst, 0, k, to_core).wait_recv()

    def hint(i, m):
        return pl.multiple_of(i, m)

    def rows(off, n, m=16):
        return pl.ds(hint(off, m), n)

    barrier = pltpu.get_barrier_semaphore()

    def greet(dev):
        pl.semaphore_signal(barrier, inc=1, device_id=dev, device_id_type=MESH)

    greet(to_core)
    greet(to_y)
    for d in range(1, F):
        greet({"fsdp": owner(d)})
    for k in range(1, C):
        greet({"ctx": lax.rem(z + k, C)})

    local = []

    def fetch(src, dst):
        cp = pltpu.make_async_copy(src, dst, ls.at[len(local)])
        cp.start()
        local.append(cp)
        return cp

    own_half = rows(core * HF, HF)
    x_copy = fetch(v.x, v.XB.at[pl.ds(0, R)])
    own_cols = pl.ds(hint(fs * DF, 128), DF)

    def by_row(dst, col0, cols):
        def region(who, off, n):
            return dst.at[rows(who * DF + off, n), pl.ds(col0, cols)]
        return region

    def by_col(dst):
        def region(who, off, n):
            return dst.at[rows(off, n), pl.ds(hint(who * DF, 128), DF)]
        return region

    weights = (
        (v.wq, by_row(v.WQKV, 0, HC), 1), (v.wk, by_row(v.WQKV, HC, HC), 1),
        (v.wv, by_row(v.WQKV, 2 * HC, HC), 1), (v.wo, by_col(v.WO), 1),
        (v.wg, by_col(v.WG), 2), (v.wu, by_col(v.WU), 2), (v.wd, by_col(v.WD), 3),
    )
    gathers = []
    count = 0
    for source, region, parts in weights:
        tall = source.shape[0]
        cuts = [0, tall // 2] if parts == 1 else [0, tall // 4, tall // 2]
        if parts == 3:
            cuts.insert(2, tall // 3 // 16 * 16)
        gathers.append((
            source, fetch(source, region(fs, 0, tall)),
            [
                (region, cuts[min(parts, 2)], tall // 2, cuts[k], cuts[k + 1] - cuts[k], count + k)
                for k in range(parts)
            ],
        ))
        count += parts
    wq, wk, wv, wo, wg, wu, wd = gathers
    te_copy = fetch(v.teacher.at[own_half], v.TE)
    up_copy = fetch(v.upstream.at[own_half], v.UP)

    pl.semaphore_wait(barrier, F + C)

    def piece_index(kind, number, d):
        return kind + number * (F - 1) + d - 1

    for source, _, pieces in gathers:
        tall = source.shape[0] // 2
        for d in range(1, F):
            group = outgoing(source.at[rows(par * tall, tall)])
            for region, passed, _, at, n, number in pieces:
                off = par * tall + at
                send(
                    source.at[rows(off, n)], region(fs, off, n), piece_index(base.wd, number, d),
                    {"fsdp": owner(d)}, None, group,
                )
                if at >= passed:
                    off = (1 - par) * tall + at
                    send(
                        source.at[rows(off, n)], region(fs, off, n),
                        piece_index(base.wr, number, d), {"fsdp": owner(d)},
                    )

    relays = {}

    def relay(weight, which):
        region, passed, tall, at, n, number = weight[2][which]
        for d in range(1, F):
            if which == 0:
                relays[number, d] = outgoing(region(owner(F - d), par * tall, passed))
            part = region(owner(F - d), par * tall + at, n)
            got(part, piece_index(base.wd, number, d))
            send(
                part, part, piece_index(base.wr, number, d), to_pair, None, relays[number - which, d]
            )

    def relayed(weight, with_own=True):
        if with_own:
            weight[1].wait()
        for region, passed, tall, at, n, number in weight[2]:
            for d in range(1, F):
                if at >= passed:
                    got(region(owner(F - d), par * tall + at, n), piece_index(base.wd, number, d))
                got(region(owner(F - d), (1 - par) * tall + at, n), piece_index(base.wr, number, d))

    def x_half(j, which):
        return v.XB.at[rows(j * R + which * HF, HF)]

    def x_eighth(j, y, k):
        return v.XB.at[rows(j * R + core * HF + y * Q + k * (Q // 2), Q // 2)]

    def x_quarter(j, y):
        return v.XB.at[rows(j * R + core * HF + y * Q, Q)]

    x_group = outgoing(x_quarter(0, yy), has_next)
    for k in range(2):
        send(
            v.x.at[rows(core * HF + yy * Q + k * (Q // 2), Q // 2)], x_eighth(1, yy, k), base.xz + k,
            to_next, has_next, x_group,
        )
    v.SG[0] = v.segment[...]
    send(v.segment, v.SG.at[1], base.sg, to_next, has_next)
    for j in range(1, W + 1):
        @pl.when(z < j)
        def _(j=j):
            v.XB[pl.ds(j * R, R), :] = jnp.zeros((R, D), bf16)
            v.SG[j] = jnp.full((1, R), -1, jnp.int32)

    def x_pass(j):
        both = (z >= j) & has_next
        onward = outgoing(x_quarter(j, yy), both) if j < W else None
        across = outgoing(x_quarter(j, yy), z >= j)
        for k in range(2):
            part = x_eighth(j, yy, k)
            pl.when(z >= j)(lambda part=part, k=k: got(part, base.xz + 2 * (j - 1) + k))
            if j < W:
                send(part, x_eighth(j + 1, yy, k), base.xz + 2 * j + k, to_next, both, onward)
            send(part, part, base.xy + 2 * (j - 1) + k, to_y, z >= j, across)
        pl.when(z >= j)(lambda: got(v.SG.at[j], base.sg + j - 1))
        if j < W:
            send(v.SG.at[j], v.SG.at[j + 1], base.sg + j, to_next, both)

    def x_join(j):
        for k in range(2):
            pl.when(z >= j)(
                lambda k=k: got(x_eighth(j, 1 - yy, k), base.xy + 2 * (j - 1) + k)
            )
        send(x_half(j, core), x_half(j, core), base.xc + j - 1, to_core, z >= j)

    def x_done(j):
        pl.when(z >= j)(lambda: got(x_half(j, 1 - core), base.xc + j - 1))

    def norm_rows(j):
        def body(i, _):
            at = rows(j * R + i * RC, RC)
            xs = v.XB[at, :].astype(f32)
            r = lax.rsqrt(jnp.mean(xs * xs, axis=-1, keepdims=True) + EPS)
            v.N1[at, :] = (xs * r * v.gain_one[...]).astype(bf16)
            return 0
        lax.fori_loop(0, R // RC, body, 0)

    eye = lax.broadcasted_iota(jnp.int32, (R, R), 0) == lax.broadcasted_iota(jnp.int32, (R, R), 1)
    lower = lax.broadcasted_iota(jnp.int32, (R, R), 1) <= lax.broadcasted_iota(jnp.int32, (R, R), 0)

    def column(row):
        return jnp.sum(jnp.where(eye, row.astype(f32), 0.0), axis=1, keepdims=True)

    x_copy.wait()
    norm_rows(0)
    v.VC[...] = jnp.broadcast_to(column(v.valid[...]), (R, 128))
    x_pass(1)
    relay(wq, 0)
    relay(wk, 0)
    relay(wv, 0)
    for j in range(1, W + 1):
        if j < W:
            x_pass(j + 1)
        x_join(j)
        if j == 1:
            relay(wo, 0)
        if j == W:
            relay(wg, 0)
        x_done(j)
        norm_rows(j)
    seg_col = column(v.SG[0])
    for j in range(W):
        seg_row = jnp.broadcast_to(v.SG[j].astype(f32), (R, R))
        if j == 0:
            seg_row = jnp.where(lower, seg_row, v.SG[W].astype(f32))
        v.BIAS[:, pl.ds(j * R, R)] = jnp.where(seg_col == seg_row, 0.0, -1e30)
    relayed(wq)
    lane_head = lax.broadcasted_iota(jnp.int32, (R, HC), 1) // HEAD_DIM

    def by_heads(ref, val):
        for h in range(H):
            ref[pl.ds(h * R, R), :] = jnp.where(lane_head == h, val, 0.0).astype(bf16)

    def from_heads(ref, other):
        mix = jnp.zeros((R, HC), f32)
        for h in range(H):
            part = jnp.dot(ref[pl.ds(h * R, R), :], other[...], preferred_element_type=f32)
            mix = jnp.where(lane_head == h, part, mix)
        return mix

    by_heads(
        v.QH,
        jnp.dot(v.N1[pl.ds(0, R), :], v.WQKV[:, pl.ds(0, HC)], preferred_element_type=f32),
    )
    relayed(wk)
    relayed(wv)
    for dst, col in ((v.KB, HC), (v.VB, 2 * HC)):
        dst[...] = jnp.dot(
            v.N1[...], v.WQKV[:, pl.ds(col, HC)], preferred_element_type=f32
        ).astype(bf16)
    relay(wg, 1)

    AR = 64 if R % 64 == 0 else R // 4
    WR = W * R

    def merged(i):
        at, inner = rows(i * AR, AR), rows(lax.rem(i, R // AR) * AR, AR)
        place = lax.broadcasted_iota(jnp.int32, (AR, R), 0) + lax.rem(i, R // AR) * AR
        low = lax.broadcasted_iota(jnp.int32, (AR, R), 1) <= place
        first = jnp.where(low, v.S[at, pl.ds(0, R)], v.S[at, pl.ds(WR, R)])
        if W > 1:
            first = jnp.concatenate([first, v.S[at, pl.ds(R, WR - R)]], axis=1)
        return first, at, inner, low

    def spread(ref, at, low, val):
        own = val[:, :R]
        ref[at, pl.ds(0, R)] = jnp.where(low, own, 0.0).astype(bf16)
        ref[at, pl.ds(WR, R)] = jnp.where(low, 0.0, own).astype(bf16)
        if W > 1:
            ref[at, pl.ds(R, WR - R)] = val[:, R:].astype(bf16)

    def soft(i, _):
        s, at, inner, low = merged(i)
        s = s * (HEAD_DIM**-0.5) + v.BIAS[inner, :]
        e = jnp.exp(s - jnp.max(s, axis=-1, keepdims=True))
        prob = e * (1.0 / jnp.sum(e, axis=-1, keepdims=True))
        v.PM[at, :] = prob
        spread(v.PB, at, low, prob)
        return 0

    for h in range(H):
        v.S[pl.ds(h * R, R), :] = contract(v.QH[pl.ds(h * R, R), :], v.KB[...], (1, 1))
    lax.fori_loop(0, H * R // AR, soft, 0)
    relay(wu, 0)
    v.OB[...] = from_heads(v.PB, v.VB).astype(bf16)

    def chunk(i):
        return pl.ds(i * RC, RC)

    def sum_begin(a, product):
        s1, r1, s2, r2 = v.S1.at[a], v.R1.at[a], v.S2.at[a], v.R2.at[a]
        s1[...] = product((1 - core) * HF).astype(bf16)
        first, second = outgoing(s1), outgoing(s2)
        for i in range(NCHK):
            send(s1.at[chunk(i)], r1.at[chunk(i)], base.a + a * NCHK + i, to_core, None, first)
        v.P32[...] = product(core * HF)
        for i in range(NCHK):
            got(r1.at[chunk(i)], base.a + a * NCHK + i)
            s2[chunk(i), :] = (v.P32[chunk(i), :] + r1[chunk(i), :].astype(f32)).astype(bf16)
            send(s2.at[chunk(i)], r2.at[chunk(i)], base.b + a * NCHK + i, to_y, None, second)

    def sum_end(a, i):
        s2, r2 = v.S2.at[a], v.R2.at[a]
        got(r2.at[chunk(i)], base.b + a * NCHK + i)
        return s2[chunk(i), :].astype(f32) + r2[chunk(i), :].astype(f32)

    def my_rows(i):
        return rows(core * HF + i * RC, RC)

    def their_rows(i):
        return rows((1 - core) * HF + i * RC, RC)

    def share(ref, flow, i):
        if i == 0:
            relays[flow] = outgoing(ref.at[own_half])
        send(ref.at[my_rows(i)], ref.at[my_rows(i)], flow + i, to_core, None, relays[flow])

    def shared(ref, flow):
        for i in range(NCHK):
            got(ref.at[their_rows(i)], flow + i)

    relayed(wo)
    sum_begin(
        0,
        lambda off: jnp.dot(v.OB[rows(off, HF), :], v.WO[...], preferred_element_type=f32),
    )
    relay(wu, 1)
    relay(wd, 0)
    for i in range(NCHK):
        h_now = v.XB[my_rows(i), :].astype(f32) + sum_end(0, i)
        v.H[chunk(i), :] = h_now
        r = lax.rsqrt(jnp.mean(h_now * h_now, axis=-1, keepdims=True) + EPS)
        v.N2[my_rows(i), :] = (h_now * r * v.gain_two[...]).astype(bf16)
        share(v.N2, base.n2, i)
        if i == 1:
            relay(wd, 1)
    shared(v.N2, base.n2)

    relayed(wg)
    v.GB[...] = contract(v.N2[...], v.WG[...], (1, 1)).astype(bf16)
    relayed(wu)
    v.UB[...] = contract(v.N2[...], v.WU[...], (1, 1)).astype(bf16)

    def activate(i, _):
        at = rows(i * RC, RC)
        g, u = v.GB[at, :].astype(f32), v.UB[at, :].astype(f32)
        v.AB[at, :] = (g / (1.0 + jnp.exp(-g)) * u).astype(bf16)
        return 0

    lax.fori_loop(0, R // RC, activate, 0)
    YR = HF // YROWS
    s1, r1, s2, r2 = v.S1.at[1], v.R1.at[1], v.S2.at[1], v.R2.at[1]
    first, second, to_share = outgoing(s1), outgoing(s2), outgoing(v.DYB.at[own_half])

    def col_block(d):
        return pl.ds(hint(owner(d) * DF, 128), DF)

    def y_parts(d):
        return [(d * YROWS + k, k * YR) for k in range(YROWS)]

    def y_begin(d):
        cols = col_block(d)
        s1[:, cols] = jnp.dot(
            v.AB[rows((1 - core) * HF, HF), :], v.WD[:, cols], preferred_element_type=f32
        ).astype(bf16)
        for i, off in y_parts(d):
            at = s1.at[pl.ds(off, YR), cols]
            send(at, r1.at[pl.ds(off, YR), cols], base.ya + i, to_core, None, first)
        v.P32[:, cols] = jnp.dot(v.AB[own_half, :], v.WD[:, cols], preferred_element_type=f32)

    def y_pass(d):
        cols = col_block(d)
        for i, off in y_parts(d):
            part = pl.ds(off, YR)
            got(r1.at[part, cols], base.ya + i)
            s2[part, cols] = (v.P32[part, cols] + r1[part, cols].astype(f32)).astype(bf16)
            send(s2.at[part, cols], r2.at[part, cols], base.ys + i, to_y, None, second)

    wd[1].wait()
    y_begin(0)
    relayed(wd, False)
    for d in range(1, F):
        y_begin(d)
    for d in range(F):
        y_pass(d)
    te_copy.wait()
    up_copy.wait()
    squares, counted = jnp.zeros((1, 1), f32), jnp.zeros((1, 1), f32)
    for d in range(F):
        cols = col_block(d)
        for i, off in y_parts(d):
            part, mine = pl.ds(off, YR), rows(core * HF + off, YR)
            got(r2.at[part, cols], base.ys + i)
            y_now = v.H[part, cols] + s2[part, cols].astype(f32) + r2[part, cols].astype(f32)
            v.YB[mine, cols] = y_now.astype(bf16)
            weighting = v.VC[mine, pl.ds(0, 1)]
            differ = y_now - v.TE[part, cols].astype(f32)
            squares = squares + total_of(weighting * differ * differ)
            if d == 0:
                counted = counted + total_of(weighting)
            dy = v.UP[part, cols].astype(f32) + weighting * differ
            v.DY[part, cols] = dy
            v.DYB[mine, cols] = dy.astype(bf16)
            at = v.DYB.at[mine, cols]
            send(at, at, base.dy + i, to_core, None, to_share)
    tile_row = lax.broadcasted_iota(jnp.int32, (8, 128), 0)
    tile = jnp.where(
        tile_row == 0, jnp.broadcast_to(squares, (8, 128)), jnp.broadcast_to(counted, (8, 128))
    )
    v.LT[...] = tile
    v.LX[fs] = tile
    for d in range(1, F):
        send(v.LT, v.LX.at[fs], base.lx + d - 1, {"fsdp": owner(d)})
    y_half = v.YB.at[own_half]
    send(y_half, y_half, base.yb, to_core)
    grads_out = [outgoing(v.XS.at[owner(d)]) for d in range(1, F)]
    group_in, group_out = outgoing(v.XS.at[fs]), outgoing(v.GRAD, jnp.logical_not(is_outer))
    for d in range(F):
        for i, off in y_parts(d):
            got(v.DYB.at[rows((1 - core) * HF + off, YR), col_block(d)], base.dy + i)

    sent, own_done = [0], [0]

    def weight_grad(left, right, at, d, flipped=False):
        who = owner(d)
        tokens = left.shape[1 if flipped else 0]
        n = left.shape[0 if flipped else 1]
        if d == 0:
            own_done[0] = at + n
        rhs = right[pl.ds(0, tokens), pl.ds(hint(who * DF, 128), DF)]
        v.XS[who, pl.ds(at, n), :] = contract(left[...], rhs, (1 if flipped else 0, 0)).astype(bf16)

    def grad_index(d, j):
        return base.gx + (d - 1) * NK + j

    def grad_send(d, at, j):
        rcopy(
            v.XS.at[owner(d), at], v.XR.at[d - 1, at], grads_out[d - 1], grad_index(d, j),
            {"fsdp": owner(d)},
        ).start()

    def grads_ready(upto):
        first, last = sent[0], min(upto // CH, NB)
        sent[0] = last

        def body(j, _):
            for d in range(1, F):
                grad_send(d, rows(j * CH, CH), j)
            return 0

        if last > first:
            lax.fori_loop(first, last, body, 0)
        if upto == N:
            for j in range(NB, NK - 1):
                for d in range(1, F):
                    grad_send(d, small(j), j)

    def small(j):
        return rows(NB * CH + (j - NB) * CS, CS)

    def inward(at, j):
        for d in range(1, F):
            got(v.XR.at[d - 1, at], grad_index(d, j))
        acc = v.XS[fs, at, :].astype(f32)
        for d in range(1, F):
            acc = acc + v.XR[d - 1, at, :].astype(f32)
        v.XS[fs, at, :] = acc.astype(bf16)

        @pl.when(jnp.logical_not(is_outer))
        def _():
            got(v.ZO.at[at], base.zo + j)
            v.XS[fs, at, :] = (acc + v.ZO[at, :].astype(f32)).astype(bf16)

        @pl.when(is_mid)
        def _():
            rcopy(v.XS.at[fs, at], v.ZI.at[at], group_in, base.zi + j, to_inner).start()

        @pl.when(jnp.logical_not(is_mid))
        def _():
            rcopy(v.XS.at[fs, at], v.ZO.at[at], group_in, base.zo + j, to_inner).start()

    def outward(at, j):
        got(v.ZI.at[at], base.zi + j)

        @pl.when(is_mid)
        def _():
            whole = v.XS[fs, at, :].astype(f32) + v.ZI[at, :].astype(f32)
            v.GRAD[at, :] = whole.astype(bf16)

        @pl.when(jnp.logical_not(is_mid))
        def _():
            v.GRAD[at, :] = v.ZI[at, :]

        @pl.when(jnp.logical_not(is_outer))
        def _():
            rcopy(v.GRAD.at[at], v.ZI.at[at], group_out, base.zi + j, to_outer).start()

        pltpu.make_async_copy(v.GRAD.at[at], v.grad_out.at[at], ls.at[10]).start()

    lag_in, lag_out = SKEW * hop, SKEW * (2 * half - 1 - hop)
    LAST = NK + SKEW * (2 * half - 1)

    def pump(first, last):
        def body(i, _):
            ja, jb = i - lag_in, i - lag_out
            pl.when((ja >= 0) & (ja < NB))(lambda: inward(rows(ja * CH, CH), ja))
            if last > NB:
                pl.when((ja >= NB) & (ja < NK))(lambda: inward(small(ja), ja))
            pl.when((jb >= 0) & (jb < NB))(lambda: outward(rows(jb * CH, CH), jb))
            if last > NB:
                pl.when((jb >= NB) & (jb < NK))(lambda: outward(small(jb), jb))
            return 0

        if last > first:
            lax.fori_loop(first, last, body, 0)

    pumped = [0]

    def pump_to(place):
        last = LAST if place > 49 else place * NCH // 49
        if place <= 49:
            last = min(last, sent[0], own_done[0] // CH)
        if last > pumped[0]:
            pump(pumped[0], last)
            pumped[0] = last

    peers = range(1, F)
    for d in peers:
        weight_grad(v.AB, v.DYB, 0, d)
    grads_ready(FF)
    v.S[pl.ds(0, R), pl.ds(0, FF)] = contract(v.DYB[...], v.WD[...], (1, 1))

    def activate_back(i, _):
        at = rows(i * RC, RC)
        g, u, da = v.GB[at, :].astype(f32), v.UB[at, :].astype(f32), v.S[at, pl.ds(0, FF)]
        sig = 1.0 / (1.0 + jnp.exp(-g))
        v.DGB[at, :] = (da * u * (sig * (1.0 + g * (1.0 - sig)))).astype(bf16)
        v.DUB[at, :] = (da * (g * sig)).astype(bf16)
        return 0

    lax.fori_loop(0, R // RC, activate_back, 0)
    sum_begin(
        2,
        lambda off: jnp.dot(v.DGB[rows(off, HF), :], v.WG[...], preferred_element_type=f32)
        + jnp.dot(v.DUB[rows(off, HF), :], v.WU[...], preferred_element_type=f32),
    )
    weight_grad(v.AB, v.DYB, 0, 0)
    for d in peers:
        got(v.LX.at[owner(F - d)], base.lx + d - 1)
    send(v.LX, v.LC, base.lc, to_core)
    for d in peers:
        weight_grad(v.DGB, v.N2, FF, d)
    grads_ready(2 * FF)
    for d in peers:
        weight_grad(v.DUB, v.N2, 2 * FF, d)
    grads_ready(3 * FF)
    weight_grad(v.DGB, v.N2, FF, 0)
    weight_grad(v.DUB, v.N2, 2 * FF, 0)
    pump_to(2)
    v.GT[0] = jnp.zeros((8, D), f32)
    for i in range(NCHK):
        dn2 = sum_end(2, i)
        h_now = v.H[chunk(i), :]
        r = lax.rsqrt(jnp.mean(h_now * h_now, axis=-1, keepdims=True) + EPS)
        gd = v.gain_two[...] * dn2
        dh = v.DY[chunk(i), :] + r * gd - h_now * (
            r * r * r * jnp.mean(gd * h_now, axis=-1, keepdims=True)
        )
        v.DH[chunk(i), :] = dh
        v.DHB[my_rows(i), :] = dh.astype(bf16)
        share(v.DHB, base.dh, i)
        part = jnp.sum(dn2 * h_now * r, axis=0, keepdims=True)
        part = jnp.where(yy == i // (NCHK // 2), part, 0.0)
        v.GT[0, pl.ds(0, 1), :] = v.GT[0, pl.ds(0, 1), :] + part
        pump_to(3 + i)
    shared(v.DHB, base.dh)
    got(v.LC, base.lc)
    v.LB[z] = v.LX[...] + v.LC[...]
    for k in range(1, C):
        send(v.LB.at[z], v.LB.at[z], base.ll + k - 1, {"ctx": lax.rem(z + k, C)})

    by_heads(v.DOH, contract(v.DHB[...], v.WO[...], (1, 1)))
    pump_to(7)
    for h in range(H):
        v.S[pl.ds(h * R, R), :] = contract(v.DOH[pl.ds(h * R, R), :], v.VB[...], (1, 1))
    for d in peers:
        weight_grad(v.OB, v.DHB, 3 * FF, d)
    grads_ready(3 * FF + HC)
    weight_grad(v.OB, v.DHB, 3 * FF, 0)
    pump_to(8)

    def soft_back(i, _):
        dp, at, _, low = merged(i)
        prob = v.PM[at, :]
        spread(v.DSB, at, low, prob * (dp - jnp.sum(prob * dp, axis=-1, keepdims=True)))
        return 0

    lax.fori_loop(0, H * R // AR, soft_back, 0)
    pump_to(9)
    scale = HEAD_DIM**-0.5
    v.DVT[...] = contract(v.DOH[...], v.PB[...], (0, 0)).astype(bf16)
    v.DKT[...] = (contract(v.QH[...], v.DSB[...], (0, 0)) * scale).astype(bf16)
    v.DQ[...] = (from_heads(v.DSB, v.KB) * scale).astype(bf16)
    pump_to(11)

    def dn1_product(j, which):
        at = pl.ds(hint(j * R + which * HF, 128), HF)
        out = contract(v.DKT[:, at], v.WQKV[:, pl.ds(HC, HC)], (0, 1))
        out = out + contract(v.DVT[:, at], v.WQKV[:, pl.ds(2 * HC, HC)], (0, 1))
        if j == 0:
            out = out + contract(v.DQ[rows(which * HF, HF), :], v.WQKV[:, pl.ds(0, HC)], (1, 1))
        return out

    for j in range(W, -1, -1):
        v.D1S[j] = dn1_product(j, 1 - core).astype(bf16)
        send(v.D1S.at[j], v.D1R.at[j], base.d1 + j, to_core)
        v.D1O[j] = dn1_product(j, core)
    for d in list(peers) + [0]:
        at = 3 * FF + HC
        weight_grad(v.DQ, v.N1, at, d)
        weight_grad(v.DKT, v.N1, at + HC, d, True)
        weight_grad(v.DVT, v.N1, at + 2 * HC, d, True)
        if d == F - 1:
            grads_ready(N)
    pump_to(13)
    for j in range(W, -1, -1):
        got(v.D1R.at[j], base.d1 + j)
        there = rows((1 - yy) * Q, Q)
        v.D2S[j] = (v.D1O[j, there, :] + v.D1R[j, there, :].astype(f32)).astype(bf16)
        send(v.D2S.at[j], v.D2R.at[j], base.d2 + j, to_y)
    pump_to(16)
    here = rows(yy * Q, Q)
    for j in range(W, 0, -1):
        got(v.D2R.at[j], base.d2 + j)
        own = v.D1O[j, here, :] + v.D1R[j, here, :].astype(f32) + v.D2R[j].astype(f32)
        v.DZS[j] = own.astype(bf16)
        if j < W:
            @pl.when(has_next & (z >= j))
            def _(j=j, own=own):
                got(v.DZR.at[j + 1], base.dz + j + 1)
                v.DZS[j] = (own + v.DZR[j + 1].astype(f32)).astype(bf16)
        send(v.DZS.at[j], v.DZR.at[j], base.dz + j, to_prev, z >= j)
        pump_to(19 + 2 * (W - j))

    pump_to(23)
    pump_to(26)
    got(v.D2R.at[0], base.d2)
    v.P32[pl.ds(0, Q), :] = (
        v.D1O[0, here, :] + v.D1R[0, here, :].astype(f32) + v.D2R[0].astype(f32)
    )

    @pl.when(has_next)
    def _():
        got(v.DZR.at[1], base.dz + 1)
        v.P32[pl.ds(0, Q), :] = v.P32[pl.ds(0, Q), :] + v.DZR[1].astype(f32)

    quarter = rows(core * HF + yy * Q, Q)
    dn1 = v.P32[pl.ds(0, Q), :]
    x_now = v.XB[quarter, :].astype(f32)
    r = lax.rsqrt(jnp.mean(x_now * x_now, axis=-1, keepdims=True) + EPS)
    gd = v.gain_one[...] * dn1
    gi = v.DH[here, :] + r * gd - x_now * (
        r * r * r * jnp.mean(gd * x_now, axis=-1, keepdims=True)
    )
    v.GIB[quarter, :] = gi.astype(bf16)
    mine = v.GIB.at[quarter]
    send(mine, mine, base.i1, to_y)
    send(mine, mine, base.i2, to_core)
    v.GT[0, pl.ds(1, 1), :] = jnp.sum(dn1 * x_now * r, axis=0, keepdims=True)
    send(v.GT.at[0], v.GR.at[0], base.g1, to_core)
    pump_to(28)
    got(v.GR.at[0], base.g1)
    v.GT[1] = v.GT[0] + v.GR[0]
    send(v.GT.at[1], v.GR.at[1], base.g2, to_y)
    from_y = v.GIB.at[rows(core * HF + (1 - yy) * Q, Q)]
    got(from_y, base.i1)
    send(from_y, from_y, base.i3, to_core)
    pump_to(32)
    got(v.GR.at[1], base.g2)
    v.GT[2] = v.GT[1] + v.GR[1]
    for d in list(peers) + [0]:
        tile = v.GT[2, :, pl.ds(hint(owner(d) * DF, 128), DF)]
        v.XS[owner(d), pl.ds(N, 16), :] = jnp.concatenate([tile, jnp.zeros_like(tile)], 0).astype(bf16)
        if d:
            grad_send(d, small(NK - 1), NK - 1)

    pump_to(49)
    for k in range(1, C):
        got(v.LB.at[lax.rem(z + C - k, C)], base.ll + k - 1)
    sums = [sum(v.LB[c, s] for c in range(C)) for s in range(F)]
    counted = sum(s[1:2, :] for s in sums)
    for s in range(F):
        v.LOSS[pl.ds(s, 1), :] = sums[s][0:1, :] * F / (counted * D)
    got(v.YB.at[rows((1 - core) * HF, HF)], base.yb)
    got(v.GIB.at[rows((1 - core) * HF + yy * Q, Q)], base.i2)
    got(v.GIB.at[rows((1 - core) * HF + (1 - yy) * Q, Q)], base.i3)
    results = (
        pltpu.make_async_copy(v.YB, v.y_out, ls.at[0]),
        pltpu.make_async_copy(v.GIB, v.gi_out, ls.at[1]),
        pltpu.make_async_copy(v.LOSS, v.loss_out, ls.at[2]),
    )
    for cp in results:
        cp.start()

    streams = grads_out + [group_in, group_out]

    def all_left(k):
        src, cond = unsent[k]

        def left():
            rcopy(src, src, k, 0, to_core).wait_send()

        if cond is None:
            left()
        else:
            pl.when(cond)(left)

    for k in range(len(unsent)):
        if k not in streams:
            all_left(k)
    pump_to(50)
    for k in streams:
        all_left(k)
    for cp in results:
        cp.wait()
    pltpu.make_async_copy(v.GRAD, v.grad_out, ls.at[10]).wait()


def finish_kernel(p, grad, gib, yb, loss, *refs):
    (y_out, loss_out, gi_out, one, gq, gk, gv, go, two, gg, gu, gd) = refs[:12]
    g_buf, i_buf, y_buf, l_buf, g_wide, i_wide, q_wide, sem_in, sem_out = refs[12:]
    FF, HC, N = p.FF, p.HC, p.N
    at = 3 * FF
    plain, flip = [], []
    for ref, first in ((gd, 0), (gg, FF), (gu, 2 * FF)):
        plain += [(ref, first, 0, FF // 2), (ref, first + FF // 2, FF // 2, FF // 2)]
    plain.append((go, at, 0, HC))
    flip = [(gq, at + HC), (gk, at + 2 * HC), (gv, at + 3 * HC)]
    loads = []

    def load(src, dst):
        cp = pltpu.make_async_copy(src, dst, sem_in.at[len(loads)])
        cp.start()
        loads.append(cp)
        return cp

    stores = []

    def store(src, dst):
        cp = pltpu.make_async_copy(src, dst, sem_out.at[len(stores)])
        cp.start()
        stores.append(cp)

    plain_in = [load(grad.at[pl.ds(f, n)], g_buf.at[pl.ds(f, n)]) for _, f, _, n in plain]
    flip_in = [load(grad.at[pl.ds(f, HC)], g_buf.at[pl.ds(f, HC)]) for _, f in flip]
    gi_in = load(gib, i_buf)
    y_in = load(yb, y_buf)
    gain_in = load(grad.at[pl.ds(N, 16)], g_buf.at[pl.ds(N, 16)])
    loss_in = load(loss, l_buf)
    for (ref, first, row, n), cp in zip(plain, plain_in):
        cp.wait()
        g_wide[pl.ds(first, n), :] = g_buf[pl.ds(first, n), :].astype(f32)
        store(g_wide.at[pl.ds(first, n)], ref.at[pl.ds(row, n)])
    for k, ((ref, first), cp) in enumerate(zip(flip, flip_in)):
        cp.wait()
        for c in range(0, HC, 128):
            w = min(128, HC - c)
            q_wide[k, :, pl.ds(c, w)] = g_buf[pl.ds(first + c, w), :].astype(f32).T
        store(q_wide.at[k], ref)
    gi_in.wait()
    i_wide[...] = i_buf[...].astype(f32)
    store(i_wide, gi_out.at[0])
    y_in.wait()
    store(y_buf, y_out.at[0])
    gain_in.wait()
    gains = g_buf[pl.ds(N, 16), :].astype(f32)
    two[...] = gains[0:1, :]
    one[...] = gains[1:2, :]
    loss_in.wait()
    for s in range(p.F):
        loss_out[s] = jnp.max(l_buf[pl.ds(s, 1), :])
    for cp in stores:
        cp.wait()


def shards(mesh_shape, seq_len, *args):
    (inputs, upstream, teacher, valid, segment, gain_one, wq, wk, wv, wo, gain_two, wg, wu, wd) = args
    _, rows_here, width = inputs.shape
    p = Plan(
        mesh_shape["fsdp"], mesh_shape["ctx"], rows_here, width, wq.shape[1], wg.shape[1], seq_len
    )
    R, D, DF, HC, FF, F = p.R, p.D, p.DF, p.HC, p.FF, p.F
    NG = p.N + 16
    scratch = scratch_of(p)
    vmem = pl.BlockSpec(memory_space=pltpu.VMEM)
    anywhere = pl.BlockSpec(memory_space=pl.ANY)
    in_specs = [anywhere] * 3 + [vmem] * 3 + [anywhere] * 4 + [vmem] + [anywhere] * 3
    sds = jax.ShapeDtypeStruct
    grad, gib, yb, loss = pl.pallas_call(
        functools.partial(layer_kernel, p, tuple(scratch)),
        out_shape=(
            sds((NG, DF), bf16), sds((R, D), bf16), sds((R, D), bf16), sds((max(F, 8), 128), f32),
        ),
        in_specs=in_specs,
        out_specs=(anywhere,) * 4,
        scratch_shapes=[pltpu.VMEM(s, dt) for s, dt in scratch.values()]
        + [
            pltpu.SemaphoreType.DMA((p.sends,)), pltpu.SemaphoreType.DMA((p.total,)),
            pltpu.SemaphoreType.DMA((11,)),
        ],
        compiler_params=pltpu.CompilerParams(
            collective_id=0, has_side_effects=True, vmem_limit_bytes=67043328
        ),
        name="layer",
    )(
        inputs.reshape(R, D), upstream.reshape(R, D), teacher.reshape(R, D), valid, segment,
        gain_one.reshape(1, D), wq, wk, wv, wo, gain_two.reshape(1, D), wg.T, wu.T, wd,
    )
    outs = pl.pallas_call(
        functools.partial(finish_kernel, p),
        out_shape=(
            sds((1, R, D), bf16), sds((F,), f32), sds((1, R, D), f32), sds((1, DF), f32),
            sds((DF, HC), f32), sds((DF, HC), f32), sds((DF, HC), f32), sds((HC, DF), f32),
            sds((1, DF), f32), sds((FF, DF), f32), sds((FF, DF), f32), sds((FF, DF), f32),
        ),
        in_specs=[anywhere] * 4,
        out_specs=(anywhere, pl.BlockSpec(memory_space=pltpu.SMEM), anywhere, vmem)
        + (anywhere,) * 4 + (vmem,) + (anywhere,) * 3,
        scratch_shapes=[
            pltpu.VMEM((NG, DF), bf16), pltpu.VMEM((R, D), bf16), pltpu.VMEM((R, D), bf16),
            pltpu.VMEM((max(F, 8), 128), f32), pltpu.VMEM((3 * FF + HC, DF), f32),
            pltpu.VMEM((R, D), f32), pltpu.VMEM((3, DF, HC), f32),
            pltpu.SemaphoreType.DMA((14,)), pltpu.SemaphoreType.DMA((12,)),
        ],
        compiler_params=pltpu.CompilerParams(vmem_limit_bytes=67043328),
        name="finish",
    )(grad, gib, yb, loss)
    outs = list(outs)
    outs[3], outs[8] = outs[3].reshape(DF), outs[8].reshape(DF)
    outs[9], outs[10] = outs[9].T, outs[10].T
    return tuple(outs)


def solution(mesh):
    def run(*args):
        token, row, col = P("fsdp", "ctx", None), P("fsdp", "tp"), P("tp", "fsdp")
        pair = P("fsdp", "ctx")
        return jax.shard_map(
            functools.partial(shards, dict(mesh.shape), args[0].shape[1]),
            mesh=mesh,
            in_specs=(token, token, token, pair, pair, P(), row, row, row, col, P(), row, row, col),
            out_specs=(
                token, P(), token, P("fsdp"), row, row, row, col, P("fsdp"), row, row, col,
            ),
            check_vma=False,
        )(*args)

    return run
```

```python
import functools
from types import SimpleNamespace

import jax
import jax.numpy as jnp
from jax import lax
from jax.experimental import pallas as pl
from jax.experimental.pallas import tpu as pltpu
from jax.sharding import PartitionSpec as P

HEAD_DIM = 64
EPS = 1e-05
MESH = pl.DeviceIdType.MESH
NCHK = 4
YROWS = 2
SKEW = 2
f32, bf16 = jnp.float32, jnp.bfloat16


class Plan:
    def __init__(self, fsdp, ctx, rows, width, head_cols, hidden, seq_len):
        self.F, self.C, self.R, self.D = fsdp, ctx, rows, width
        self.HC, self.FF = head_cols, hidden
        self.DF = width // fsdp
        self.W = -(-(seq_len // 2) // rows)
        self.N = 3 * hidden + 4 * head_cols
        self.CH = next(
            k for k in range(16, self.N + 1, 16) if self.N % k == 0 and k * self.DF >= 57344
        )
        self.NCH = self.N // self.CH
        self.NB = self.NCH - max(1, 224 // self.CH)
        rest = self.N + 16 - self.NB * self.CH
        self.CS = next(k for k in (48, 64, 80, 32, 16) if rest % k == 0)
        self.NK = self.NB + rest // self.CS
        self.base, self.total = SimpleNamespace(), 0
        peers = fsdp - 1
        for name, count in dict(
            ya=YROWS * fsdp, ys=YROWS * fsdp, xz=2 * self.W, sg=self.W, xy=2 * self.W, xc=self.W, wd=11 * peers, wr=11 * peers,
            a=3 * NCHK, b=3 * NCHK, n2=NCHK, yb=1, dy=YROWS * fsdp, dh=NCHK,
            lc=1, ll=ctx - 1, lx=peers, d1=self.W + 1, d2=self.W + 1, dz=self.W + 1,
            g1=1, g2=1, i1=1, i2=1, i3=1, gx=peers * self.NK, zo=self.NK, zi=self.NK,
        ).items():
            setattr(self.base, name, self.total)
            self.total += count
        self.sends = 4 * self.W + 2 + 14 * peers + 9 + 3 + 2 * ctx + peers + 3 * self.W + 2 + 5 + peers + 2


def contract(left, right, dims):
    return lax.dot_general(left, right, ((dims[:1], dims[1:]), ((), ())), preferred_element_type=f32)


def total_of(v):
    return jnp.sum(jnp.sum(v, axis=1, keepdims=True), axis=0, keepdims=True)


def scratch_of(p):
    R, D, HC, FF, DF, F, C, W = p.R, p.D, p.HC, p.FF, p.DF, p.F, p.C, p.W
    HF, Q, KR, H = R // 2, R // 4, (p.W + 1) * p.R, p.HC // HEAD_DIM
    NG = p.N + 16
    return dict(
        XB=((KR, D), bf16), SG=((W + 1, 1, R), jnp.int32), N1=((KR, D), bf16),
        WQKV=((D, 3 * HC), bf16), WO=((HC, D), bf16), WG=((FF, D), bf16),
        WU=((FF, D), bf16), WD=((FF, D), bf16),
        QH=((H * R, HC), bf16), KB=((KR, HC), bf16), VB=((KR, HC), bf16), DOH=((H * R, HC), bf16),
        PM=((H * R, W * R), f32), S=((H * R, KR), f32), PB=((H * R, KR), bf16), DSB=((H * R, KR), bf16),
        BIAS=((R, W * R), f32), DQ=((R, HC), bf16), DKT=((HC, KR), bf16), DVT=((HC, KR), bf16),
        OB=((R, HC), bf16), VC=((R, 128), f32),
        H=((HF, D), f32), DY=((HF, D), f32), DH=((HF, D), f32), P32=((HF, D), f32),
        UP=((HF, D), bf16), TE=((HF, D), bf16),
        N2=((R, D), bf16), DYB=((R, D), bf16), DHB=((R, D), bf16),
        GB=((R, FF), bf16), UB=((R, FF), bf16), AB=((R, FF), bf16),
        DGB=((R, FF), bf16), DUB=((R, FF), bf16),
        D1S=((W + 1, HF, D), bf16), D1R=((W + 1, HF, D), bf16), D1O=((W + 1, HF, D), f32),
        D2S=((W + 1, Q, D), bf16), D2R=((W + 1, Q, D), bf16), DZR=((W + 1, Q, D), bf16),
        DZS=((W + 1, Q, D), bf16),
        GT=((3, 8, D), f32), GR=((2, 8, D), f32),
        LT=((8, 128), f32), LX=((F, 8, 128), f32), LC=((F, 8, 128), f32), LB=((C, F, 8, 128), f32),
        XS=((F, NG, DF), bf16), XR=((F - 1, NG, DF), bf16),
        ZO=((NG, DF), bf16), ZI=((NG, DF), bf16), GRAD=((NG, DF), bf16), GIB=((R, D), bf16),
        YB=((R, D), bf16), LOSS=((max(F, 8), 128), f32),
        S1=((3, HF, D), bf16), R1=((3, HF, D), bf16), S2=((3, HF, D), bf16), R2=((3, HF, D), bf16),
    )


def layer_kernel(p, names, *refs):
    v = SimpleNamespace(**dict(zip(names, refs[18:], strict=False)))
    (
        v.x, v.upstream, v.teacher, v.valid, v.segment, v.gain_one, v.wq, v.wk, v.wv, v.wo,
        v.gain_two, v.wg, v.wu, v.wd, v.grad_out, v.gi_out, v.y_out, v.loss_out,
    ) = refs[:18]
    ss, rs, ls = refs[-3:]
    R, D, HC, FF, DF, F, C, W, N, CH, NCH, CS, NB, NK = (
        p.R, p.D, p.HC, p.FF, p.DF, p.F, p.C, p.W, p.N, p.CH, p.NCH, p.CS, p.NB, p.NK
    )
    HF, Q, KR, H = R // 2, R // 4, (W + 1) * R, HC // HEAD_DIM
    RC = HF // NCHK
    base = p.base
    fs, z, t = lax.axis_index("fsdp"), lax.axis_index("ctx"), lax.axis_index("tp")
    core, yy, par = lax.rem(t, 2), t // 2, lax.rem(z, 2)
    to_core, to_y = {"tp": t + 1 - 2 * core}, {"tp": lax.rem(t + 2, 4)}
    to_next, to_prev = {"ctx": lax.rem(z + 1, C)}, {"ctx": lax.rem(z + C - 1, C)}
    to_pair = {"ctx": z + 1 - 2 * par}
    has_next, has_prev = z < C - 1, z > 0
    half = C // 2
    left_side = z < half
    hop = jnp.where(left_side, z, C - 1 - z)
    step_in = jnp.where(left_side, 1, -1)
    to_inner = {"ctx": z + step_in}
    to_outer = {"ctx": lax.rem(z - step_in + C, C)}
    is_outer, is_mid = hop == 0, hop == half - 1

    def owner(d):
        return lax.rem(fs + d, F)

    def rcopy(src, dst, sk, rk, dev):
        return pltpu.make_async_remote_copy(
            src_ref=src, dst_ref=dst, send_sem=ss.at[sk], recv_sem=rs.at[rk],
            device_id=dev, device_id_type=MESH,
        )

    unsent = []

    def outgoing(src, cond=None):
        unsent.append((src, cond))
        assert len(unsent) <= p.sends
        return len(unsent) - 1

    def send(src, dst, k, dev, cond=None, group=None):
        sk = outgoing(src, cond) if group is None else group
        if cond is None:
            rcopy(src, dst, sk, k, dev).start()
        else:
            pl.when(cond)(lambda: rcopy(src, dst, sk, k, dev).start())

    def got(dst, k):
        rcopy(dst, dst, 0, k, to_core).wait_recv()

    def hint(i, m):
        return pl.multiple_of(i, m)

    def rows(off, n, m=16):
        return pl.ds(hint(off, m), n)

    barrier = pltpu.get_barrier_semaphore()

    def greet(dev):
        pl.semaphore_signal(barrier, inc=1, device_id=dev, device_id_type=MESH)

    greet(to_core)
    greet(to_y)
    for d in range(1, F):
        greet({"fsdp": owner(d)})
    for k in range(1, C):
        greet({"ctx": lax.rem(z + k, C)})

    local = []

    def fetch(src, dst):
        cp = pltpu.make_async_copy(src, dst, ls.at[len(local)])
        cp.start()
        local.append(cp)
        return cp

    own_half = rows(core * HF, HF)
    x_copy = fetch(v.x, v.XB.at[pl.ds(0, R)])
    own_cols = pl.ds(hint(fs * DF, 128), DF)

    def by_row(dst, col0, cols):
        def region(who, off, n):
            return dst.at[rows(who * DF + off, n), pl.ds(col0, cols)]
        return region

    def by_col(dst):
        def region(who, off, n):
            return dst.at[rows(off, n), pl.ds(hint(who * DF, 128), DF)]
        return region

    weights = (
        (v.wq, by_row(v.WQKV, 0, HC), 1), (v.wk, by_row(v.WQKV, HC, HC), 1),
        (v.wv, by_row(v.WQKV, 2 * HC, HC), 1), (v.wo, by_col(v.WO), 1),
        (v.wg, by_col(v.WG), 2), (v.wu, by_col(v.WU), 2), (v.wd, by_col(v.WD), 3),
    )
    gathers = []
    count = 0
    for source, region, parts in weights:
        tall = source.shape[0]
        cuts = [0, tall // 2] if parts == 1 else [0, tall // 4, tall // 2]
        if parts == 3:
            cuts.insert(2, tall // 3 // 16 * 16)
        gathers.append((
            source, fetch(source, region(fs, 0, tall)),
            [
                (region, cuts[min(parts, 2)], tall // 2, cuts[k], cuts[k + 1] - cuts[k], count + k)
                for k in range(parts)
            ],
        ))
        count += parts
    wq, wk, wv, wo, wg, wu, wd = gathers
    te_copy = fetch(v.teacher.at[own_half], v.TE)
    up_copy = fetch(v.upstream.at[own_half], v.UP)

    pl.semaphore_wait(barrier, F + C)

    def piece_index(kind, number, d):
        return kind + number * (F - 1) + d - 1

    for source, _, pieces in gathers:
        tall = source.shape[0] // 2
        for d in range(1, F):
            group = outgoing(source.at[rows(par * tall, tall)])
            for region, passed, _, at, n, number in pieces:
                off = par * tall + at
                send(
                    source.at[rows(off, n)], region(fs, off, n), piece_index(base.wd, number, d),
                    {"fsdp": owner(d)}, None, group,
                )
                if at >= passed:
                    off = (1 - par) * tall + at
                    send(
                        source.at[rows(off, n)], region(fs, off, n),
                        piece_index(base.wr, number, d), {"fsdp": owner(d)},
                    )

    relays = {}

    def relay(weight, which):
        region, passed, tall, at, n, number = weight[2][which]
        for d in range(1, F):
            if which == 0:
                relays[number, d] = outgoing(region(owner(F - d), par * tall, passed))
            part = region(owner(F - d), par * tall + at, n)
            got(part, piece_index(base.wd, number, d))
            send(
                part, part, piece_index(base.wr, number, d), to_pair, None, relays[number - which, d]
            )

    def relayed(weight, with_own=True):
        if with_own:
            weight[1].wait()
        for region, passed, tall, at, n, number in weight[2]:
            for d in range(1, F):
                if at >= passed:
                    got(region(owner(F - d), par * tall + at, n), piece_index(base.wd, number, d))
                got(region(owner(F - d), (1 - par) * tall + at, n), piece_index(base.wr, number, d))

    def x_half(j, which):
        return v.XB.at[rows(j * R + which * HF, HF)]

    def x_eighth(j, y, k):
        return v.XB.at[rows(j * R + core * HF + y * Q + k * (Q // 2), Q // 2)]

    def x_quarter(j, y):
        return v.XB.at[rows(j * R + core * HF + y * Q, Q)]

    x_group = outgoing(x_quarter(0, yy), has_next)
    for k in range(2):
        send(
            v.x.at[rows(core * HF + yy * Q + k * (Q // 2), Q // 2)], x_eighth(1, yy, k), base.xz + k,
            to_next, has_next, x_group,
        )
    v.SG[0] = v.segment[...]
    send(v.segment, v.SG.at[1], base.sg, to_next, has_next)
    for j in range(1, W + 1):
        @pl.when(z < j)
        def _(j=j):
            v.XB[pl.ds(j * R, R), :] = jnp.zeros((R, D), bf16)
            v.SG[j] = jnp.full((1, R), -1, jnp.int32)

    def x_pass(j):
        both = (z >= j) & has_next
        onward = outgoing(x_quarter(j, yy), both) if j < W else None
        across = outgoing(x_quarter(j, yy), z >= j)
        for k in range(2):
            part = x_eighth(j, yy, k)
            pl.when(z >= j)(lambda part=part, k=k: got(part, base.xz + 2 * (j - 1) + k))
            if j < W:
                send(part, x_eighth(j + 1, yy, k), base.xz + 2 * j + k, to_next, both, onward)
            send(part, part, base.xy + 2 * (j - 1) + k, to_y, z >= j, across)
        pl.when(z >= j)(lambda: got(v.SG.at[j], base.sg + j - 1))
        if j < W:
            send(v.SG.at[j], v.SG.at[j + 1], base.sg + j, to_next, both)

    def x_join(j):
        for k in range(2):
            pl.when(z >= j)(
                lambda k=k: got(x_eighth(j, 1 - yy, k), base.xy + 2 * (j - 1) + k)
            )
        send(x_half(j, core), x_half(j, core), base.xc + j - 1, to_core, z >= j)

    def x_done(j):
        pl.when(z >= j)(lambda: got(x_half(j, 1 - core), base.xc + j - 1))

    def norm_rows(j):
        def body(i, _):
            at = rows(j * R + i * RC, RC)
            xs = v.XB[at, :].astype(f32)
            r = lax.rsqrt(jnp.mean(xs * xs, axis=-1, keepdims=True) + EPS)
            v.N1[at, :] = (xs * r * v.gain_one[...]).astype(bf16)
            return 0
        lax.fori_loop(0, R // RC, body, 0)

    eye = lax.broadcasted_iota(jnp.int32, (R, R), 0) == lax.broadcasted_iota(jnp.int32, (R, R), 1)
    lower = lax.broadcasted_iota(jnp.int32, (R, R), 1) <= lax.broadcasted_iota(jnp.int32, (R, R), 0)

    def column(row):
        return jnp.sum(jnp.where(eye, row.astype(f32), 0.0), axis=1, keepdims=True)

    x_copy.wait()
    norm_rows(0)
    v.VC[...] = jnp.broadcast_to(column(v.valid[...]), (R, 128))
    x_pass(1)
    relay(wq, 0)
    relay(wk, 0)
    relay(wv, 0)
    for j in range(1, W + 1):
        if j < W:
            x_pass(j + 1)
        x_join(j)
        if j == 1:
            relay(wo, 0)
        if j == W:
            relay(wg, 0)
        x_done(j)
        norm_rows(j)
    seg_col = column(v.SG[0])
    for j in range(W):
        seg_row = jnp.broadcast_to(v.SG[j].astype(f32), (R, R))
        if j == 0:
            seg_row = jnp.where(lower, seg_row, v.SG[W].astype(f32))
        v.BIAS[:, pl.ds(j * R, R)] = jnp.where(seg_col == seg_row, 0.0, -1e30)
    relayed(wq)
    lane_head = lax.broadcasted_iota(jnp.int32, (R, HC), 1) // HEAD_DIM

    def by_heads(ref, val):
        for h in range(H):
            ref[pl.ds(h * R, R), :] = jnp.where(lane_head == h, val, 0.0).astype(bf16)

    def from_heads(ref, other):
        mix = jnp.zeros((R, HC), f32)
        for h in range(H):
            part = jnp.dot(ref[pl.ds(h * R, R), :], other[...], preferred_element_type=f32)
            mix = jnp.where(lane_head == h, part, mix)
        return mix

    by_heads(
        v.QH,
        jnp.dot(v.N1[pl.ds(0, R), :], v.WQKV[:, pl.ds(0, HC)], preferred_element_type=f32),
    )
    relayed(wk)
    relayed(wv)
    for dst, col in ((v.KB, HC), (v.VB, 2 * HC)):
        dst[...] = jnp.dot(
            v.N1[...], v.WQKV[:, pl.ds(col, HC)], preferred_element_type=f32
        ).astype(bf16)
    relay(wg, 1)

    AR = 64 if R % 64 == 0 else R // 4
    WR = W * R

    def merged(i):
        at, inner = rows(i * AR, AR), rows(lax.rem(i, R // AR) * AR, AR)
        place = lax.broadcasted_iota(jnp.int32, (AR, R), 0) + lax.rem(i, R // AR) * AR
        low = lax.broadcasted_iota(jnp.int32, (AR, R), 1) <= place
        first = jnp.where(low, v.S[at, pl.ds(0, R)], v.S[at, pl.ds(WR, R)])
        if W > 1:
            first = jnp.concatenate([first, v.S[at, pl.ds(R, WR - R)]], axis=1)
        return first, at, inner, low

    def spread(ref, at, low, val):
        own = val[:, :R]
        ref[at, pl.ds(0, R)] = jnp.where(low, own, 0.0).astype(bf16)
        ref[at, pl.ds(WR, R)] = jnp.where(low, 0.0, own).astype(bf16)
        if W > 1:
            ref[at, pl.ds(R, WR - R)] = val[:, R:].astype(bf16)

    def soft(i, _):
        s, at, inner, low = merged(i)
        s = s * (HEAD_DIM**-0.5) + v.BIAS[inner, :]
        e = jnp.exp(s - jnp.max(s, axis=-1, keepdims=True))
        prob = e * (1.0 / jnp.sum(e, axis=-1, keepdims=True))
        v.PM[at, :] = prob
        spread(v.PB, at, low, prob)
        return 0

    for h in range(H):
        v.S[pl.ds(h * R, R), :] = contract(v.QH[pl.ds(h * R, R), :], v.KB[...], (1, 1))
    lax.fori_loop(0, H * R // AR, soft, 0)
    relay(wu, 0)
    v.OB[...] = from_heads(v.PB, v.VB).astype(bf16)

    def chunk(i):
        return pl.ds(i * RC, RC)

    def sum_begin(a, product):
        s1, r1, s2, r2 = v.S1.at[a], v.R1.at[a], v.S2.at[a], v.R2.at[a]
        s1[...] = product((1 - core) * HF).astype(bf16)
        first, second = outgoing(s1), outgoing(s2)
        for i in range(NCHK):
            send(s1.at[chunk(i)], r1.at[chunk(i)], base.a + a * NCHK + i, to_core, None, first)
        v.P32[...] = product(core * HF)
        for i in range(NCHK):
            got(r1.at[chunk(i)], base.a + a * NCHK + i)
            s2[chunk(i), :] = (v.P32[chunk(i), :] + r1[chunk(i), :].astype(f32)).astype(bf16)
            send(s2.at[chunk(i)], r2.at[chunk(i)], base.b + a * NCHK + i, to_y, None, second)

    def sum_end(a, i):
        s2, r2 = v.S2.at[a], v.R2.at[a]
        got(r2.at[chunk(i)], base.b + a * NCHK + i)
        return s2[chunk(i), :].astype(f32) + r2[chunk(i), :].astype(f32)

    def my_rows(i):
        return rows(core * HF + i * RC, RC)

    def their_rows(i):
        return rows((1 - core) * HF + i * RC, RC)

    def share(ref, flow, i):
        if i == 0:
            relays[flow] = outgoing(ref.at[own_half])
        send(ref.at[my_rows(i)], ref.at[my_rows(i)], flow + i, to_core, None, relays[flow])

    def shared(ref, flow):
        for i in range(NCHK):
            got(ref.at[their_rows(i)], flow + i)

    relayed(wo)
    sum_begin(
        0,
        lambda off: jnp.dot(v.OB[rows(off, HF), :], v.WO[...], preferred_element_type=f32),
    )
    relay(wu, 1)
    relay(wd, 0)
    for i in range(NCHK):
        h_now = v.XB[my_rows(i), :].astype(f32) + sum_end(0, i)
        v.H[chunk(i), :] = h_now
        r = lax.rsqrt(jnp.mean(h_now * h_now, axis=-1, keepdims=True) + EPS)
        v.N2[my_rows(i), :] = (h_now * r * v.gain_two[...]).astype(bf16)
        share(v.N2, base.n2, i)
        if i == 1:
            relay(wd, 1)

    relayed(wg)
    v.GB[own_half, :] = contract(v.N2[own_half, :], v.WG[...], (1, 1)).astype(bf16)
    shared(v.N2, base.n2)
    other_half = rows((1 - core) * HF, HF)
    v.GB[other_half, :] = contract(v.N2[other_half, :], v.WG[...], (1, 1)).astype(bf16)
    relayed(wu)
    v.UB[...] = contract(v.N2[...], v.WU[...], (1, 1)).astype(bf16)

    def activate(i, _):
        at = rows(i * RC, RC)
        g, u = v.GB[at, :].astype(f32), v.UB[at, :].astype(f32)
        v.AB[at, :] = (g / (1.0 + jnp.exp(-g)) * u).astype(bf16)
        return 0

    lax.fori_loop(0, R // RC, activate, 0)
    YR = HF // YROWS
    s1, r1, s2, r2 = v.S1.at[1], v.R1.at[1], v.S2.at[1], v.R2.at[1]
    first, second, to_share = outgoing(s1), outgoing(s2), outgoing(v.DYB.at[own_half])

    def col_block(d):
        return pl.ds(hint(owner(d) * DF, 128), DF)

    def y_parts(d):
        return [(d * YROWS + k, k * YR) for k in range(YROWS)]

    def y_begin(d):
        cols = col_block(d)
        s1[:, cols] = jnp.dot(
            v.AB[rows((1 - core) * HF, HF), :], v.WD[:, cols], preferred_element_type=f32
        ).astype(bf16)
        for i, off in y_parts(d):
            at = s1.at[pl.ds(off, YR), cols]
            send(at, r1.at[pl.ds(off, YR), cols], base.ya + i, to_core, None, first)
        v.P32[:, cols] = jnp.dot(v.AB[own_half, :], v.WD[:, cols], preferred_element_type=f32)

    def y_pass(d):
        cols = col_block(d)
        for i, off in y_parts(d):
            part = pl.ds(off, YR)
            got(r1.at[part, cols], base.ya + i)
            s2[part, cols] = (v.P32[part, cols] + r1[part, cols].astype(f32)).astype(bf16)
            send(s2.at[part, cols], r2.at[part, cols], base.ys + i, to_y, None, second)

    wd[1].wait()
    y_begin(0)
    relayed(wd, False)
    for d in range(1, F):
        y_begin(d)
    for d in range(F):
        y_pass(d)
    te_copy.wait()
    up_copy.wait()
    squares, counted = jnp.zeros((1, 1), f32), jnp.zeros((1, 1), f32)
    for d in range(F):
        cols = col_block(d)
        for i, off in y_parts(d):
            part, mine = pl.ds(off, YR), rows(core * HF + off, YR)
            got(r2.at[part, cols], base.ys + i)
            y_now = v.H[part, cols] + s2[part, cols].astype(f32) + r2[part, cols].astype(f32)
            v.YB[mine, cols] = y_now.astype(bf16)
            weighting = v.VC[mine, pl.ds(0, 1)]
            differ = y_now - v.TE[part, cols].astype(f32)
            squares = squares + total_of(weighting * differ * differ)
            if d == 0:
                counted = counted + total_of(weighting)
            dy = v.UP[part, cols].astype(f32) + weighting * differ
            v.DY[part, cols] = dy
            v.DYB[mine, cols] = dy.astype(bf16)
            at = v.DYB.at[mine, cols]
            send(at, at, base.dy + i, to_core, None, to_share)
    tile_row = lax.broadcasted_iota(jnp.int32, (8, 128), 0)
    tile = jnp.where(
        tile_row == 0, jnp.broadcast_to(squares, (8, 128)), jnp.broadcast_to(counted, (8, 128))
    )
    v.LT[...] = tile
    v.LX[fs] = tile
    for d in range(1, F):
        send(v.LT, v.LX.at[fs], base.lx + d - 1, {"fsdp": owner(d)})
    y_half = v.YB.at[own_half]
    send(y_half, y_half, base.yb, to_core)
    grads_out = [outgoing(v.XS.at[owner(d)]) for d in range(1, F)]
    group_in, group_out = outgoing(v.XS.at[fs]), outgoing(v.GRAD, jnp.logical_not(is_outer))
    for d in range(F):
        for i, off in y_parts(d):
            got(v.DYB.at[rows((1 - core) * HF + off, YR), col_block(d)], base.dy + i)

    sent, own_done = [0], [0]

    def weight_grad(left, right, at, d, flipped=False):
        who = owner(d)
        tokens = left.shape[1 if flipped else 0]
        n = left.shape[0 if flipped else 1]
        if d == 0:
            own_done[0] = at + n
        rhs = right[pl.ds(0, tokens), pl.ds(hint(who * DF, 128), DF)]
        v.XS[who, pl.ds(at, n), :] = contract(left[...], rhs, (1 if flipped else 0, 0)).astype(bf16)

    def grad_index(d, j):
        return base.gx + (d - 1) * NK + j

    def grad_send(d, at, j):
        rcopy(
            v.XS.at[owner(d), at], v.XR.at[d - 1, at], grads_out[d - 1], grad_index(d, j),
            {"fsdp": owner(d)},
        ).start()

    def grads_ready(upto):
        first, last = sent[0], min(upto // CH, NB)
        sent[0] = last

        def body(j, _):
            for d in range(1, F):
                grad_send(d, rows(j * CH, CH), j)
            return 0

        if last > first:
            lax.fori_loop(first, last, body, 0)
        if upto == N:
            for j in range(NB, NK - 1):
                for d in range(1, F):
                    grad_send(d, small(j), j)

    def small(j):
        return rows(NB * CH + (j - NB) * CS, CS)

    def inward(at, j):
        for d in range(1, F):
            got(v.XR.at[d - 1, at], grad_index(d, j))
        acc = v.XS[fs, at, :].astype(f32)
        for d in range(1, F):
            acc = acc + v.XR[d - 1, at, :].astype(f32)
        v.XS[fs, at, :] = acc.astype(bf16)

        @pl.when(jnp.logical_not(is_outer))
        def _():
            got(v.ZO.at[at], base.zo + j)
            v.XS[fs, at, :] = (acc + v.ZO[at, :].astype(f32)).astype(bf16)

        @pl.when(is_mid)
        def _():
            rcopy(v.XS.at[fs, at], v.ZI.at[at], group_in, base.zi + j, to_inner).start()

        @pl.when(jnp.logical_not(is_mid))
        def _():
            rcopy(v.XS.at[fs, at], v.ZO.at[at], group_in, base.zo + j, to_inner).start()

    def outward(at, j):
        got(v.ZI.at[at], base.zi + j)

        @pl.when(is_mid)
        def _():
            whole = v.XS[fs, at, :].astype(f32) + v.ZI[at, :].astype(f32)
            v.GRAD[at, :] = whole.astype(bf16)

        @pl.when(jnp.logical_not(is_mid))
        def _():
            v.GRAD[at, :] = v.ZI[at, :]

        @pl.when(jnp.logical_not(is_outer))
        def _():
            rcopy(v.GRAD.at[at], v.ZI.at[at], group_out, base.zi + j, to_outer).start()

        pltpu.make_async_copy(v.GRAD.at[at], v.grad_out.at[at], ls.at[10]).start()

    lag_in, lag_out = SKEW * hop, SKEW * (2 * half - 1 - hop)
    LAST = NK + SKEW * (2 * half - 1)

    def pump(first, last):
        def body(i, _):
            ja, jb = i - lag_in, i - lag_out
            pl.when((ja >= 0) & (ja < NB))(lambda: inward(rows(ja * CH, CH), ja))
            if last > NB:
                pl.when((ja >= NB) & (ja < NK))(lambda: inward(small(ja), ja))
            pl.when((jb >= 0) & (jb < NB))(lambda: outward(rows(jb * CH, CH), jb))
            if last > NB:
                pl.when((jb >= NB) & (jb < NK))(lambda: outward(small(jb), jb))
            return 0

        if last > first:
            lax.fori_loop(first, last, body, 0)

    pumped = [0]

    def pump_to(place):
        last = LAST if place > 49 else place * NCH // 49
        if place <= 49:
            last = min(last, sent[0], own_done[0] // CH)
        if last > pumped[0]:
            pump(pumped[0], last)
            pumped[0] = last

    peers = range(1, F)
    for d in peers:
        weight_grad(v.AB, v.DYB, 0, d)
    grads_ready(FF)
    v.S[pl.ds(0, R), pl.ds(0, FF)] = contract(v.DYB[...], v.WD[...], (1, 1))

    def activate_back(i, _):
        at = rows(i * RC, RC)
        g, u, da = v.GB[at, :].astype(f32), v.UB[at, :].astype(f32), v.S[at, pl.ds(0, FF)]
        sig = 1.0 / (1.0 + jnp.exp(-g))
        v.DGB[at, :] = (da * u * (sig * (1.0 + g * (1.0 - sig)))).astype(bf16)
        v.DUB[at, :] = (da * (g * sig)).astype(bf16)
        return 0

    lax.fori_loop(0, R // RC, activate_back, 0)
    sum_begin(
        2,
        lambda off: jnp.dot(v.DGB[rows(off, HF), :], v.WG[...], preferred_element_type=f32)
        + jnp.dot(v.DUB[rows(off, HF), :], v.WU[...], preferred_element_type=f32),
    )
    weight_grad(v.AB, v.DYB, 0, 0)
    for d in peers:
        got(v.LX.at[owner(F - d)], base.lx + d - 1)
    send(v.LX, v.LC, base.lc, to_core)
    for d in peers:
        weight_grad(v.DGB, v.N2, FF, d)
    grads_ready(2 * FF)
    for d in peers:
        weight_grad(v.DUB, v.N2, 2 * FF, d)
    grads_ready(3 * FF)
    weight_grad(v.DGB, v.N2, FF, 0)
    weight_grad(v.DUB, v.N2, 2 * FF, 0)
    pump_to(2)
    v.GT[0] = jnp.zeros((8, D), f32)
    for i in range(NCHK):
        dn2 = sum_end(2, i)
        h_now = v.H[chunk(i), :]
        r = lax.rsqrt(jnp.mean(h_now * h_now, axis=-1, keepdims=True) + EPS)
        gd = v.gain_two[...] * dn2
        dh = v.DY[chunk(i), :] + r * gd - h_now * (
            r * r * r * jnp.mean(gd * h_now, axis=-1, keepdims=True)
        )
        v.DH[chunk(i), :] = dh
        v.DHB[my_rows(i), :] = dh.astype(bf16)
        share(v.DHB, base.dh, i)
        part = jnp.sum(dn2 * h_now * r, axis=0, keepdims=True)
        part = jnp.where(yy == i // (NCHK // 2), part, 0.0)
        v.GT[0, pl.ds(0, 1), :] = v.GT[0, pl.ds(0, 1), :] + part
        pump_to(3 + i)
    shared(v.DHB, base.dh)
    got(v.LC, base.lc)
    v.LB[z] = v.LX[...] + v.LC[...]
    for k in range(1, C):
        send(v.LB.at[z], v.LB.at[z], base.ll + k - 1, {"ctx": lax.rem(z + k, C)})

    by_heads(v.DOH, contract(v.DHB[...], v.WO[...], (1, 1)))
    pump_to(7)
    for h in range(H):
        v.S[pl.ds(h * R, R), :] = contract(v.DOH[pl.ds(h * R, R), :], v.VB[...], (1, 1))
    for d in peers:
        weight_grad(v.OB, v.DHB, 3 * FF, d)
    grads_ready(3 * FF + HC)
    weight_grad(v.OB, v.DHB, 3 * FF, 0)
    pump_to(8)

    def soft_back(i, _):
        dp, at, _, low = merged(i)
        prob = v.PM[at, :]
        spread(v.DSB, at, low, prob * (dp - jnp.sum(prob * dp, axis=-1, keepdims=True)))
        return 0

    lax.fori_loop(0, H * R // AR, soft_back, 0)
    pump_to(9)
    scale = HEAD_DIM**-0.5
    v.DVT[...] = contract(v.DOH[...], v.PB[...], (0, 0)).astype(bf16)
    v.DKT[...] = (contract(v.QH[...], v.DSB[...], (0, 0)) * scale).astype(bf16)
    v.DQ[...] = (from_heads(v.DSB, v.KB) * scale).astype(bf16)
    pump_to(11)

    def dn1_product(j, which):
        at = pl.ds(hint(j * R + which * HF, 128), HF)
        out = contract(v.DKT[:, at], v.WQKV[:, pl.ds(HC, HC)], (0, 1))
        out = out + contract(v.DVT[:, at], v.WQKV[:, pl.ds(2 * HC, HC)], (0, 1))
        if j == 0:
            out = out + contract(v.DQ[rows(which * HF, HF), :], v.WQKV[:, pl.ds(0, HC)], (1, 1))
        return out

    for j in range(W, -1, -1):
        v.D1S[j] = dn1_product(j, 1 - core).astype(bf16)
        send(v.D1S.at[j], v.D1R.at[j], base.d1 + j, to_core)
        v.D1O[j] = dn1_product(j, core)
    for d in list(peers) + [0]:
        at = 3 * FF + HC
        weight_grad(v.DQ, v.N1, at, d)
        weight_grad(v.DKT, v.N1, at + HC, d, True)
        weight_grad(v.DVT, v.N1, at + 2 * HC, d, True)
        if d == F - 1:
            grads_ready(N)
    pump_to(13)
    for j in range(W, -1, -1):
        got(v.D1R.at[j], base.d1 + j)
        there = rows((1 - yy) * Q, Q)
        v.D2S[j] = (v.D1O[j, there, :] + v.D1R[j, there, :].astype(f32)).astype(bf16)
        send(v.D2S.at[j], v.D2R.at[j], base.d2 + j, to_y)
    pump_to(16)
    here = rows(yy * Q, Q)
    for j in range(W, 0, -1):
        got(v.D2R.at[j], base.d2 + j)
        own = v.D1O[j, here, :] + v.D1R[j, here, :].astype(f32) + v.D2R[j].astype(f32)
        v.DZS[j] = own.astype(bf16)
        if j < W:
            @pl.when(has_next & (z >= j))
            def _(j=j, own=own):
                got(v.DZR.at[j + 1], base.dz + j + 1)
                v.DZS[j] = (own + v.DZR[j + 1].astype(f32)).astype(bf16)
        send(v.DZS.at[j], v.DZR.at[j], base.dz + j, to_prev, z >= j)
        pump_to(19 + 2 * (W - j))

    pump_to(23)
    pump_to(26)
    got(v.D2R.at[0], base.d2)
    v.P32[pl.ds(0, Q), :] = (
        v.D1O[0, here, :] + v.D1R[0, here, :].astype(f32) + v.D2R[0].astype(f32)
    )

    @pl.when(has_next)
    def _():
        got(v.DZR.at[1], base.dz + 1)
        v.P32[pl.ds(0, Q), :] = v.P32[pl.ds(0, Q), :] + v.DZR[1].astype(f32)

    quarter = rows(core * HF + yy * Q, Q)
    dn1 = v.P32[pl.ds(0, Q), :]
    x_now = v.XB[quarter, :].astype(f32)
    r = lax.rsqrt(jnp.mean(x_now * x_now, axis=-1, keepdims=True) + EPS)
    gd = v.gain_one[...] * dn1
    gi = v.DH[here, :] + r * gd - x_now * (
        r * r * r * jnp.mean(gd * x_now, axis=-1, keepdims=True)
    )
    v.GIB[quarter, :] = gi.astype(bf16)
    mine = v.GIB.at[quarter]
    send(mine, mine, base.i1, to_y)
    send(mine, mine, base.i2, to_core)
    v.GT[0, pl.ds(1, 1), :] = jnp.sum(dn1 * x_now * r, axis=0, keepdims=True)
    send(v.GT.at[0], v.GR.at[0], base.g1, to_core)
    pump_to(28)
    got(v.GR.at[0], base.g1)
    v.GT[1] = v.GT[0] + v.GR[0]
    send(v.GT.at[1], v.GR.at[1], base.g2, to_y)
    from_y = v.GIB.at[rows(core * HF + (1 - yy) * Q, Q)]
    got(from_y, base.i1)
    send(from_y, from_y, base.i3, to_core)
    pump_to(32)
    got(v.GR.at[1], base.g2)
    v.GT[2] = v.GT[1] + v.GR[1]
    for d in list(peers) + [0]:
        tile = v.GT[2, :, pl.ds(hint(owner(d) * DF, 128), DF)]
        v.XS[owner(d), pl.ds(N, 16), :] = jnp.concatenate([tile, jnp.zeros_like(tile)], 0).astype(bf16)
        if d:
            grad_send(d, small(NK - 1), NK - 1)

    pump_to(49)
    for k in range(1, C):
        got(v.LB.at[lax.rem(z + C - k, C)], base.ll + k - 1)
    sums = [sum(v.LB[c, s] for c in range(C)) for s in range(F)]
    counted = sum(s[1:2, :] for s in sums)
    for s in range(F):
        v.LOSS[pl.ds(s, 1), :] = sums[s][0:1, :] * F / (counted * D)
    got(v.YB.at[rows((1 - core) * HF, HF)], base.yb)
    got(v.GIB.at[rows((1 - core) * HF + yy * Q, Q)], base.i2)
    got(v.GIB.at[rows((1 - core) * HF + (1 - yy) * Q, Q)], base.i3)
    results = (
        pltpu.make_async_copy(v.YB, v.y_out, ls.at[0]),
        pltpu.make_async_copy(v.GIB, v.gi_out, ls.at[1]),
        pltpu.make_async_copy(v.LOSS, v.loss_out, ls.at[2]),
    )
    for cp in results:
        cp.start()

    streams = grads_out + [group_in, group_out]

    def all_left(k):
        src, cond = unsent[k]

        def left():
            rcopy(src, src, k, 0, to_core).wait_send()

        if cond is None:
            left()
        else:
            pl.when(cond)(left)

    for k in range(len(unsent)):
        if k not in streams:
            all_left(k)
    pump_to(50)
    for k in streams:
        all_left(k)
    for cp in results:
        cp.wait()
    pltpu.make_async_copy(v.GRAD, v.grad_out, ls.at[10]).wait()


def finish_kernel(p, grad, gib, yb, loss, *refs):
    (y_out, loss_out, gi_out, one, gq, gk, gv, go, two, gg, gu, gd) = refs[:12]
    g_buf, i_buf, y_buf, l_buf, g_wide, i_wide, q_wide, sem_in, sem_out = refs[12:]
    FF, HC, N = p.FF, p.HC, p.N
    at = 3 * FF
    plain, flip = [], []
    for ref, first in ((gd, 0), (gg, FF), (gu, 2 * FF)):
        plain += [(ref, first, 0, FF // 2), (ref, first + FF // 2, FF // 2, FF // 2)]
    plain.append((go, at, 0, HC))
    flip = [(gq, at + HC), (gk, at + 2 * HC), (gv, at + 3 * HC)]
    loads = []

    def load(src, dst):
        cp = pltpu.make_async_copy(src, dst, sem_in.at[len(loads)])
        cp.start()
        loads.append(cp)
        return cp

    stores = []

    def store(src, dst):
        cp = pltpu.make_async_copy(src, dst, sem_out.at[len(stores)])
        cp.start()
        stores.append(cp)

    plain_in = [load(grad.at[pl.ds(f, n)], g_buf.at[pl.ds(f, n)]) for _, f, _, n in plain]
    flip_in = [load(grad.at[pl.ds(f, HC)], g_buf.at[pl.ds(f, HC)]) for _, f in flip]
    gi_in = load(gib, i_buf)
    y_in = load(yb, y_buf)
    gain_in = load(grad.at[pl.ds(N, 16)], g_buf.at[pl.ds(N, 16)])
    loss_in = load(loss, l_buf)
    for (ref, first, row, n), cp in zip(plain, plain_in):
        cp.wait()
        g_wide[pl.ds(first, n), :] = g_buf[pl.ds(first, n), :].astype(f32)
        store(g_wide.at[pl.ds(first, n)], ref.at[pl.ds(row, n)])
    for k, ((ref, first), cp) in enumerate(zip(flip, flip_in)):
        cp.wait()
        for c in range(0, HC, 128):
            w = min(128, HC - c)
            q_wide[k, :, pl.ds(c, w)] = g_buf[pl.ds(first + c, w), :].astype(f32).T
        store(q_wide.at[k], ref)
    gi_in.wait()
    i_wide[...] = i_buf[...].astype(f32)
    store(i_wide, gi_out.at[0])
    y_in.wait()
    store(y_buf, y_out.at[0])
    gain_in.wait()
    gains = g_buf[pl.ds(N, 16), :].astype(f32)
    two[...] = gains[0:1, :]
    one[...] = gains[1:2, :]
    loss_in.wait()
    for s in range(p.F):
        loss_out[s] = jnp.max(l_buf[pl.ds(s, 1), :])
    for cp in stores:
        cp.wait()


def shards(mesh_shape, seq_len, *args):
    (inputs, upstream, teacher, valid, segment, gain_one, wq, wk, wv, wo, gain_two, wg, wu, wd) = args
    _, rows_here, width = inputs.shape
    p = Plan(
        mesh_shape["fsdp"], mesh_shape["ctx"], rows_here, width, wq.shape[1], wg.shape[1], seq_len
    )
    R, D, DF, HC, FF, F = p.R, p.D, p.DF, p.HC, p.FF, p.F
    NG = p.N + 16
    scratch = scratch_of(p)
    vmem = pl.BlockSpec(memory_space=pltpu.VMEM)
    anywhere = pl.BlockSpec(memory_space=pl.ANY)
    in_specs = [anywhere] * 3 + [vmem] * 3 + [anywhere] * 4 + [vmem] + [anywhere] * 3
    sds = jax.ShapeDtypeStruct
    grad, gib, yb, loss = pl.pallas_call(
        functools.partial(layer_kernel, p, tuple(scratch)),
        out_shape=(
            sds((NG, DF), bf16), sds((R, D), bf16), sds((R, D), bf16), sds((max(F, 8), 128), f32),
        ),
        in_specs=in_specs,
        out_specs=(anywhere,) * 4,
        scratch_shapes=[pltpu.VMEM(s, dt) for s, dt in scratch.values()]
        + [
            pltpu.SemaphoreType.DMA((p.sends,)), pltpu.SemaphoreType.DMA((p.total,)),
            pltpu.SemaphoreType.DMA((11,)),
        ],
        compiler_params=pltpu.CompilerParams(
            collective_id=0, has_side_effects=True, vmem_limit_bytes=67043328
        ),
        name="layer",
    )(
        inputs.reshape(R, D), upstream.reshape(R, D), teacher.reshape(R, D), valid, segment,
        gain_one.reshape(1, D), wq, wk, wv, wo, gain_two.reshape(1, D), wg.T, wu.T, wd,
    )
    outs = pl.pallas_call(
        functools.partial(finish_kernel, p),
        out_shape=(
            sds((1, R, D), bf16), sds((F,), f32), sds((1, R, D), f32), sds((1, DF), f32),
            sds((DF, HC), f32), sds((DF, HC), f32), sds((DF, HC), f32), sds((HC, DF), f32),
            sds((1, DF), f32), sds((FF, DF), f32), sds((FF, DF), f32), sds((FF, DF), f32),
        ),
        in_specs=[anywhere] * 4,
        out_specs=(anywhere, pl.BlockSpec(memory_space=pltpu.SMEM), anywhere, vmem)
        + (anywhere,) * 4 + (vmem,) + (anywhere,) * 3,
        scratch_shapes=[
            pltpu.VMEM((NG, DF), bf16), pltpu.VMEM((R, D), bf16), pltpu.VMEM((R, D), bf16),
            pltpu.VMEM((max(F, 8), 128), f32), pltpu.VMEM((3 * FF + HC, DF), f32),
            pltpu.VMEM((R, D), f32), pltpu.VMEM((3, DF, HC), f32),
            pltpu.SemaphoreType.DMA((14,)), pltpu.SemaphoreType.DMA((12,)),
        ],
        compiler_params=pltpu.CompilerParams(vmem_limit_bytes=67043328),
        name="finish",
    )(grad, gib, yb, loss)
    outs = list(outs)
    outs[3], outs[8] = outs[3].reshape(DF), outs[8].reshape(DF)
    outs[9], outs[10] = outs[9].T, outs[10].T
    return tuple(outs)


def solution(mesh):
    def run(*args):
        token, row, col = P("fsdp", "ctx", None), P("fsdp", "tp"), P("tp", "fsdp")
        pair = P("fsdp", "ctx")
        return jax.shard_map(
            functools.partial(shards, dict(mesh.shape), args[0].shape[1]),
            mesh=mesh,
            in_specs=(token, token, token, pair, pair, P(), row, row, row, col, P(), row, row, col),
            out_specs=(
                token, P(), token, P("fsdp"), row, row, row, col, P("fsdp"), row, row, col,
            ),
            check_vma=False,
        )(*args)

    return run
```
